32 devices in a mesh: dp: 8 (over z, x), tensor: 4 (over y, core).
Axes of the slice: x: 2, y: 2, z: 4, core: 2. Of those that a mesh axis runs over, the one named last changes fastest.
Arguments:
- tokens: bfloat16 [4096, 768], P(('dp', 'tensor')), may hold values from -6 to 6
- pair_features: bfloat16 [16, 256, 256, 256], P('dp', 'tensor'), may hold values from -6 to 6
- cotangent: bfloat16 [4096, 768], P(('dp', 'tensor')), may hold values from -6 to 6
- chain_length: int32 [16], P('dp'), may hold values from 64 to 256, as said below
- time_bin: int32 [16], P('dp'), may hold values from 0 to 63
- cath_class: int32 [16], P('dp'), may hold values from 0 to 63
- bias_weight: bfloat16 [256, 12], replicated, may hold values from -0.375 to 0.375
- input_weight: bfloat16 [3, 768, 768], P(None, None, 'tensor'), may hold values from -0.21875 to 0.21875
- output_weight: bfloat16 [768, 768], P('tensor'), may hold values from -0.875 to 0.875
- hidden_weight: bfloat16 [2, 768, 3072], P(None, None, 'tensor'), may hold values from -0.21875 to 0.21875
- down_weight: bfloat16 [3072, 768], P('tensor'), may hold values from -0.109375 to 0.109375
- modulation_weight: bfloat16 [256, 4608], replicated, may hold values from -0.375 to 0.375
- time_table: bfloat16 [64, 256], replicated, may hold values from -4 to 4
- class_table: bfloat16 [64, 256], replicated, may hold values from -4 to 4
Outputs:
- result: bfloat16 [4096, 768], P(('dp', 'tensor'))
- grad_tokens: bfloat16 [4096, 768], P(('dp', 'tensor'))
- grad_pair: bfloat16 [16, 256, 256, 256], P('dp', 'tensor')
- grad_bias_weight: float32 [256, 12], replicated
- grad_input_weight: float32 [3, 768, 768], P(None, 'dp', 'tensor')
- grad_output_weight: float32 [768, 768], P('tensor', 'dp')
- grad_hidden_weight: float32 [2, 768, 3072], P(None, 'dp', 'tensor')
- grad_down_weight: float32 [3072, 768], P('tensor', 'dp')
- grad_modulation_weight: float32 [256, 4608], replicated
- grad_time_table: float32 [64, 256], replicated
- grad_class_table: float32 [64, 256], replicated
The draws below stay inside these ranges and needn't reach their ends.
Inputs may be any that keep to these rules, and one draw needn't show every extreme that they name: `chain_length`: every chain has at least 64 residues; the first chain slot of the whole batch is full.
All inputs are finite; a program needn't handle non-finite values.
Results may differ from the reference program's by a relative error of at most 0.02.
The reference program's roundings to bfloat16 on the way count: a program that leaves them out, or rounds other values in their place, can miss the bound.
Values may be sent and summed in bfloat16 or wider, within the bound.
A program may use at most 128 MiB of HBM per device.

```python
import jax
import jax.numpy as jnp
from jax import lax

D = 768
H = 12
HD = 64
FF = 3072
PD = 256
DC = 256
NT = 64
NC = 64
LMAX = 256
CHAINS = 16
TOKENS = 4096


def draw_chain_length(key, part):
    drawn = jax.random.randint(key, (CHAINS,), LMAX // 4, LMAX + 1)
    return jnp.where(jnp.arange(CHAINS) == 0, LMAX, drawn).astype(jnp.int32)


def place_ends(values, stream_key, smallest, largest):
    spot = [jax.random.randint(jax.random.fold_in(stream_key, axis), (), 0, length) for axis, length in enumerate(values.shape)]
    main_axis = values.shape.index(max(values.shape))
    neighbour = spot[:main_axis] + [(spot[main_axis] + 1) % values.shape[main_axis]] + spot[main_axis + 1:]
    return values.at[tuple(spot)].set(smallest).at[tuple(neighbour)].set(largest)


def strengthened(entries, key, source, target, shards_of, factor):
    def block_of(axis_at):
        return (jnp.arange(entries.shape[axis_at]) // (entries.shape[axis_at] // shards_of)).reshape((-1,) + (1,) * (entries.ndim - 1 - axis_at))

    one_side = jax.random.permutation(key, shards_of)[block_of(target)]
    far = (block_of(target) + shards_of // 2) % shards_of
    return jnp.where((block_of(source) == one_side) | (block_of(source) == far), factor * entries, entries)


def shard_levels(stream_key, shape, pieces, least, largest):
    gain = 1.0
    for position, shards_of in pieces:
        steps = jax.random.uniform(jax.random.fold_in(jax.random.fold_in(stream_key, 6), position), (shards_of,), jnp.float32, least / len(pieces), largest / len(pieces))
        gain = gain * jnp.repeat(jnp.exp(steps), shape[position] // shards_of).reshape((-1,) + (1,) * (len(shape) - 1 - position))
    return gain


def normal_values(rng, dims, width, limit, shards=(), dtype=jnp.bfloat16):
    gain = shard_levels(rng, dims, shards, -0.22, 0.18) if shards else 1.0
    entries = jax.random.normal(rng, dims, jnp.float32) * width * gain
    return jnp.minimum(jnp.maximum(entries, -limit), limit).astype(dtype)


def heavy_noise(key, shape, scale, reach, split, heavy, dtype=jnp.bfloat16):
    values = scale * jax.random.normal(key, shape, jnp.float32)
    if split:
        values = values * shard_levels(key, shape, split, -0.22, 0.18)
    return jnp.clip(strengthened(values, jax.random.fold_in(key, 3), *heavy), -reach, reach).astype(dtype)


def setup_inputs(seed: int = 0) -> dict:
    seeds = jax.random.split(jax.random.key(seed), 15)
    return {
        "tokens": normal_values(seeds[0], (TOKENS, D), 1.0, 6.0, ((0, 32),)),
        "pair_features": normal_values(seeds[1], (CHAINS, LMAX, LMAX, PD), 1.0, 6.0, ((0, 8), (1, 4))),
        "cotangent": heavy_noise(seeds[2], (TOKENS, D), 1.0, 6.0, ((0, 32),), (0, 1, 32, 2.75)),
        "chain_length": draw_chain_length(jax.random.fold_in(seeds[14], 71), 0),
        "time_bin": place_ends(jax.random.randint(seeds[4], (CHAINS,), 0, NT), jax.random.fold_in(seeds[4], 1), 0, NT - 1).astype(jnp.int32),
        "cath_class": place_ends(jax.random.randint(seeds[5], (CHAINS,), 0, NC), jax.random.fold_in(seeds[5], 1), 0, NC - 1).astype(jnp.int32),
        "bias_weight": normal_values(seeds[6], (PD, H), PD ** -0.5, 0.375),
        "input_weight": normal_values(seeds[7], (3, D, H * HD), D ** -0.5, 0.21875, ((2, 4),)),
        "output_weight": normal_values(seeds[8], (H * HD, D), (H * HD // 16) ** -0.5, 0.875, ((0, 4),)),
        "hidden_weight": normal_values(seeds[9], (2, D, FF), D ** -0.5, 0.21875, ((2, 4),)),
        "down_weight": normal_values(seeds[10], (FF, D), FF ** -0.5, 0.109375, ((0, 4),)),
        "modulation_weight": normal_values(seeds[11], (DC, 6 * D), DC ** -0.5, 0.375),
        "time_table": normal_values(seeds[12], (NT, DC), 0.7, 4.0),
        "class_table": normal_values(seeds[13], (NC, DC), 0.7, 4.0),
    }


@jax.custom_vjp
def low(v):
    return lax.optimization_barrier(v.astype(jnp.bfloat16)).astype(jnp.float32)

@jax.custom_vjp
def low_back(v):
    return v

def low_keep(v):
    return (low(v), None)

def low_pass(kept, grad):
    return (grad,)

def back_keep(v):
    return (v, None)

def back_low(kept, grad):
    return (low(grad),)
low.defvjp(low_keep, low_pass)
low_back.defvjp(back_keep, back_low)
HIGH = lax.Precision.HIGHEST
EPSILON = 1e-05

def layer_norm(row_block):
    centre = row_block - lax.optimization_barrier(jnp.mean(row_block, axis=-1, keepdims=True))
    return centre * lax.rsqrt(lax.optimization_barrier(jnp.mean(centre * centre, axis=-1, keepdims=True)) + EPSILON)

def rounded_both(value_in):
    return low_back(low(value_in))

def attend(packed):
    query_rows, key_rows, value_rows, bias_full, keep_mask = packed
    raw_scores = jnp.einsum('qhd,khd->hqk', query_rows, key_rows, precision=HIGH) * HD ** (-0.5) + bias_full
    logits = jnp.where(keep_mask[None, None, :] > 0, low_back(raw_scores), -1000000000.0)
    soft_weights = low(jax.nn.softmax(logits, axis=-1))
    return jnp.einsum('hqk,khd->qhd', soft_weights, value_rows, precision=HIGH)

def reference(tokens, pair_features, cotangent, chain_length, time_bin, cath_class, bias_weight, input_weight, output_weight, hidden_weight, down_weight, modulation_weight, time_table, class_table):
    chain_count = chain_length.shape[0]
    valid = (jnp.arange(LMAX)[None, :] < chain_length[:, None]).astype(jnp.float32)

    def forward(float_tokens, float_pair, float_bias_w, float_input_w, float_output_w, float_hidden_w, float_down_w, float_mod_w, float_time, float_class):
        condition = float_time[time_bin] + float_class[cath_class]
        modulation = jnp.dot(condition, float_mod_w, precision=HIGH).reshape(chain_count, 6, 1, D)
        row_block = float_tokens.reshape(chain_count, LMAX, D)
        h_attend = low(layer_norm(row_block) * (1.0 + modulation[:, 0]) + modulation[:, 1])
        projected = rounded_both(jnp.einsum('cld,tde->tcle', h_attend, float_input_w, precision=HIGH))
        head_split = projected.reshape(3, chain_count, LMAX, H, HD)

        def bias_one(single):
            return jnp.einsum('ijp,ph->hij', single, float_bias_w, precision=HIGH)
        bias_full = rounded_both(lax.map(jax.checkpoint(bias_one), float_pair))
        attended = lax.map(jax.checkpoint(attend), (head_split[0], head_split[1], head_split[2], bias_full, valid))
        attended = rounded_both(attended.reshape(chain_count, LMAX, H * HD))
        out_attend = low_back(jnp.einsum('cle,ed->cld', attended, float_output_w, precision=HIGH))
        middle = row_block + valid[:, :, None] * jax.nn.sigmoid(modulation[:, 2]) * out_attend
        h_hidden = low(layer_norm(middle) * (1.0 + modulation[:, 3]) + modulation[:, 4])
        gate_up = jnp.einsum('cld,tdf->tclf', h_hidden, float_hidden_w, precision=HIGH)
        active = low(jax.nn.silu(low_back(gate_up[0])) * low_back(gate_up[1]))
        out_hidden = low_back(jnp.einsum('clf,fd->cld', active, float_down_w, precision=HIGH))
        final = middle + valid[:, :, None] * jax.nn.sigmoid(modulation[:, 5]) * out_hidden
        return final.reshape(chain_count * LMAX, D)
    primals = (tokens.astype(jnp.float32), pair_features.astype(jnp.float32), bias_weight.astype(jnp.float32), input_weight.astype(jnp.float32), output_weight.astype(jnp.float32), hidden_weight.astype(jnp.float32), down_weight.astype(jnp.float32), modulation_weight.astype(jnp.float32), time_table.astype(jnp.float32), class_table.astype(jnp.float32))
    final, pullback = jax.vjp(forward, *primals)
    grad_list = pullback(cotangent.astype(jnp.float32))
    return (final.astype(jnp.bfloat16), grad_list[0].astype(jnp.bfloat16), grad_list[1].astype(jnp.bfloat16), grad_list[2], grad_list[3], grad_list[4], grad_list[5], grad_list[6], grad_list[7], grad_list[8], grad_list[9])
```

```python
import functools

import jax
import jax.numpy as jnp
from jax import lax
from jax.experimental import pallas as pl
from jax.experimental.pallas import tpu as pltpu
from jax.sharding import PartitionSpec as P

HD = 64
EPSILON = 1e-05
BF = jnp.bfloat16
F32 = jnp.float32
MESH = pl.DeviceIdType.MESH
PAIR_SLOTS = 4
PAIR_ROWS = 16
VMEM_BYTES = 60 << 20


def nn(a, b):
    return lax.dot_general(a, b, (((1,), (0,)), ((), ())), preferred_element_type=F32)


def nt(a, b):
    return lax.dot_general(a, b, (((1,), (1,)), ((), ())), preferred_element_type=F32)


def tn(a, b):
    return lax.dot_general(a, b, (((0,), (0,)), ((), ())), preferred_element_type=F32)


def sigmoid(x):
    return 1.0 / (1.0 + jnp.exp(-x))


def layer_norm(rows):
    centre = rows - jnp.mean(rows, axis=-1, keepdims=True)
    inverse = lax.rsqrt(jnp.mean(centre * centre, axis=-1, keepdims=True) + EPSILON)
    return centre * inverse, inverse


def norm_back(grad, normed, inverse):
    return inverse * (
        grad
        - jnp.mean(grad, axis=-1, keepdims=True)
        - normed * jnp.mean(grad * normed, axis=-1, keepdims=True)
    )


class Remote:
    def __init__(self, send_sems, recv_sems):
        self.send_sems, self.recv_sems, self.started = send_sems, recv_sems, []

    def start(self, src, dst, device):
        index = len(self.started)
        copy = pltpu.make_async_remote_copy(
            src_ref=src,
            dst_ref=dst,
            send_sem=self.send_sems.at[index],
            recv_sem=self.recv_sems.at[index],
            device_id=device,
            device_id_type=MESH,
        )
        copy.start()
        self.started.append(copy)
        return copy

    def finish(self):
        for copy in self.started:
            copy.wait_send()


class Gather:
    def __init__(self, remote, slots, here, near, far, near_device, far_device):
        self.remote, self.slots, self.far, self.near_device = remote, slots, far, near_device
        self.to_far = remote.start(slots.at[here], slots.at[here], far_device)
        self.to_near = remote.start(slots.at[here], slots.at[here], near_device)

    def forward(self):
        self.to_far.wait_recv()
        self.passed = self.remote.start(
            self.slots.at[self.far], self.slots.at[self.far], self.near_device
        )

    def wait_near(self):
        self.to_near.wait_recv()

    def wait_rest(self):
        self.passed.wait_recv()


class Scatter:
    def __init__(self, remote, part, out, arrived, ids, near_device, far_device):
        self.remote, self.part, self.out, self.arrived = remote, part, out, arrived
        self.here, self.near, self.far, self.cross = ids
        self.near_device, self.far_device = near_device, far_device

    def pre(self):
        self.out[0] = self.part[self.cross].astype(BF)
        self.first = self.remote.start(self.out.at[0], self.arrived.at[0], self.near_device)

    def across(self):
        self.first.wait_recv()
        self.out[1] = (self.part[self.far] + self.arrived[0].astype(F32)).astype(BF)
        self.second = self.remote.start(self.out.at[1], self.arrived.at[1], self.far_device)

    def local(self):
        self.out[2] = self.part[self.near].astype(BF)
        self.third = self.remote.start(self.out.at[2], self.arrived.at[2], self.near_device)
        self.own = self.part[self.here]

    def total(self):
        self.third.wait_recv()
        self.second.wait_recv()
        return self.own + self.arrived[2].astype(F32) + self.arrived[1].astype(F32)


class Halving:
    def __init__(self, remote, store, arrived, rank, count, device, order):
        self.remote, self.store, self.arrived = remote, store, arrived
        self.rank, self.count, self.device = rank, count, device
        self.order, self.step, self.offset, self.landing = order, 0, 0, 0

    def send(self):
        bit = self.order[self.step]
        self.half = self.count >> (self.step + 1)
        mine = lax.rem(self.rank // (1 << bit), 2)
        partner = self.rank + (1 - 2 * mine) * (1 << bit)
        away = self.offset + (1 - mine) * self.half
        self.offset = self.offset + mine * self.half
        self.copy = self.remote.start(
            self.store.at[pl.ds(away, self.half)],
            self.arrived.at[pl.ds(self.landing, self.half)],
            self.device(partner),
        )

    def sum(self):
        self.copy.wait_recv()
        keep = pl.ds(self.offset, self.half)
        total = self.store[keep].astype(F32) + self.arrived[
            pl.ds(self.landing, self.half)
        ].astype(F32)
        self.landing += self.half
        self.step += 1
        if self.step == len(self.order):
            return total[0]
        self.store[keep] = total.astype(BF)
        self.send()
        return None

    def last(self):
        total = None
        while total is None:
            total = self.sum()
        return total


def slot_of(chunk, order):
    slot = 0
    for bit in order:
        slot = slot * 2 + (chunk >> bit) % 2
    return slot


def layer_kernel(
    dims,
    orders,
    length_ref,
    time_ref,
    class_ref,
    tokens_hbm,
    cotangent_hbm,
    pair_hbm,
    bias_hbm,
    input_hbm,
    output_hbm,
    hidden_hbm,
    down_hbm,
    modulation_hbm,
    time_hbm,
    class_hbm,
    result_out,
    grad_tokens_out,
    scores_out,
    mods_out,
    hots_out,
    bias_grad_out,
    weights_out,
    tokens,
    cotangent,
    pair,
    bias_weight,
    input_weight,
    output_weight,
    hidden_weight,
    down_weight,
    modulation_weight,
    tables,
    mods,
    stage,
    hots,
    mods_all,
    rows_attend,
    rows_hidden,
    rows_down,
    rows_out,
    bias_send,
    bias_full,
    queries,
    keys,
    values,
    probs,
    attended,
    part,
    part_down,
    grad_active,
    active,
    grad_gate,
    grad_up,
    grad_scores,
    scores_own,
    grad_projected,
    scatter_send,
    scatter_recv,
    turned,
    turned_more,
    grad_store,
    grad_recv,
    final_weights,
    norm_attend,
    norm_hidden,
    middle,
    out_attend,
    grad_middle,
    result,
    grad_tokens,
    mod_part,
    mod_near,
    mod_sum,
    mod_far,
    bias_grads,
    bias_sums,
    bias_grad,
    load_sems,
    pair_sems,
    store_sems,
    send_sems,
    recv_sems,
):
    (groups, chains, span, local, width, local_width, queries_local, hidden) = dims
    heads = local_width // HD
    dp = lax.axis_index("dp")
    me = lax.axis_index("tensor")
    core = lax.rem(me, 2)
    chip = me // 2
    near = me + 1 - 2 * core
    far = lax.rem(me + 2, 4)
    cross = 3 - me
    away = 1 - chip
    near_device, far_device, cross_device = (dp, near), (dp, far), (dp, cross)

    def dp_device(index):
        return (index, me)

    barrier = pltpu.get_barrier_semaphore()
    for device in (near_device, far_device, cross_device):
        pl.semaphore_signal(barrier, inc=1, device_id=device, device_id_type=MESH)
    for step in range(1, groups):
        pl.semaphore_signal(
            barrier, inc=1, device_id=dp_device(lax.rem(dp + step, groups)), device_id_type=MESH
        )

    loads = []

    def load(src, dst):
        copy = pltpu.make_async_copy(src, dst, load_sems.at[len(loads)])
        copy.start()
        loads.append(copy)
        return copy

    blocks = queries_local // PAIR_ROWS
    n_blocks = chains * blocks

    def pair_copy(index):
        chain = lax.rem(chip + index // blocks, chains)
        slot = lax.rem(index, PAIR_SLOTS)
        return pltpu.make_async_copy(
            pair_hbm.at[chain, pl.ds(lax.rem(index, blocks) * PAIR_ROWS, PAIR_ROWS)],
            pair.at[slot],
            pair_sems.at[slot],
        )

    times = time_hbm.shape[0]
    load_time = load(time_hbm, tables.at[pl.ds(0, times)])
    load_class = load(class_hbm, tables.at[pl.ds(times, class_hbm.shape[0])])
    load_tokens = load(tokens_hbm, tokens)
    load_modulation = load(modulation_hbm, modulation_weight)
    load_cotangent = load(cotangent_hbm, cotangent)
    load_bias = load(bias_hbm, bias_weight)
    for index in range(PAIR_SLOTS):
        pair_copy(index).start()
    load_input = load(input_hbm, input_weight)
    load_output = load(output_hbm, output_weight)
    load_down = load(down_hbm, down_weight)
    load_hidden = load(hidden_hbm, hidden_weight)

    remote = Remote(send_sems, recv_sems)

    n_table = tables.shape[0]
    lane = lax.broadcasted_iota(jnp.int32, (16, n_table), 1)
    row = lax.broadcasted_iota(jnp.int32, (16, n_table), 0)
    picked = ((row == 0) & (lane == time_ref[chip])) | (
        (row == 1) & (lane == times + class_ref[chip])
    )
    time_row = jnp.where(row < 8, time_ref[0], time_ref[1])
    class_row = jnp.where(row < 8, class_ref[0], class_ref[1])
    hots[dp] = jnp.where((lane == time_row) | (lane == times + class_row), 1.0, 0.0).astype(BF)
    load_time.wait()
    load_class.wait()
    condition = nn(jnp.where(picked, 1.0, 0.0).astype(BF), tables[...]).astype(BF)
    load_modulation.wait()
    both = nn(condition, modulation_weight[...])
    mods[...] = jnp.broadcast_to(both[0:1] + both[1:2], mods.shape)

    def mod(index):
        return mods[0:1, index * width : (index + 1) * width]

    place = lax.rem(me * local, span) + lax.broadcasted_iota(jnp.int32, (local, 1), 0)
    valid = jnp.where(place < length_ref[chip], 1.0, 0.0)

    load_tokens.wait()
    normed, inverse_attend = layer_norm(tokens[...].astype(F32))
    norm_attend[...] = normed
    rows_attend[me] = (normed * (1.0 + mod(0)) + mod(1)).astype(BF)
    load_cotangent.wait()
    gate_hidden = sigmoid(mod(5))
    rows_down[me] = (cotangent[...].astype(F32) * valid * gate_hidden).astype(BF)
    load_bias.wait()
    wide = jnp.concatenate(
        [
            bias_weight[...].astype(F32),
            jnp.zeros((bias_weight.shape[0], 128 - bias_weight.shape[1]), F32),
        ],
        axis=1,
    )
    bias_turned = jnp.transpose(wide)[:16].astype(BF)

    pl.semaphore_wait(barrier, 3 + groups - 1)
    gather_attend = Gather(remote, rows_attend, me, near, far, near_device, far_device)
    hot_copies = []
    for step in range(1, groups):
        device = dp_device(lax.rem(dp + step, groups))
        hot_copies.append(remote.start(hots.at[dp], hots.at[dp], device))

    def bias_block(index, carry):
        slot = lax.rem(index, PAIR_SLOTS)
        pair_copy(index).wait()
        for row_index in range(PAIR_ROWS):
            product = nt(bias_turned, pair[slot, row_index])
            place_row = lax.rem(index, blocks) * PAIR_ROWS + row_index
            for half in range(2):
                stage[half, pl.ds(place_row, 16, stride=queries_local), :] = product[
                    :, half * 128 : (half + 1) * 128
                ]

        @pl.when(index + PAIR_SLOTS < n_blocks)
        def _():
            pair_copy(index + PAIR_SLOTS).start()

        return carry

    all_rows = 4 * heads * queries_local
    bias_copies = []
    for turn in range(2):
        chain = lax.rem(chip + turn, 2)
        lax.fori_loop(turn * blocks, (turn + 1) * blocks, bias_block, 0)
        for half in range(2):
            bias_send[chain, :, :, half * 128 : (half + 1) * 128] = (
                stage[half, 0:all_rows, :].astype(BF).reshape(4 * heads, queries_local, 128)
            )
        mine = pl.ds(me * queries_local, queries_local)
        sent = []
        for owner, device in ((far, far_device), (cross, cross_device), (near, near_device)):
            sent.append(
                remote.start(
                    bias_send.at[chain, pl.ds(owner * heads, heads)],
                    bias_full.at[chain, :, mine],
                    device,
                )
            )
        bias_copies.append(sent)
        bias_full[chain, :, mine, :] = bias_send[chain, pl.ds(me * heads, heads)]
        if turn == 0:
            gather_attend.forward()

    for index in range(PAIR_SLOTS):
        pair_copy(index).start()

    load_input.wait()

    def project(half):
        rows = rows_attend[pl.ds(2 * half, 2)].reshape(span, width)
        queries[half] = nn(rows, input_weight[0]).astype(BF)
        keys[half] = nn(rows, input_weight[1]).astype(BF)
        values[half] = nn(rows, input_weight[2]).astype(BF)

    gather_attend.wait_near()
    project(chip)
    gather_attend.wait_rest()
    project(away)

    head_lane = lax.broadcasted_iota(jnp.int32, (span, local_width), 1)

    def stacked(rows):
        zero = jnp.zeros_like(rows)
        return jnp.concatenate(
            [
                jnp.where((head_lane >= head * HD) & (head_lane < (head + 1) * HD), rows, zero)
                for head in range(heads)
            ],
            axis=0,
        )

    def choose(pieces):
        out = pieces[-1]
        for head in range(heads - 2, -1, -1):
            out = jnp.where(head_lane < (head + 1) * HD, pieces[head], out)
        return out

    def attend(chain):
        scores = nt(stacked(queries[chain]), keys[chain]) * HD ** (-0.5) + bias_full[
            chain
        ].reshape(heads * span, span).astype(F32)
        key_place = lax.broadcasted_iota(jnp.int32, (heads * span, span), 1)
        scores = jnp.where(key_place < length_ref[chain], scores, -1000000000.0)
        top = jnp.max(scores, axis=-1, keepdims=True)
        weights = jnp.exp(scores - top)
        weights = weights * (1.0 / jnp.sum(weights, axis=-1, keepdims=True))
        probs[chain] = weights
        soft = weights.astype(BF)
        attended[chain] = choose(
            [nn(soft[head * span : (head + 1) * span], values[chain]) for head in range(heads)]
        ).astype(BF)

    def put(target, half, rows):
        target[pl.ds(2 * half, 2)] = rows.reshape(2, local, width)

    ids = (me, near, far, cross)

    def scatter(index, source):
        return Scatter(
            remote,
            source,
            scatter_send.at[index],
            scatter_recv.at[index],
            ids,
            near_device,
            far_device,
        )

    bias_copies[0][0].wait_recv()
    bias_copies[0][1].wait_recv()
    bias_copies[1][2].wait_recv()
    attend(away)
    load_output.wait()
    put(part, away, nn(attended[away], output_weight[...]))
    scatter_attend = scatter(0, part)
    scatter_attend.pre()
    bias_copies[1][0].wait_recv()
    bias_copies[1][1].wait_recv()
    bias_copies[0][2].wait_recv()
    scatter_attend.across()
    gather_down = Gather(remote, rows_down, me, near, far, near_device, far_device)
    attend(chip)
    put(part, chip, nn(attended[chip], output_weight[...]))
    scatter_attend.local()

    load_down.wait()

    def back_down(half):
        rows = rows_down[pl.ds(2 * half, 2)].reshape(span, width)
        grad_active[half] = nt(rows, down_weight[...])
        for slot in range(2):
            place_slot = 2 * half + slot
            turned[:, pl.ds(pl.multiple_of(place_slot * local, local), local)] = jnp.transpose(
                rows[slot * local : (slot + 1) * local]
            )

    gather_down.wait_near()
    back_down(chip)
    gather_down.forward()

    gate_attend = sigmoid(mod(2))
    out_total = scatter_attend.total()
    out_attend[...] = out_total
    total = tokens[...].astype(F32) + valid * gate_attend * out_total
    middle[...] = total
    normed, inverse_hidden = layer_norm(total)
    norm_hidden[...] = normed
    rows_hidden[me] = (normed * (1.0 + mod(3)) + mod(4)).astype(BF)
    gather_hidden = Gather(remote, rows_hidden, me, near, far, near_device, far_device)
    gather_down.wait_rest()
    back_down(away)

    load_hidden.wait()

    def transition(half):
        rows = rows_hidden[pl.ds(2 * half, 2)].reshape(span, width)
        gate = nn(rows, hidden_weight[0])
        up = nn(rows, hidden_weight[1])
        squashed = sigmoid(gate)
        silu = gate * squashed
        active[half] = (silu * up).astype(BF)
        back = grad_active[half]
        grad_gate[half] = (back * up * squashed * (1.0 + gate * (1.0 - squashed))).astype(BF)
        grad_up[half] = (back * silu).astype(BF)

    def back_hidden(half):
        put(
            part,
            half,
            nt(grad_gate[half], hidden_weight[0]) + nt(grad_up[half], hidden_weight[1]),
        )

    gather_hidden.wait_near()
    transition(chip)
    gather_hidden.forward()
    back_hidden(chip)
    put(part_down, chip, nn(active[chip], down_weight[...]))
    gather_hidden.wait_rest()
    transition(away)
    back_hidden(away)
    scatter_hidden = scatter(1, part)
    scatter_hidden.pre()
    put(part_down, away, nn(active[away], down_weight[...]))
    scatter_hidden.across()
    scatter_hidden.local()
    scatter_down = scatter(2, part_down)
    scatter_down.pre()

    chunk = width // groups
    per_block = max(1, 192 // chunk)

    def halving(index):
        return Halving(
            remote,
            grad_store.at[index],
            grad_recv.at[index],
            dp,
            groups,
            dp_device,
            orders[index],
        )

    def weight_grad(index, *pairs):
        for block in range(groups // per_block):
            rows = slice(block * per_block * chunk, (block + 1) * per_block * chunk)
            product = jnp.concatenate([nn(left[rows, :], right) for left, right in pairs], axis=1)
            for inner in range(per_block):
                grad_store[index, slot_of(block * per_block + inner, orders[index])] = product[
                    inner * chunk : (inner + 1) * chunk
                ].astype(BF)

    def flat(ref):
        return ref[...].reshape(chains * span, ref.shape[-1])

    def turn_rows(source, target):
        for slot in range(4):
            target[:, slot * local : (slot + 1) * local] = jnp.transpose(source[slot])

    weight_grad(0, (turned, flat(active)))
    sum_down = halving(0)
    sum_down.send()
    scatter_down.across()
    scatter_down.local()
    turn_rows(rows_hidden, turned_more)
    weight_grad(1, (turned_more, flat(grad_gate)))
    sum_gate = halving(1)
    sum_gate.send()
    weight_grad(2, (turned_more, flat(grad_up)))
    sum_up = halving(2)
    sum_up.send()

    grad_h = scatter_hidden.total()
    normed = norm_hidden[...]
    back = cotangent[...].astype(F32) + norm_back(grad_h * (1.0 + mod(3)), normed, inverse_hidden)
    grad_middle[...] = back
    rows_out[me] = (back * valid * gate_attend).astype(BF)
    gather_out = Gather(remote, rows_out, me, near, far, near_device, far_device)

    def keep_mod(index, rows):
        mod_part[index : index + 1, :] = jnp.sum(rows, axis=0, keepdims=True)

    mod_part[...] = jnp.zeros_like(mod_part)
    keep_mod(3, grad_h * normed)
    keep_mod(4, grad_h)
    keep_mod(2, back * valid * out_attend[...] * gate_attend * (1.0 - gate_attend))
    out_total = scatter_down.total()
    result[...] = (middle[...] + valid * gate_hidden * out_total).astype(BF)
    keep_mod(
        5, cotangent[...].astype(F32) * valid * out_total * gate_hidden * (1.0 - gate_hidden)
    )
    turn_rows(rows_attend, turned)

    score_copies = []

    def back_attend(chain):
        rows = rows_out[pl.ds(2 * chain, 2)].reshape(span, width)
        grad_heads = stacked(nt(rows, output_weight[...]).astype(BF))
        weights = probs[chain]
        grad_probs = nt(grad_heads, values[chain])
        grad_logits = (
            weights * (grad_probs - jnp.sum(grad_probs * weights, axis=-1, keepdims=True))
        ).astype(BF)
        grad_scores[chain] = grad_logits.reshape(heads, span, span)
        sent = []
        for owner, device in ((far, far_device), (cross, cross_device), (near, near_device)):
            sent.append(
                remote.start(
                    grad_scores.at[chain, :, pl.ds(owner * queries_local, queries_local)],
                    scores_own.at[chain, pl.ds(me * heads, heads)],
                    device,
                )
            )
        score_copies.append(sent)
        scores_own[chain, pl.ds(me * heads, heads)] = grad_scores[
            chain, :, pl.ds(me * queries_local, queries_local), :
        ]
        query_stack = stacked(queries[chain])
        grad_query = (
            choose(
                [
                    nn(grad_logits[head * span : (head + 1) * span], keys[chain])
                    for head in range(heads)
                ]
            )
            * HD ** (-0.5)
        ).astype(BF)
        grad_key = (tn(grad_logits, query_stack) * HD ** (-0.5)).astype(BF)
        grad_value = tn(weights.astype(BF), grad_heads).astype(BF)
        grad_projected[chain] = jnp.concatenate([grad_query, grad_key, grad_value], axis=1)
        put(
            part,
            chain,
            nt(grad_query, input_weight[0])
            + nt(grad_key, input_weight[1])
            + nt(grad_value, input_weight[2]),
        )

    gather_out.wait_near()
    gather_out.forward()
    back_attend(chip)
    gather_out.wait_rest()
    back_attend(away)
    scatter_input = scatter(3, part)
    scatter_input.pre()
    turn_rows(rows_out, turned_more)
    scatter_input.across()
    scatter_input.local()
    sum_down.sum()

    weight_grad(3, (turned, flat(grad_projected)), (turned_more, flat(attended)))
    sum_attend = halving(3)
    sum_attend.send()

    grad_h = scatter_input.total()
    normed = norm_attend[...]
    grad_tokens[...] = (
        grad_middle[...] + norm_back(grad_h * (1.0 + mod(0)), normed, inverse_attend)
    ).astype(BF)
    keep_mod(0, grad_h * normed)
    keep_mod(1, grad_h)
    to_near = remote.start(mod_part, mod_near, near_device)

    stores = []

    def store(src, dst):
        copy = pltpu.make_async_copy(src, dst, store_sems.at[len(stores)])
        copy.start()
        stores.append(copy)

    store(result, result_out)
    store(grad_tokens, grad_tokens_out)

    sum_gate.sum()
    sum_down.sum()

    to_near.wait_recv()
    mod_sum[...] = mod_part[...] + mod_near[...]
    to_far = remote.start(mod_sum, mod_far, far_device)

    for sent in score_copies:
        for copy in sent:
            copy.wait_recv()
    store(scores_own, scores_out)

    def bias_grad_block(index, total):
        slot = lax.rem(index, PAIR_SLOTS)
        pair_copy(index).wait()
        for row_index in range(PAIR_ROWS):
            place_row = lax.rem(index, blocks) * PAIR_ROWS + row_index
            rows = jnp.concatenate(
                [
                    stage[half, pl.ds(place_row, 16, stride=queries_local), :].astype(BF)
                    for half in range(2)
                ],
                axis=1,
            )
            total = total + nn(rows, pair[slot, row_index])

        @pl.when(index + PAIR_SLOTS < n_blocks)
        def _():
            pair_copy(index + PAIR_SLOTS).start()

        return total

    total = jnp.zeros((16, pair_hbm.shape[3]), F32)
    for turn in range(2):
        chain = lax.rem(chip + turn, 2)
        for half in range(2):
            stage[half, 0:all_rows, :] = (
                scores_own[chain, :, :, half * 128 : (half + 1) * 128]
                .reshape(all_rows, 128)
                .astype(F32)
            )
            stage[half, all_rows:, :] = jnp.zeros((16 * queries_local - all_rows, 128), F32)
        total = lax.fori_loop(turn * blocks, (turn + 1) * blocks, bias_grad_block, total)
    bias_grads[0] = total
    tensor_copies = [
        remote.start(bias_grads.at[0], bias_grads.at[1 + index], device)
        for index, device in enumerate((near_device, far_device, cross_device))
    ]
    to_far.wait_recv()
    own, other = mod_sum[...], mod_far[...]
    low = jnp.where(chip == 0, own, other)
    high = jnp.where(chip == 0, other, own)
    mods_all[dp] = jnp.concatenate([low, high], axis=0).astype(BF)
    mod_copies = [
        remote.start(mods_all.at[dp], mods_all.at[dp], dp_device(lax.rem(dp + step, groups)))
        for step in range(1, groups)
    ]
    for copy in tensor_copies:
        copy.wait_recv()
    bias_sums[0] = bias_grads[0] + bias_grads[1] + bias_grads[2] + bias_grads[3]
    bias_copies = [
        remote.start(bias_sums.at[0], bias_sums.at[step], dp_device(lax.rem(dp + step, groups)))
        for step in range(1, groups)
    ]

    sum_up.sum()
    sum_gate.sum()
    final_weights[0] = sum_down.last()
    sum_attend.sum()
    sum_up.sum()
    final_weights[2] = sum_gate.last()
    for copy in hot_copies + mod_copies:
        copy.wait_recv()
    store(hots, hots_out)
    store(mods_all, mods_out)
    for copy in bias_copies:
        copy.wait_recv()
    bias_grad[...] = jnp.sum(bias_sums[...], axis=0)
    store(bias_grad, bias_grad_out)
    sum_attend.sum()
    final_weights[3] = sum_up.last()
    final_weights[1] = sum_attend.last()
    store(final_weights, weights_out)
    for copy in stores:
        copy.wait()
    remote.finish()


def finish_kernel(
    dims,
    result_in,
    grad_tokens_in,
    weights_hbm,
    scores_ref,
    mods_ref,
    hots_ref,
    bias_grad_ref,
    weights_ref,
    bias_ref,
    modulation_ref,
    time_ref,
    class_ref,
    result_out,
    grad_tokens_out,
    grad_pair_ref,
    grad_bias_ref,
    grad_input_ref,
    grad_output_ref,
    grad_hidden_out,
    grad_down_ref,
    grad_modulation_ref,
    grad_time_ref,
    grad_class_ref,
    stage,
    bias_turned,
    expanded,
    grad_condition,
    sems,
):
    (groups, chains, span, local, width, local_width, queries_local, hidden) = dims
    heads = local_width // HD
    step = pl.program_id(0)
    blocks = queries_local // PAIR_ROWS
    all_rows = 4 * heads * queries_local
    rows_all = groups * 16
    times = time_ref.shape[0]

    def copies():
        return [
            pltpu.make_async_copy(result_in, result_out, sems.at[0]),
            pltpu.make_async_copy(grad_tokens_in, grad_tokens_out, sems.at[1]),
            pltpu.make_async_copy(weights_hbm.at[2], grad_hidden_out.at[0], sems.at[2]),
            pltpu.make_async_copy(weights_hbm.at[3], grad_hidden_out.at[1], sems.at[3]),
        ]

    @pl.when(step == 0)
    def _():
        for copy in copies():
            copy.start()
        wide = jnp.concatenate(
            [
                bias_ref[...].astype(F32),
                jnp.zeros((bias_ref.shape[0], 128 - bias_ref.shape[1]), F32),
            ],
            axis=1,
        )
        bias_turned[...] = jnp.transpose(wide)[:16].astype(BF)
        for half in range(2):
            stage[half, all_rows:, :] = jnp.zeros((16 * queries_local - all_rows, 128), F32)
        hot = hots_ref[...].reshape(rows_all, hots_ref.shape[2])
        lane = lax.broadcasted_iota(jnp.int32, hot.shape, 1)
        zero = jnp.zeros_like(hot)
        expanded[0] = nn(jnp.where(lane < times, hot, zero)[:, :times], time_ref[...]).astype(BF)
        expanded[1] = nn(jnp.where(lane < times, zero, hot)[:, times:], class_ref[...]).astype(BF)
        grad_condition[...] = jnp.zeros_like(grad_condition)

    @pl.when(lax.rem(step, blocks) == 0)
    def _():
        chain = step // blocks
        for half in range(2):
            stage[half, 0:all_rows, :] = (
                scores_ref[chain, :, :, half * 128 : (half + 1) * 128]
                .reshape(all_rows, 128)
                .astype(F32)
            )

    @pl.when(step < 6)
    def _():
        member = lax.broadcasted_iota(jnp.int32, (rows_all, 1), 0)
        mine = jnp.where(lax.rem(member, 8) == step, 1.0, 0.0)
        rows = mods_ref[...].reshape(rows_all, width)
        time_rows = (expanded[0].astype(F32) * mine).astype(BF)
        class_rows = (expanded[1].astype(F32) * mine).astype(BF)
        grad_modulation_ref[...] = tn(time_rows, rows) + tn(class_rows, rows)
        grad_condition[...] += mine * nt(rows, modulation_ref[...])

    @pl.when(step == 6)
    def _():
        hot = hots_ref[...].reshape(rows_all, hots_ref.shape[2])
        rest = grad_condition[...]
        table = jnp.zeros((hot.shape[1], rest.shape[1]), F32)
        for _ in range(3):
            piece = rest.astype(BF)
            table = table + tn(hot, piece)
            rest = rest - piece.astype(F32)
        grad_time_ref[...] = table[:times]
        grad_class_ref[...] = table[times:]
        grad_bias_ref[...] = jnp.transpose(bias_grad_ref[...])[:, : 4 * heads]

    @pl.when(step == 7)
    def _():
        grad_down_ref[...] = jnp.transpose(weights_ref[0])
        for index in range(3):
            grad_input_ref[index] = weights_ref[1, :, index * local_width : (index + 1) * local_width]
        grad_output_ref[...] = jnp.transpose(weights_ref[1, :, 3 * local_width :])

    for row_index in range(PAIR_ROWS):
        place_row = lax.rem(step, blocks) * PAIR_ROWS + row_index
        rows = jnp.concatenate(
            [
                stage[half, pl.ds(place_row, 16, stride=queries_local), :].astype(BF)
                for half in range(2)
            ],
            axis=1,
        )
        grad_pair_ref[row_index] = tn(rows, bias_turned[...]).astype(BF)

    @pl.when(step == pl.num_programs(0) - 1)
    def _():
        for copy in copies():
            copy.wait()


def body(
    groups,
    tokens,
    pair_features,
    cotangent,
    chain_length,
    time_bin,
    cath_class,
    bias_weight,
    input_weight,
    output_weight,
    hidden_weight,
    down_weight,
    modulation_weight,
    time_table,
    class_table,
):
    chains, queries_local, span, channels = pair_features.shape
    local, width = tokens.shape
    local_width = input_weight.shape[2]
    hidden = down_weight.shape[0]
    heads = local_width // HD
    rows = chains * span
    chunk = width // groups
    assert chains == 2 and rows == 4 * local and span == 2 * local
    assert span == 256 and channels == 256 and 4 * local_width == width == hidden
    assert queries_local % PAIR_ROWS == 0
    dims = (groups, chains, span, local, width, local_width, queries_local, hidden)
    bits = groups.bit_length() - 1
    assert groups == 1 << bits
    straight = tuple(range(bits))
    orders = (straight, straight, straight, straight)
    n_table = time_table.shape[0] + class_table.shape[0]

    anywhere = pl.BlockSpec(memory_space=pl.ANY)
    scalars = pl.BlockSpec(memory_space=pltpu.SMEM)
    vmem = pltpu.VMEM
    half_rows = (chains, span, width)
    slots = (4, local, width)
    messages = 3 * 8 + 6 * 2 + 4 * bits + 3 * (groups - 1) + 5
    weights_shape = (4, chunk, width)
    outs = pl.pallas_call(
        functools.partial(layer_kernel, dims, orders),
        out_shape=(
            jax.ShapeDtypeStruct((local, width), BF),
            jax.ShapeDtypeStruct((local, width), BF),
            jax.ShapeDtypeStruct((chains, 4 * heads, queries_local, span), BF),
            jax.ShapeDtypeStruct((groups, 16, width), BF),
            jax.ShapeDtypeStruct((groups, 16, n_table), BF),
            jax.ShapeDtypeStruct((16, channels), F32),
            jax.ShapeDtypeStruct(weights_shape, F32),
        ),
        in_specs=[scalars] * 3 + [anywhere] * 11,
        out_specs=[anywhere] * 7,
        scratch_shapes=[
            vmem((local, width), BF),
            vmem((local, width), BF),
            vmem((PAIR_SLOTS, PAIR_ROWS, span, channels), BF),
            vmem(bias_weight.shape, BF),
            vmem(input_weight.shape, BF),
            vmem(output_weight.shape, BF),
            vmem(hidden_weight.shape, BF),
            vmem(down_weight.shape, BF),
            vmem(modulation_weight.shape, BF),
            vmem((n_table, time_table.shape[1]), BF),
            vmem((8, modulation_weight.shape[1]), F32),
            vmem((2, 16 * queries_local, 128), F32),
            vmem((groups, 16, n_table), BF),
            vmem((groups, 16, width), BF),
            vmem(slots, BF),
            vmem(slots, BF),
            vmem(slots, BF),
            vmem(slots, BF),
            vmem((chains, 4 * heads, queries_local, span), BF),
            vmem((chains, heads, span, span), BF),
            vmem((chains, span, local_width), BF),
            vmem((chains, span, local_width), BF),
            vmem((chains, span, local_width), BF),
            vmem((chains, heads * span, span), F32),
            vmem((chains, span, local_width), BF),
            vmem(slots, F32),
            vmem(slots, F32),
            vmem(half_rows, F32),
            vmem(half_rows, BF),
            vmem(half_rows, BF),
            vmem(half_rows, BF),
            vmem((chains, heads, span, span), BF),
            vmem((chains, 4 * heads, queries_local, span), BF),
            vmem((chains, span, 3 * local_width), BF),
            vmem((4, 3, local, width), BF),
            vmem((4, 3, local, width), BF),
            vmem((width, rows), BF),
            vmem((width, rows), BF),
            vmem((4, groups, chunk, width), BF),
            vmem((4, groups, chunk, width), BF),
            vmem(weights_shape, F32),
            vmem((local, width), F32),
            vmem((local, width), F32),
            vmem((local, width), F32),
            vmem((local, width), F32),
            vmem((local, width), F32),
            vmem((local, width), BF),
            vmem((local, width), BF),
            vmem((8, width), F32),
            vmem((8, width), F32),
            vmem((8, width), F32),
            vmem((8, width), F32),
            vmem((4, 16, channels), F32),
            vmem((groups, 16, channels), F32),
            vmem((16, channels), F32),
            pltpu.SemaphoreType.DMA((11,)),
            pltpu.SemaphoreType.DMA((PAIR_SLOTS,)),
            pltpu.SemaphoreType.DMA((8,)),
            pltpu.SemaphoreType.DMA((messages,)),
            pltpu.SemaphoreType.DMA((messages,)),
        ],
        compiler_params=pltpu.CompilerParams(
            collective_id=0, has_side_effects=True, vmem_limit_bytes=VMEM_BYTES
        ),
        name="layer",
    )(
        chain_length,
        time_bin,
        cath_class,
        tokens,
        cotangent,
        pair_features,
        bias_weight,
        input_weight,
        output_weight,
        hidden_weight,
        down_weight,
        modulation_weight,
        time_table,
        class_table,
    )
    result, grad_tokens, scores, mods_all, hots, bias_grad, weights = outs

    blocks = queries_local // PAIR_ROWS

    def whole(shape):
        return pl.BlockSpec(shape, lambda i: (0,) * len(shape))

    kept = weights
    sixth = modulation_weight.shape[1] // 6

    def by_vector(i):
        return (0, jnp.minimum(i, 5))

    outs = pl.pallas_call(
        functools.partial(finish_kernel, dims),
        grid=(chains * blocks,),
        out_shape=(
            jax.ShapeDtypeStruct((local, width), BF),
            jax.ShapeDtypeStruct((local, width), BF),
            jax.ShapeDtypeStruct(pair_features.shape, BF),
            jax.ShapeDtypeStruct(bias_weight.shape, F32),
            jax.ShapeDtypeStruct((3, chunk, local_width), F32),
            jax.ShapeDtypeStruct((local_width, chunk), F32),
            jax.ShapeDtypeStruct((2, chunk, hidden), F32),
            jax.ShapeDtypeStruct((hidden, chunk), F32),
            jax.ShapeDtypeStruct(modulation_weight.shape, F32),
            jax.ShapeDtypeStruct(time_table.shape, F32),
            jax.ShapeDtypeStruct(class_table.shape, F32),
        ),
        in_specs=[
            anywhere,
            anywhere,
            anywhere,
            whole(scores.shape),
            whole(mods_all.shape),
            whole(hots.shape),
            whole(bias_grad.shape),
            pl.BlockSpec((2, chunk, width), lambda i: (0, 0, 0)),
            whole(bias_weight.shape),
            pl.BlockSpec((modulation_weight.shape[0], sixth), by_vector),
            whole(time_table.shape),
            whole(class_table.shape),
        ],
        out_specs=[
            anywhere,
            anywhere,
            pl.BlockSpec(
                (None, PAIR_ROWS, span, channels), lambda i: (i // blocks, lax.rem(i, blocks), 0, 0)
            ),
            whole(bias_weight.shape),
            whole((3, chunk, local_width)),
            whole((local_width, chunk)),
            anywhere,
            whole((hidden, chunk)),
            pl.BlockSpec((modulation_weight.shape[0], sixth), by_vector),
            whole(time_table.shape),
            whole(class_table.shape),
        ],
        scratch_shapes=[
            vmem((2, 16 * queries_local, 128), F32),
            vmem((16, channels), BF),
            vmem((2, groups * 16, time_table.shape[1]), BF),
            vmem((groups * 16, time_table.shape[1]), F32),
            pltpu.SemaphoreType.DMA((4,)),
        ],
        compiler_params=pltpu.CompilerParams(vmem_limit_bytes=48 << 20),
        name="finish",
    )(
        result,
        grad_tokens,
        weights,
        scores,
        mods_all,
        hots,
        bias_grad,
        kept,
        bias_weight,
        modulation_weight,
        time_table,
        class_table,
    )
    return outs


def solution(mesh):
    placed = (
        P(("dp", "tensor"), None),
        P("dp", "tensor", None, None),
        P(("dp", "tensor"), None),
        P("dp"),
        P("dp"),
        P("dp"),
        P(),
        P(None, None, "tensor"),
        P("tensor", None),
        P(None, None, "tensor"),
        P("tensor", None),
        P(),
        P(),
        P(),
    )
    assert mesh.shape["tensor"] == 4
    return jax.shard_map(
        functools.partial(body, mesh.shape["dp"]),
        mesh=mesh,
        in_specs=placed,
        out_specs=(
            P(("dp", "tensor"), None),
            P(("dp", "tensor"), None),
            P("dp", "tensor", None, None),
            P(),
            P(None, "dp", "tensor"),
            P("tensor", "dp"),
            P(None, "dp", "tensor"),
            P("tensor", "dp"),
            P(),
            P(),
            P(),
        ),
        check_vma=False,
    )
```

```python
import functools

import jax
import jax.numpy as jnp
from jax import lax
from jax.experimental import pallas as pl
from jax.experimental.pallas import tpu as pltpu
from jax.sharding import PartitionSpec as P

HD = 64
EPSILON = 1e-05
BF = jnp.bfloat16
F32 = jnp.float32
MESH = pl.DeviceIdType.MESH
PAIR_SLOTS = 4
PAIR_ROWS = 16
VMEM_BYTES = 60 << 20
PIECES = (
    (0, 0, 384, 2),
    (0, 384, 384, 2),
    (2, 0, 384, 0),
    (2, 384, 384, 0),
    (3, 0, 384, 0),
    (3, 384, 384, 0),
    (1, 0, 256, 0),
    (1, 256, 256, 0),
    (1, 512, 256, 0),
)


def nn(a, b):
    return lax.dot_general(a, b, (((1,), (0,)), ((), ())), preferred_element_type=F32)


def nt(a, b):
    return lax.dot_general(a, b, (((1,), (1,)), ((), ())), preferred_element_type=F32)


def tn(a, b):
    return lax.dot_general(a, b, (((0,), (0,)), ((), ())), preferred_element_type=F32)


def sigmoid(x):
    return 1.0 / (1.0 + jnp.exp(-x))


def layer_norm(rows):
    centre = rows - jnp.mean(rows, axis=-1, keepdims=True)
    inverse = lax.rsqrt(jnp.mean(centre * centre, axis=-1, keepdims=True) + EPSILON)
    return centre * inverse, inverse


def norm_back(grad, normed, inverse):
    return inverse * (
        grad
        - jnp.mean(grad, axis=-1, keepdims=True)
        - normed * jnp.mean(grad * normed, axis=-1, keepdims=True)
    )


class Remote:
    def __init__(self, send_sems, recv_sems):
        self.send_sems, self.recv_sems, self.started = send_sems, recv_sems, []

    def start(self, src, dst, device):
        index = len(self.started)
        copy = pltpu.make_async_remote_copy(
            src_ref=src,
            dst_ref=dst,
            send_sem=self.send_sems.at[index],
            recv_sem=self.recv_sems.at[index],
            device_id=device,
            device_id_type=MESH,
        )
        copy.start()
        self.started.append(copy)
        return copy

    def finish(self):
        for copy in self.started:
            copy.wait_send()


class Gather:
    def __init__(self, remote, slots, here, near, far, near_device, far_device):
        self.remote, self.slots, self.far, self.near_device = remote, slots, far, near_device
        self.to_far = remote.start(slots.at[here], slots.at[here], far_device)
        self.to_near = remote.start(slots.at[here], slots.at[here], near_device)

    def forward(self):
        self.to_far.wait_recv()
        self.passed = self.remote.start(
            self.slots.at[self.far], self.slots.at[self.far], self.near_device
        )

    def wait_near(self):
        self.to_near.wait_recv()

    def wait_rest(self):
        self.passed.wait_recv()


class Scatter:
    def __init__(self, remote, part, out, arrived, ids, near_device, far_device):
        self.remote, self.part, self.out, self.arrived = remote, part, out, arrived
        self.here, self.near, self.far, self.cross = ids
        self.near_device, self.far_device = near_device, far_device

    def pre(self):
        self.out[0] = self.part[self.cross].astype(BF)
        self.first = self.remote.start(self.out.at[0], self.arrived.at[0], self.near_device)

    def across(self):
        self.first.wait_recv()
        self.out[1] = (self.part[self.far] + self.arrived[0].astype(F32)).astype(BF)
        self.second = self.remote.start(self.out.at[1], self.arrived.at[1], self.far_device)

    def local(self):
        self.out[2] = self.part[self.near].astype(BF)
        self.third = self.remote.start(self.out.at[2], self.arrived.at[2], self.near_device)
        self.own = self.part[self.here]

    def total(self):
        self.third.wait_recv()
        self.second.wait_recv()
        return self.own + self.arrived[2].astype(F32) + self.arrived[1].astype(F32)


class Halving:
    def __init__(self, remote, store, arrived, rank, count, device, order):
        self.remote, self.store, self.arrived = remote, store, arrived
        self.rank, self.count, self.device = rank, count, device
        self.order, self.step, self.offset, self.landing = order, 0, 0, 0

    def send(self):
        bit = self.order[self.step]
        self.half = self.count >> (self.step + 1)
        mine = lax.rem(self.rank // (1 << bit), 2)
        partner = self.rank + (1 - 2 * mine) * (1 << bit)
        away = self.offset + (1 - mine) * self.half
        self.offset = self.offset + mine * self.half
        self.copy = self.remote.start(
            self.store.at[pl.ds(away, self.half)],
            self.arrived.at[pl.ds(self.landing, self.half)],
            self.device(partner),
        )

    def sum(self):
        self.copy.wait_recv()
        keep = pl.ds(self.offset, self.half)
        total = self.store[keep].astype(F32) + self.arrived[
            pl.ds(self.landing, self.half)
        ].astype(F32)
        self.landing += self.half
        self.step += 1
        if self.step == len(self.order):
            self.result = total[0]
            return
        self.store[keep] = total.astype(BF)
        self.send()

    def finish(self):
        while self.step < len(self.order):
            self.sum()
        return self.result


def padded(rows):
    more = jnp.zeros((16 - rows.shape[0], rows.shape[1]), F32)
    return jnp.concatenate([rows.astype(F32), more], axis=0).astype(BF)


def slot_of(chunk, order):
    slot = 0
    for bit in order:
        slot = slot * 2 + (chunk >> bit) % 2
    return slot


def layer_kernel(
    dims,
    orders,
    length_ref,
    time_ref,
    class_ref,
    tokens_hbm,
    cotangent_hbm,
    pair_hbm,
    bias_hbm,
    input_hbm,
    output_hbm,
    hidden_hbm,
    down_hbm,
    modulation_hbm,
    time_hbm,
    class_hbm,
    result_out,
    grad_tokens_out,
    scores_out,
    mods_out,
    expanded_out,
    tables_out,
    bias_grad_out,
    weights_out,
    tokens,
    cotangent,
    pair,
    bias_weight,
    input_weight,
    output_weight,
    hidden_weight,
    down_weight,
    modulation_weight,
    tables,
    mods,
    stage,
    hots,
    mods_all,
    rows_attend,
    rows_hidden,
    rows_down,
    rows_out,
    bias_send,
    bias_full,
    queries,
    keys,
    values,
    probs,
    attended,
    part,
    part_down,
    grad_active,
    active,
    grad_gate,
    grad_up,
    grad_scores,
    scores_own,
    grad_projected,
    scatter_send,
    scatter_recv,
    turned,
    turned_more,
    final_weights,
    norm_attend,
    norm_hidden,
    middle,
    out_attend,
    grad_middle,
    result,
    grad_tokens,
    mod_part,
    mod_near,
    mod_sum,
    mod_far,
    bias_grads,
    bias_sums,
    bias_grad,
    expanded,
    tables_grad,
    load_sems,
    pair_sems,
    store_sems,
    send_sems,
    recv_sems,
    *piece_refs,
):
    piece_store, piece_recv = piece_refs[: len(PIECES)], piece_refs[len(PIECES) :]
    (groups, chains, span, local, width, local_width, queries_local, hidden) = dims
    heads = local_width // HD
    dp = lax.axis_index("dp")
    me = lax.axis_index("tensor")
    core = lax.rem(me, 2)
    chip = me // 2
    near = me + 1 - 2 * core
    far = lax.rem(me + 2, 4)
    cross = 3 - me
    away = 1 - chip
    near_device, far_device, cross_device = (dp, near), (dp, far), (dp, cross)

    def dp_device(index):
        return (index, me)

    barrier = pltpu.get_barrier_semaphore()
    for device in (near_device, far_device, cross_device):
        pl.semaphore_signal(barrier, inc=1, device_id=device, device_id_type=MESH)
    for step in range(1, groups):
        pl.semaphore_signal(
            barrier, inc=1, device_id=dp_device(lax.rem(dp + step, groups)), device_id_type=MESH
        )

    loads = []

    def load(src, dst):
        copy = pltpu.make_async_copy(src, dst, load_sems.at[len(loads)])
        copy.start()
        loads.append(copy)
        return copy

    blocks = queries_local // PAIR_ROWS
    n_blocks = chains * blocks

    def pair_copy(index):
        chain = lax.rem(chip + index // blocks, chains)
        slot = lax.rem(index, PAIR_SLOTS)
        return pltpu.make_async_copy(
            pair_hbm.at[chain, pl.ds(lax.rem(index, blocks) * PAIR_ROWS, PAIR_ROWS)],
            pair.at[slot],
            pair_sems.at[slot],
        )

    times = time_hbm.shape[0]
    load_time = load(time_hbm, tables.at[pl.ds(0, times)])
    load_class = load(class_hbm, tables.at[pl.ds(times, class_hbm.shape[0])])
    load_tokens = load(tokens_hbm, tokens)
    load_modulation = load(modulation_hbm, modulation_weight)
    load_cotangent = load(cotangent_hbm, cotangent)
    load_bias = load(bias_hbm, bias_weight)
    pair_copy(0).start()

    remote = Remote(send_sems, recv_sems)

    n_table = tables.shape[0]
    lane = lax.broadcasted_iota(jnp.int32, (16, n_table), 1)
    row = lax.broadcasted_iota(jnp.int32, (16, n_table), 0)
    picked = ((row == 0) & (lane == time_ref[chip])) | (
        (row == 1) & (lane == times + class_ref[chip])
    )
    time_row = jnp.where(row < 8, time_ref[0], time_ref[1])
    class_row = jnp.where(row < 8, class_ref[0], class_ref[1])
    hots[dp] = jnp.where((lane == time_row) | (lane == times + class_row), 1.0, 0.0).astype(BF)
    load_time.wait()
    load_class.wait()
    condition = nn(jnp.where(picked, 1.0, 0.0).astype(BF), tables[...]).astype(BF)
    load_modulation.wait()
    for index in range(1, PAIR_SLOTS):
        pair_copy(index).start()
    load_input = load(input_hbm, input_weight)
    both = nn(condition, modulation_weight[...])
    mods[...] = jnp.broadcast_to(both[0:1] + both[1:2], mods.shape)

    def mod(index):
        return mods[0:1, index * width : (index + 1) * width]

    place = lax.rem(me * local, span) + lax.broadcasted_iota(jnp.int32, (local, 1), 0)
    valid = jnp.where(place < length_ref[chip], 1.0, 0.0)

    load_tokens.wait()
    normed, inverse_attend = layer_norm(tokens[...].astype(F32))
    norm_attend[...] = normed
    rows_attend[me] = (normed * (1.0 + mod(0)) + mod(1)).astype(BF)
    load_cotangent.wait()
    gate_hidden = sigmoid(mod(5))
    rows_down[me] = (cotangent[...].astype(F32) * valid * gate_hidden).astype(BF)
    load_bias.wait()
    bias_rows = padded(bias_weight[...])

    pl.semaphore_wait(barrier, 3 + groups - 1)
    gather_attend = Gather(remote, rows_attend, me, near, far, near_device, far_device)
    hot_copies = []
    for step in range(1, groups):
        device = dp_device(lax.rem(dp + step, groups))
        hot_copies.append(remote.start(hots.at[dp], hots.at[dp], device))

    def bias_block(index, carry):
        slot = lax.rem(index, PAIR_SLOTS)
        pair_copy(index).wait()
        for row_index in range(PAIR_ROWS):
            product = nt(bias_rows, pair[slot, row_index])
            place_row = lax.rem(index, blocks) * PAIR_ROWS + row_index
            for half in range(2):
                stage[half, pl.ds(place_row, 16, stride=queries_local), :] = product[
                    :, half * 128 : (half + 1) * 128
                ]

        @pl.when(index + PAIR_SLOTS < n_blocks)
        def _():
            pair_copy(index + PAIR_SLOTS).start()

        return carry

    all_rows = 4 * heads * queries_local
    bias_copies = []
    for turn in range(2):
        chain = lax.rem(chip + turn, 2)
        lax.fori_loop(turn * blocks, (turn + 1) * blocks, bias_block, 0)
        for half in range(2):
            bias_send[chain, :, :, half * 128 : (half + 1) * 128] = (
                stage[half, 0:all_rows, :].astype(BF).reshape(4 * heads, queries_local, 128)
            )
        mine = pl.ds(me * queries_local, queries_local)
        sent = []
        for owner, device in ((far, far_device), (cross, cross_device), (near, near_device)):
            sent.append(
                remote.start(
                    bias_send.at[chain, pl.ds(owner * heads, heads)],
                    bias_full.at[chain, :, mine],
                    device,
                )
            )
        bias_copies.append(sent)
        bias_full[chain, :, mine, :] = bias_send[chain, pl.ds(me * heads, heads)]
        if turn == 0:
            gather_attend.forward()
            load_output = load(output_hbm, output_weight)
            load_down = load(down_hbm, down_weight)
            load_hidden = load(hidden_hbm, hidden_weight)

    gather_down = Gather(remote, rows_down, me, near, far, near_device, far_device)

    for index in range(PAIR_SLOTS):
        pair_copy(index).start()

    load_input.wait()

    def project(half):
        rows = rows_attend[pl.ds(2 * half, 2)].reshape(span, width)
        queries[half] = nt(rows, input_weight[0]).astype(BF)
        keys[half] = nt(rows, input_weight[1]).astype(BF)
        values[half] = nt(rows, input_weight[2]).astype(BF)

    gather_attend.wait_near()
    project(chip)
    gather_attend.wait_rest()
    project(away)

    head_lane = lax.broadcasted_iota(jnp.int32, (span, local_width), 1)

    def stacked(rows):
        zero = jnp.zeros_like(rows)
        return jnp.concatenate(
            [
                jnp.where((head_lane >= head * HD) & (head_lane < (head + 1) * HD), rows, zero)
                for head in range(heads)
            ],
            axis=0,
        )

    def choose(pieces):
        out = pieces[-1]
        for head in range(heads - 2, -1, -1):
            out = jnp.where(head_lane < (head + 1) * HD, pieces[head], out)
        return out

    def attend(chain):
        scores = nt(stacked(queries[chain]), keys[chain]) * HD ** (-0.5) + bias_full[
            chain
        ].reshape(heads * span, span).astype(F32)
        key_place = lax.broadcasted_iota(jnp.int32, (heads * span, span), 1)
        scores = jnp.where(key_place < length_ref[chain], scores, -1000000000.0)
        top = jnp.max(scores, axis=-1, keepdims=True)
        weights = jnp.exp(scores - top)
        weights = weights * (1.0 / jnp.sum(weights, axis=-1, keepdims=True))
        probs[chain] = weights
        soft = weights.astype(BF)
        attended[chain] = choose(
            [nn(soft[head * span : (head + 1) * span], values[chain]) for head in range(heads)]
        ).astype(BF)

    def put(target, half, rows):
        target[pl.ds(2 * half, 2)] = rows.reshape(2, local, width)

    ids = (me, near, far, cross)

    def scatter(index, source):
        return Scatter(
            remote,
            source,
            scatter_send.at[index],
            scatter_recv.at[index],
            ids,
            near_device,
            far_device,
        )

    bias_copies[0][0].wait_recv()
    bias_copies[0][1].wait_recv()
    bias_copies[1][2].wait_recv()
    attend(away)
    load_output.wait()
    put(part, away, nn(attended[away], output_weight[...]))
    scatter_attend = scatter(0, part)
    scatter_attend.pre()
    bias_copies[1][0].wait_recv()
    bias_copies[1][1].wait_recv()
    bias_copies[0][2].wait_recv()
    scatter_attend.across()
    attend(chip)
    put(part, chip, nn(attended[chip], output_weight[...]))
    scatter_attend.local()

    load_down.wait()

    def back_down(half):
        rows = rows_down[pl.ds(2 * half, 2)].reshape(span, width)
        grad_active[half] = nt(rows, down_weight[...])
        for slot in range(2):
            place_slot = 2 * half + slot
            turned[:, pl.ds(pl.multiple_of(place_slot * local, local), local)] = jnp.transpose(
                rows[slot * local : (slot + 1) * local]
            )

    gather_down.forward()
    gather_down.wait_near()
    back_down(chip)
    gather_down.wait_rest()
    back_down(away)

    gate_attend = sigmoid(mod(2))
    out_total = scatter_attend.total()
    out_attend[...] = out_total
    total = tokens[...].astype(F32) + valid * gate_attend * out_total
    middle[...] = total
    normed, inverse_hidden = layer_norm(total)
    norm_hidden[...] = normed
    rows_hidden[me] = (normed * (1.0 + mod(3)) + mod(4)).astype(BF)
    gather_hidden = Gather(remote, rows_hidden, me, near, far, near_device, far_device)

    load_hidden.wait()

    def transition(half):
        rows = rows_hidden[pl.ds(2 * half, 2)].reshape(span, width)
        gate = nn(rows, hidden_weight[0])
        up = nn(rows, hidden_weight[1])
        squashed = sigmoid(gate)
        silu = gate * squashed
        active[half] = (silu * up).astype(BF)
        back = grad_active[half]
        grad_gate[half] = (back * up * squashed * (1.0 + gate * (1.0 - squashed))).astype(BF)
        grad_up[half] = (back * silu).astype(BF)

    def back_hidden(half):
        put(
            part,
            half,
            nt(grad_gate[half], hidden_weight[0]) + nt(grad_up[half], hidden_weight[1]),
        )

    chunk = width // groups
    per_block = max(1, 192 // chunk)

    def weight_grad(pieces, *pairs):
        for block in range(groups // per_block):
            rows = slice(block * per_block * chunk, (block + 1) * per_block * chunk)
            product = jnp.concatenate([nn(left[rows, :], right) for left, right in pairs], axis=1)
            for index in pieces:
                first, size = PIECES[index][1:3]
                for inner in range(per_block):
                    slot = slot_of(block * per_block + inner, orders[index])
                    piece_store[index][slot] = product[
                        inner * chunk : (inner + 1) * chunk, first : first + size
                    ].astype(BF)
        for index in pieces:
            sums[index] = Halving(
                remote,
                piece_store[index],
                piece_recv[index],
                dp,
                groups,
                dp_device,
                orders[index],
            )
            sums[index].send()

    sums = {}

    def advance(*indices):
        for index in indices:
            sums[index].sum()

    def complete(*indices):
        for index in indices:
            matrix, first, size = PIECES[index][:3]
            final_weights[matrix, :, first : first + size] = sums[index].finish()

    def flat(ref):
        return ref[...].reshape(chains * span, ref.shape[-1])

    def turn_rows(source, target):
        for slot in range(4):
            target[:, slot * local : (slot + 1) * local] = jnp.transpose(source[slot])

    gather_hidden.wait_near()
    transition(chip)
    gather_hidden.forward()
    back_hidden(chip)
    put(part_down, chip, nn(active[chip], down_weight[...]))
    gather_hidden.wait_rest()
    transition(away)
    weight_grad((0, 1), (turned, flat(active)))
    back_hidden(away)
    scatter_hidden = scatter(1, part)
    scatter_hidden.pre()
    put(part_down, away, nn(active[away], down_weight[...]))
    scatter_hidden.across()
    scatter_hidden.local()
    scatter_down = scatter(2, part_down)
    scatter_down.pre()

    scatter_down.across()
    scatter_down.local()
    turn_rows(rows_hidden, turned_more)
    weight_grad((2, 3), (turned_more, flat(grad_gate)))

    grad_h = scatter_hidden.total()
    normed = norm_hidden[...]
    back = cotangent[...].astype(F32) + norm_back(grad_h * (1.0 + mod(3)), normed, inverse_hidden)
    grad_middle[...] = back
    rows_out[me] = (back * valid * gate_attend).astype(BF)
    gather_out = Gather(remote, rows_out, me, near, far, near_device, far_device)

    weight_grad((4, 5), (turned_more, flat(grad_up)))

    def keep_mod(index, rows):
        mod_part[index : index + 1, :] = jnp.sum(rows, axis=0, keepdims=True)

    mod_part[...] = jnp.zeros_like(mod_part)
    keep_mod(3, grad_h * normed)
    keep_mod(4, grad_h)
    keep_mod(2, back * valid * out_attend[...] * gate_attend * (1.0 - gate_attend))
    out_total = scatter_down.total()
    result[...] = (middle[...] + valid * gate_hidden * out_total).astype(BF)
    keep_mod(
        5, cotangent[...].astype(F32) * valid * out_total * gate_hidden * (1.0 - gate_hidden)
    )
    turn_rows(rows_attend, turned)

    score_copies = []

    def back_attend(chain):
        rows = rows_out[pl.ds(2 * chain, 2)].reshape(span, width)
        grad_heads = stacked(nt(rows, output_weight[...]).astype(BF))
        weights = probs[chain]
        grad_probs = nt(grad_heads, values[chain])
        grad_logits = (
            weights * (grad_probs - jnp.sum(grad_probs * weights, axis=-1, keepdims=True))
        ).astype(BF)
        grad_scores[chain] = grad_logits.reshape(heads, span, span)
        sent = []
        for owner, device in ((far, far_device), (cross, cross_device), (near, near_device)):
            sent.append(
                remote.start(
                    grad_scores.at[chain, :, pl.ds(owner * queries_local, queries_local)],
                    scores_own.at[chain, pl.ds(me * heads, heads)],
                    device,
                )
            )
        score_copies.append(sent)
        scores_own[chain, pl.ds(me * heads, heads)] = grad_scores[
            chain, :, pl.ds(me * queries_local, queries_local), :
        ]
        query_stack = stacked(queries[chain])
        grad_query = (
            choose(
                [
                    nn(grad_logits[head * span : (head + 1) * span], keys[chain])
                    for head in range(heads)
                ]
            )
            * HD ** (-0.5)
        ).astype(BF)
        grad_key = (tn(grad_logits, query_stack) * HD ** (-0.5)).astype(BF)
        grad_value = tn(weights.astype(BF), grad_heads).astype(BF)
        grad_projected[chain] = jnp.concatenate([grad_query, grad_key, grad_value], axis=1)
        put(
            part,
            chain,
            nn(grad_query, input_weight[0])
            + nn(grad_key, input_weight[1])
            + nn(grad_value, input_weight[2]),
        )

    gather_out.wait_near()
    gather_out.forward()
    back_attend(chip)
    advance(0, 2)
    gather_out.wait_rest()
    back_attend(away)
    scatter_input = scatter(3, part)
    scatter_input.pre()
    turn_rows(rows_out, turned_more)
    scatter_input.across()
    scatter_input.local()
    weight_grad((6, 7, 8), (turned, flat(grad_projected)), (turned_more, flat(attended)))
    advance(1, 3)
    stores = []

    def store(src, dst):
        copy = pltpu.make_async_copy(src, dst, store_sems.at[len(stores)])
        copy.start()
        stores.append(copy)

    for sent in score_copies:
        for copy in sent:
            copy.wait_recv()
    store(scores_own, scores_out)
    def bias_grad_block(index, total):
        slot = lax.rem(index, PAIR_SLOTS)
        pair_copy(index).wait()
        for row_index in range(PAIR_ROWS):
            place_row = lax.rem(index, blocks) * PAIR_ROWS + row_index
            rows = jnp.concatenate(
                [
                    stage[half, pl.ds(place_row, 16, stride=queries_local), :].astype(BF)
                    for half in range(2)
                ],
                axis=1,
            )
            total = total + nn(rows, pair[slot, row_index])

        @pl.when(index + PAIR_SLOTS < n_blocks)
        def _():
            pair_copy(index + PAIR_SLOTS).start()

        return total

    def bias_grad_chain(turn, total):
        chain = lax.rem(chip + turn, 2)
        for half in range(2):
            stage[half, 0:all_rows, :] = (
                scores_own[chain, :, :, half * 128 : (half + 1) * 128]
                .reshape(all_rows, 128)
                .astype(F32)
            )
            stage[half, all_rows:, :] = jnp.zeros((16 * queries_local - all_rows, 128), F32)
        return lax.fori_loop(turn * blocks, (turn + 1) * blocks, bias_grad_block, total)

    total = bias_grad_chain(0, jnp.zeros((16, pair_hbm.shape[3]), F32))
    advance(0, 2, 4)
    bias_grads[0] = bias_grad_chain(1, total)
    tensor_copies = [
        remote.start(bias_grads.at[0], bias_grads.at[1 + index], device)
        for index, device in enumerate((near_device, far_device, cross_device))
    ]

    grad_h = scatter_input.total()
    normed = norm_attend[...]
    grad_tokens[...] = (
        grad_middle[...] + norm_back(grad_h * (1.0 + mod(0)), normed, inverse_attend)
    ).astype(BF)
    keep_mod(0, grad_h * normed)
    keep_mod(1, grad_h)
    to_near = remote.start(mod_part, mod_near, near_device)

    store(result, result_out)
    store(grad_tokens, grad_tokens_out)

    advance(1, 3)

    to_near.wait_recv()
    mod_sum[...] = mod_part[...] + mod_near[...]
    to_far = remote.start(mod_sum, mod_far, far_device)
    for copy in tensor_copies:
        copy.wait_recv()
    bias_sums[0] = bias_grads[0] + bias_grads[1] + bias_grads[2] + bias_grads[3]
    bias_copies = [
        remote.start(bias_sums.at[0], bias_sums.at[step], dp_device(lax.rem(dp + step, groups)))
        for step in range(1, groups)
    ]
    advance(5)
    to_far.wait_recv()
    own, other = mod_sum[...], mod_far[...]
    low = jnp.where(chip == 0, own, other)
    high = jnp.where(chip == 0, other, own)
    mods_all[dp] = jnp.concatenate([low, high], axis=0).astype(BF)
    mod_copies = [
        remote.start(mods_all.at[dp], mods_all.at[dp], dp_device(lax.rem(dp + step, groups)))
        for step in range(1, groups)
    ]
    complete(2)
    advance(4, 6)
    complete(3)
    store(final_weights.at[2], weights_out.at[2])
    for copy in hot_copies:
        copy.wait_recv()
    rows_all = groups * 16
    hot = hots[...].reshape(rows_all, n_table)
    hot_lane = lax.broadcasted_iota(jnp.int32, hot.shape, 1)
    zero = jnp.zeros_like(hot)
    time_rows = nn(jnp.where(hot_lane < times, hot, zero), tables[...])
    class_rows = nn(jnp.where(hot_lane < times, zero, hot), tables[...])
    expanded[:, :rows_all] = jnp.transpose(time_rows)
    expanded[:, rows_all:] = jnp.transpose(class_rows)
    store(expanded, expanded_out)
    advance(5, 7)
    complete(4)
    advance(6, 8)
    for copy in mod_copies:
        copy.wait_recv()
    store(mods_all, mods_out)
    rows = mods_all[...].reshape(rows_all, width)
    member = lax.rem(lax.broadcasted_iota(jnp.int32, (rows_all, 1), 0), 8)
    rest = jnp.zeros((rows_all, tables.shape[1]), F32)
    for vector in range(6):
        product = nt(rows, modulation_weight[:, vector * width : (vector + 1) * width])
        rest = rest + jnp.where(member == vector, product, 0.0)
    table = jnp.zeros((n_table, tables.shape[1]), F32)
    for _ in range(3):
        piece = rest.astype(BF)
        table = table + tn(hot, piece)
        rest = rest - piece.astype(F32)
    tables_grad[...] = table
    store(tables_grad, tables_out)
    complete(0, 5)
    store(final_weights.at[3], weights_out.at[3])
    advance(7)
    complete(1)
    store(final_weights.at[0], weights_out.at[0])
    for copy in bias_copies:
        copy.wait_recv()
    bias_grad[...] = jnp.sum(bias_sums[...], axis=0)
    store(bias_grad, bias_grad_out)
    complete(6)
    advance(8)
    complete(7, 8)
    store(final_weights.at[1], weights_out.at[1])
    for copy in stores:
        copy.wait()
    remote.finish()


def finish_kernel(
    dims,
    result_hbm,
    grad_tokens_hbm,
    weights_hbm,
    scores_hbm,
    mods_hbm,
    expanded_hbm,
    tables_hbm,
    bias_grad_hbm,
    bias_hbm,
    result_out,
    grad_tokens_out,
    pair_out,
    bias_grad_out,
    input_out,
    output_out,
    hidden_out,
    down_out,
    modulation_out,
    time_out,
    class_out,
    rows_pass,
    weights,
    scores,
    mods,
    expanded,
    tables,
    bias_grad,
    bias,
    places,
    pair,
    modulation,
    input_grad,
    output_grad,
    bias_rows,
    load_sems,
    pair_sems,
    store_sems,
):
    (groups, chains, span, local, width, local_width, queries_local, hidden) = dims
    heads = local_width // HD
    blocks = queries_local // PAIR_ROWS
    times = time_out.shape[0]

    def start(src, dst, semaphore):
        copy = pltpu.make_async_copy(src, dst, semaphore)
        copy.start()
        return copy

    moves = (
        (bias_hbm, bias),
        (scores_hbm.at[0], scores.at[0]),
        (scores_hbm.at[1], scores.at[1]),
        (expanded_hbm, expanded),
        (mods_hbm, mods),
        (weights_hbm, weights),
        (result_hbm, rows_pass.at[0]),
        (grad_tokens_hbm, rows_pass.at[1]),
        (tables_hbm, tables),
        (bias_grad_hbm, bias_grad),
    )
    loads = [start(src, dst, load_sems.at[index]) for index, (src, dst) in enumerate(moves)]

    loads[0].wait()
    weight_rows = bias[...].astype(F32)
    spread = jnp.concatenate(
        [
            jnp.broadcast_to(weight_rows[head : head + 1], (PAIR_ROWS, weight_rows.shape[1]))
            for head in range(4 * heads)
        ],
        axis=0,
    )
    member = lax.rem(lax.broadcasted_iota(jnp.int32, spread.shape, 0), PAIR_ROWS)
    for row_index in range(PAIR_ROWS):
        places[row_index] = jnp.where(member == row_index, spread, 0.0).astype(BF)

    def pair_copy(index):
        slot = lax.rem(index, PAIR_SLOTS)
        return pltpu.make_async_copy(
            pair.at[slot],
            pair_out.at[
                index // blocks, pl.ds(lax.rem(index, blocks) * PAIR_ROWS, PAIR_ROWS)
            ],
            pair_sems.at[slot],
        )

    def pair_block(index, carry):
        @pl.when(index >= PAIR_SLOTS)
        def _():
            pair_copy(index - PAIR_SLOTS).wait()

        rows = scores[index // blocks, :, pl.ds(lax.rem(index, blocks) * PAIR_ROWS, PAIR_ROWS)]
        across = jnp.transpose(rows.reshape(4 * heads * PAIR_ROWS, rows.shape[2]))
        slot = lax.rem(index, PAIR_SLOTS)
        for row_index in range(PAIR_ROWS):
            pair[slot, row_index] = nn(across, places[row_index]).astype(BF)
        pair_copy(index).start()
        return carry

    n_blocks = chains * blocks
    loads[1].wait()
    loads[2].wait()
    lax.fori_loop(0, n_blocks, pair_block, 0)

    stores = []

    def store(src, dst):
        stores.append(start(src, dst, store_sems.at[len(stores)]))

    loads[3].wait()
    loads[4].wait()
    rows = mods[...].reshape(groups * 16, width)
    both = jnp.concatenate([rows, rows], axis=0)
    lane = lax.rem(lax.broadcasted_iota(jnp.int32, expanded.shape, 1), 8)
    for vector in range(6):
        left = jnp.where(lane == vector, expanded[...], 0.0).astype(BF)
        modulation[vector] = nn(left, both)
        store(modulation.at[vector], modulation_out.at[:, pl.ds(vector * width, width)])
    for copy in loads[5:]:
        copy.wait()
    store(weights.at[0], down_out)
    store(weights.at[2], hidden_out.at[0])
    store(weights.at[3], hidden_out.at[1])
    store(rows_pass.at[0], result_out)
    store(rows_pass.at[1], grad_tokens_out)
    store(tables.at[pl.ds(0, times)], time_out)
    store(tables.at[pl.ds(times, class_out.shape[0])], class_out)
    bias_rows[...] = bias_grad[: 4 * heads]
    store(bias_rows, bias_grad_out)
    for index in range(3):
        input_grad[index] = weights[1, :, index * local_width : (index + 1) * local_width]
    store(input_grad, input_out)
    output_grad[...] = jnp.transpose(weights[1, :, 3 * local_width :])
    store(output_grad, output_out)
    for index in range(n_blocks - PAIR_SLOTS, n_blocks):
        pair_copy(index).wait()
    for copy in stores:
        copy.wait()


def body(
    groups,
    tokens,
    pair_features,
    cotangent,
    chain_length,
    time_bin,
    cath_class,
    bias_weight,
    input_weight,
    output_weight,
    hidden_weight,
    down_weight,
    modulation_weight,
    time_table,
    class_table,
):
    chains, queries_local, span, channels = pair_features.shape
    local, width = tokens.shape
    local_width = input_weight.shape[2]
    hidden = down_weight.shape[0]
    heads = local_width // HD
    rows = chains * span
    chunk = width // groups
    assert chains == 2 and rows == 4 * local and span == 2 * local
    assert span == 256 and channels == 256 and 4 * local_width == width == hidden
    assert queries_local % PAIR_ROWS == 0
    dims = (groups, chains, span, local, width, local_width, queries_local, hidden)
    bits = groups.bit_length() - 1
    assert groups == 1 << bits
    straight = tuple(range(bits))
    turns = (straight, straight[1:2] + straight[:1] + straight[2:], straight[1:] + straight[:1])
    orders = tuple(turns[piece[3]] for piece in PIECES)
    n_table = time_table.shape[0] + class_table.shape[0]
    input_turned = jnp.swapaxes(input_weight, 1, 2)
    bias_turned = bias_weight.T

    anywhere = pl.BlockSpec(memory_space=pl.ANY)
    scalars = pl.BlockSpec(memory_space=pltpu.SMEM)
    vmem = pltpu.VMEM
    half_rows = (chains, span, width)
    slots = (4, local, width)
    messages = 3 * 8 + 6 * 2 + len(PIECES) * bits + 3 * (groups - 1) + 5
    weights_shape = (4, chunk, width)
    outs = pl.pallas_call(
        functools.partial(layer_kernel, dims, orders),
        out_shape=(
            jax.ShapeDtypeStruct((local, width), BF),
            jax.ShapeDtypeStruct((local, width), BF),
            jax.ShapeDtypeStruct((chains, 4 * heads, queries_local, span), BF),
            jax.ShapeDtypeStruct((groups, 16, width), BF),
            jax.ShapeDtypeStruct((time_table.shape[1], 2 * groups * 16), F32),
            jax.ShapeDtypeStruct((n_table, time_table.shape[1]), F32),
            jax.ShapeDtypeStruct((16, channels), F32),
            jax.ShapeDtypeStruct(weights_shape, F32),
        ),
        in_specs=[scalars] * 3 + [anywhere] * 11,
        out_specs=[anywhere] * 8,
        scratch_shapes=[
            vmem((local, width), BF),
            vmem((local, width), BF),
            vmem((PAIR_SLOTS, PAIR_ROWS, span, channels), BF),
            vmem(bias_turned.shape, BF),
            vmem(input_turned.shape, BF),
            vmem(output_weight.shape, BF),
            vmem(hidden_weight.shape, BF),
            vmem(down_weight.shape, BF),
            vmem(modulation_weight.shape, BF),
            vmem((n_table, time_table.shape[1]), BF),
            vmem((8, modulation_weight.shape[1]), F32),
            vmem((2, 16 * queries_local, 128), F32),
            vmem((groups, 16, n_table), BF),
            vmem((groups, 16, width), BF),
            vmem(slots, BF),
            vmem(slots, BF),
            vmem(slots, BF),
            vmem(slots, BF),
            vmem((chains, 4 * heads, queries_local, span), BF),
            vmem((chains, heads, span, span), BF),
            vmem((chains, span, local_width), BF),
            vmem((chains, span, local_width), BF),
            vmem((chains, span, local_width), BF),
            vmem((chains, heads * span, span), F32),
            vmem((chains, span, local_width), BF),
            vmem(slots, F32),
            vmem(slots, F32),
            vmem(half_rows, F32),
            vmem(half_rows, BF),
            vmem(half_rows, BF),
            vmem(half_rows, BF),
            vmem((chains, heads, span, span), BF),
            vmem((chains, 4 * heads, queries_local, span), BF),
            vmem((chains, span, 3 * local_width), BF),
            vmem((4, 3, local, width), BF),
            vmem((4, 3, local, width), BF),
            vmem((width, rows), BF),
            vmem((width, rows), BF),
            vmem(weights_shape, F32),
            vmem((local, width), F32),
            vmem((local, width), F32),
            vmem((local, width), F32),
            vmem((local, width), F32),
            vmem((local, width), F32),
            vmem((local, width), BF),
            vmem((local, width), BF),
            vmem((8, width), F32),
            vmem((8, width), F32),
            vmem((8, width), F32),
            vmem((8, width), F32),
            vmem((4, 16, channels), F32),
            vmem((groups, 16, channels), F32),
            vmem((16, channels), F32),
            vmem((time_table.shape[1], 2 * groups * 16), F32),
            vmem((n_table, time_table.shape[1]), F32),
            pltpu.SemaphoreType.DMA((11,)),
            pltpu.SemaphoreType.DMA((PAIR_SLOTS,)),
            pltpu.SemaphoreType.DMA((14,)),
            pltpu.SemaphoreType.DMA((messages,)),
            pltpu.SemaphoreType.DMA((messages,)),
        ]
        + [vmem((groups, chunk, piece[2]), BF) for piece in PIECES] * 2,
        compiler_params=pltpu.CompilerParams(
            collective_id=0, has_side_effects=True, vmem_limit_bytes=VMEM_BYTES
        ),
        name="layer",
    )(
        chain_length,
        time_bin,
        cath_class,
        tokens,
        cotangent,
        pair_features,
        bias_turned,
        input_turned,
        output_weight,
        hidden_weight,
        down_weight,
        modulation_weight,
        time_table,
        class_table,
    )
    result, grad_tokens, scores, mods_all, expanded, tables, bias_grad, weights = outs

    outs = pl.pallas_call(
        functools.partial(finish_kernel, dims),
        out_shape=(
            jax.ShapeDtypeStruct((local, width), BF),
            jax.ShapeDtypeStruct((local, width), BF),
            jax.ShapeDtypeStruct(pair_features.shape, BF),
            jax.ShapeDtypeStruct(bias_turned.shape, F32),
            jax.ShapeDtypeStruct((3, chunk, local_width), F32),
            jax.ShapeDtypeStruct((local_width, chunk), F32),
            jax.ShapeDtypeStruct((2, chunk, hidden), F32),
            jax.ShapeDtypeStruct((chunk, hidden), F32),
            jax.ShapeDtypeStruct(modulation_weight.shape, F32),
            jax.ShapeDtypeStruct(time_table.shape, F32),
            jax.ShapeDtypeStruct(class_table.shape, F32),
        ),
        in_specs=[anywhere] * 9,
        out_specs=[anywhere] * 11,
        scratch_shapes=[
            vmem((2, local, width), BF),
            vmem(weights.shape, F32),
            vmem(scores.shape, BF),
            vmem(mods_all.shape, BF),
            vmem(expanded.shape, F32),
            vmem(tables.shape, F32),
            vmem(bias_grad.shape, F32),
            vmem(bias_turned.shape, BF),
            vmem((PAIR_ROWS, 4 * heads * PAIR_ROWS, channels), BF),
            vmem((PAIR_SLOTS, PAIR_ROWS, span, channels), BF),
            vmem((6, modulation_weight.shape[0], width), F32),
            vmem((3, chunk, local_width), F32),
            vmem((local_width, chunk), F32),
            vmem(bias_turned.shape, F32),
            pltpu.SemaphoreType.DMA((10,)),
            pltpu.SemaphoreType.DMA((PAIR_SLOTS,)),
            pltpu.SemaphoreType.DMA((16,)),
        ],
        compiler_params=pltpu.CompilerParams(vmem_limit_bytes=VMEM_BYTES),
        name="finish",
    )(
        result,
        grad_tokens,
        weights,
        scores,
        mods_all,
        expanded,
        tables,
        bias_grad,
        bias_turned,
    )
    outs = list(outs)
    outs[3], outs[7] = outs[3].T, outs[7].T
    return tuple(outs)


def solution(mesh):
    placed = (
        P(("dp", "tensor"), None),
        P("dp", "tensor", None, None),
        P(("dp", "tensor"), None),
        P("dp"),
        P("dp"),
        P("dp"),
        P(),
        P(None, None, "tensor"),
        P("tensor", None),
        P(None, None, "tensor"),
        P("tensor", None),
        P(),
        P(),
        P(),
    )
    assert mesh.shape["tensor"] == 4
    return jax.shard_map(
        functools.partial(body, mesh.shape["dp"]),
        mesh=mesh,
        in_specs=placed,
        out_specs=(
            P(("dp", "tensor"), None),
            P(("dp", "tensor"), None),
            P("dp", "tensor", None, None),
            P(),
            P(None, "dp", "tensor"),
            P("tensor", "dp"),
            P(None, "dp", "tensor"),
            P("tensor", "dp"),
            P(),
            P(),
            P(),
        ),
        check_vma=False,
    )
```

```python
import functools

import jax
import jax.numpy as jnp
from jax import lax
from jax.experimental import pallas as pl
from jax.experimental.pallas import tpu as pltpu
from jax.sharding import PartitionSpec as P

HD = 64
EPSILON = 1e-05
BF = jnp.bfloat16
F32 = jnp.float32
MESH = pl.DeviceIdType.MESH
PAIR_SLOTS = 4
PAIR_ROWS = 16
GATHER_PARTS = 2
VMEM_BYTES = 60 << 20
PIECES = (
    (0, 0, 384, 0),
    (0, 384, 384, 2),
    (2, 0, 384, 1),
    (2, 384, 384, 0),
    (3, 0, 384, 0),
    (3, 384, 384, 1),
    (1, 0, 256, 0),
    (1, 256, 256, 0),
    (1, 512, 256, 0),
)
SUMS = (
    (0, 2),
    (1, 3),
    (0, 2, 4),
    (1, 3),
    (5,),
    (2, 4, 6, 3),
    (5, 7, 4, 6, 8),
    (0, 5, 7, 1, 6, 8, 7, 8),
)


def nn(a, b):
    return lax.dot_general(a, b, (((1,), (0,)), ((), ())), preferred_element_type=F32)


def nt(a, b):
    return lax.dot_general(a, b, (((1,), (1,)), ((), ())), preferred_element_type=F32)


def tn(a, b):
    return lax.dot_general(a, b, (((0,), (0,)), ((), ())), preferred_element_type=F32)


def sigmoid(x):
    return 1.0 / (1.0 + jnp.exp(-x))


def layer_norm(rows):
    centre = rows - jnp.mean(rows, axis=-1, keepdims=True)
    inverse = lax.rsqrt(jnp.mean(centre * centre, axis=-1, keepdims=True) + EPSILON)
    return centre * inverse, inverse


def norm_back(grad, normed, inverse):
    return inverse * (
        grad
        - jnp.mean(grad, axis=-1, keepdims=True)
        - normed * jnp.mean(grad * normed, axis=-1, keepdims=True)
    )


class Remote:
    def __init__(self, send_sems, recv_sems):
        self.send_sems, self.recv_sems, self.started = send_sems, recv_sems, []

    def start(self, src, dst, device):
        index = len(self.started)
        copy = pltpu.make_async_remote_copy(
            src_ref=src,
            dst_ref=dst,
            send_sem=self.send_sems.at[index],
            recv_sem=self.recv_sems.at[index],
            device_id=device,
            device_id_type=MESH,
        )
        copy.start()
        self.started.append(copy)
        return copy

    def finish(self):
        for copy in self.started:
            copy.wait_send()


class Gather:
    def __init__(self, remote, slots, here, far, near_device, far_device):
        self.remote, self.slots, self.here, self.far = remote, slots, here, far
        self.near_device, self.far_device = near_device, far_device
        self.rows = slots.shape[1] // GATHER_PARTS
        self.to_far, self.to_near, self.passed = [], [], []

    def view(self, slot, part):
        return self.slots.at[slot, pl.ds(part * self.rows, self.rows)]

    def start(self, *parts):
        for part in parts:
            own = self.view(self.here, part)
            self.to_far.append(self.remote.start(own, own, self.far_device))
        for part in parts:
            own = self.view(self.here, part)
            self.to_near.append(self.remote.start(own, own, self.near_device))

    def forward(self):
        for part, copy in enumerate(self.to_far):
            copy.wait_recv()
            other = self.view(self.far, part)
            self.passed.append(self.remote.start(other, other, self.near_device))

    def wait_near(self):
        for copy in self.to_near:
            copy.wait_recv()

    def wait_rest(self):
        for copy in self.passed:
            copy.wait_recv()


class Scatter:
    def __init__(self, remote, part, out, arrived, ids, near_device, far_device):
        self.remote, self.part, self.out, self.arrived = remote, part, out, arrived
        self.here, self.near, self.far, self.cross = ids
        self.near_device, self.far_device = near_device, far_device

    def pre(self):
        self.out[0] = self.part[self.cross].astype(BF)
        self.first = self.remote.start(self.out.at[0], self.arrived.at[0], self.near_device)

    def across(self):
        self.first.wait_recv()
        self.out[1] = (self.part[self.far] + self.arrived[0].astype(F32)).astype(BF)
        self.second = self.remote.start(self.out.at[1], self.arrived.at[1], self.far_device)

    def local(self):
        self.out[2] = self.part[self.near].astype(BF)
        self.third = self.remote.start(self.out.at[2], self.arrived.at[2], self.near_device)
        self.own = self.part[self.here]

    def total(self):
        self.third.wait_recv()
        self.second.wait_recv()
        return self.own + self.arrived[2].astype(F32) + self.arrived[1].astype(F32)


class Halving:
    def __init__(self, remote, store, arrived, rank, count, device, order):
        self.remote, self.store, self.arrived = remote, store, arrived
        self.rank, self.count, self.device = rank, count, device
        self.order, self.step, self.offset, self.landing = order, 0, 0, 0

    def send(self):
        bit = self.order[self.step]
        self.half = self.count >> (self.step + 1)
        mine = lax.rem(self.rank // (1 << bit), 2)
        partner = self.rank + (1 - 2 * mine) * (1 << bit)
        away = self.offset + (1 - mine) * self.half
        self.offset = self.offset + mine * self.half
        self.copy = self.remote.start(
            self.store.at[pl.ds(away, self.half)],
            self.arrived.at[pl.ds(self.landing, self.half)],
            self.device(partner),
        )

    def sum(self):
        self.copy.wait_recv()
        keep = pl.ds(self.offset, self.half)
        total = self.store[keep].astype(F32) + self.arrived[
            pl.ds(self.landing, self.half)
        ].astype(F32)
        self.landing += self.half
        self.step += 1
        if self.step == len(self.order):
            self.result = total[0]
            return
        self.store[keep] = total.astype(BF)
        self.send()

    def done(self):
        return self.step == len(self.order)


def padded(rows):
    more = jnp.zeros((16 - rows.shape[0], rows.shape[1]), F32)
    return jnp.concatenate([rows.astype(F32), more], axis=0).astype(BF)


def mod_rows(gathered):
    half = gathered.shape[3]
    pieces = [gathered[index].reshape(-1, half) for index in range(4)]
    return jnp.concatenate(
        [jnp.concatenate(pieces[2 * chain : 2 * chain + 2], axis=1) for chain in range(2)], axis=0
    )


def slot_of(chunk, order):
    slot = 0
    for bit in order:
        slot = slot * 2 + (chunk >> bit) % 2
    return slot


def layer_kernel(
    dims,
    orders,
    length_ref,
    time_ref,
    class_ref,
    tokens_hbm,
    cotangent_hbm,
    pair_hbm,
    bias_hbm,
    input_hbm,
    output_hbm,
    hidden_hbm,
    down_hbm,
    modulation_hbm,
    time_hbm,
    class_hbm,
    result_out,
    grad_tokens_out,
    scores_out,
    mods_out,
    expanded_out,
    tables_out,
    bias_grad_out,
    weights_out,
    tokens,
    cotangent,
    pair,
    bias_weight,
    input_weight,
    output_weight,
    hidden_weight,
    down_weight,
    modulation_weight,
    tables,
    mods,
    stage,
    hots,
    mods_all,
    mods_gather,
    mod_halves,
    rows_attend,
    rows_hidden,
    rows_down,
    rows_out,
    bias_send,
    bias_full,
    queries,
    keys,
    values,
    probs,
    attended,
    part,
    part_down,
    grad_active,
    active,
    grad_gate,
    grad_up,
    grad_scores,
    scores_own,
    grad_projected,
    scatter_send,
    scatter_recv,
    turned,
    turned_more,
    final_weights,
    norm_attend,
    norm_hidden,
    middle,
    out_attend,
    grad_middle,
    result,
    grad_tokens,
    mod_part,
    mod_near,
    bias_quarters,
    bias_parts,
    bias_sums,
    bias_grad,
    expanded,
    tables_grad,
    load_sems,
    pair_sems,
    store_sems,
    send_sems,
    recv_sems,
    *piece_refs,
):
    piece_store, piece_recv = piece_refs[: len(PIECES)], piece_refs[len(PIECES) :]
    (groups, chains, span, local, width, local_width, queries_local, hidden) = dims
    heads = local_width // HD
    dp = lax.axis_index("dp")
    me = lax.axis_index("tensor")
    core = lax.rem(me, 2)
    chip = me // 2
    near = me + 1 - 2 * core
    far = lax.rem(me + 2, 4)
    cross = 3 - me
    away = 1 - chip
    near_device, far_device, cross_device = (dp, near), (dp, far), (dp, cross)

    def dp_device(index):
        return (index, me)

    def gather(slots):
        return Gather(remote, slots, me, far, near_device, far_device)

    barrier = pltpu.get_barrier_semaphore()
    for device in (near_device, far_device, cross_device):
        pl.semaphore_signal(barrier, inc=1, device_id=device, device_id_type=MESH)
    for step in range(1, groups):
        pl.semaphore_signal(
            barrier, inc=1, device_id=dp_device(lax.rem(dp + step, groups)), device_id_type=MESH
        )

    loads = []

    def load(src, dst):
        copy = pltpu.make_async_copy(src, dst, load_sems.at[len(loads)])
        copy.start()
        loads.append(copy)
        return copy

    blocks = queries_local // PAIR_ROWS
    n_blocks = chains * blocks

    def pair_copy(index):
        chain = lax.rem(chip + index // blocks, chains)
        slot = lax.rem(index, PAIR_SLOTS)
        return pltpu.make_async_copy(
            pair_hbm.at[chain, pl.ds(lax.rem(index, blocks) * PAIR_ROWS, PAIR_ROWS)],
            pair.at[slot],
            pair_sems.at[slot],
        )

    times = time_hbm.shape[0]
    load_time = load(time_hbm, tables.at[pl.ds(0, times)])
    load_class = load(class_hbm, tables.at[pl.ds(times, class_hbm.shape[0])])
    load_tokens = load(tokens_hbm, tokens)
    load_modulation = load(modulation_hbm, modulation_weight)
    load_cotangent = load(cotangent_hbm, cotangent)
    load_bias = load(bias_hbm, bias_weight)
    pair_copy(0).start()

    remote = Remote(send_sems, recv_sems)
    stores = []

    def store(src, dst):
        copy = pltpu.make_async_copy(src, dst, store_sems.at[len(stores)])
        copy.start()
        stores.append(copy)

    n_table = tables.shape[0]
    lane = lax.broadcasted_iota(jnp.int32, (16, n_table), 1)
    row = lax.broadcasted_iota(jnp.int32, (16, n_table), 0)
    hot_lane = lax.broadcasted_iota(jnp.int32, (8, n_table), 1)
    picked = ((row == 0) & (lane == time_ref[chip])) | (
        (row == 1) & (lane == times + class_ref[chip])
    )
    for chain in range(chains):
        hots[dp, chain] = jnp.where(
            (hot_lane == time_ref[chain]) | (hot_lane == times + class_ref[chain]), 1.0, 0.0
        )
    load_time.wait()
    load_class.wait()
    condition = nn(jnp.where(picked, 1.0, 0.0).astype(BF), tables[...]).astype(BF)
    load_modulation.wait()
    for index in range(1, PAIR_SLOTS):
        pair_copy(index).start()
    load_input = load(input_hbm, input_weight)
    both = nn(condition, modulation_weight[...])
    mods[...] = jnp.broadcast_to(both[0:1] + both[1:2], mods.shape)

    def mod(index):
        return mods[0:1, index * width : (index + 1) * width]

    place = lax.rem(me * local, span) + lax.broadcasted_iota(jnp.int32, (local, 1), 0)
    valid = jnp.where(place < length_ref[chip], 1.0, 0.0)

    load_tokens.wait()
    normed, inverse_attend = layer_norm(tokens[...].astype(F32))
    norm_attend[...] = normed
    rows_attend[me] = (normed * (1.0 + mod(0)) + mod(1)).astype(BF)
    load_cotangent.wait()
    gate_hidden = sigmoid(mod(5))
    rows_down[me] = (cotangent[...].astype(F32) * valid * gate_hidden).astype(BF)
    load_bias.wait()
    bias_rows = padded(bias_weight[...])

    pl.semaphore_wait(barrier, 3 + groups - 1)
    gather_attend = gather(rows_attend)
    gather_attend.start(*range(GATHER_PARTS))
    hot_copies = []
    for step in range(1, groups):
        device = dp_device(lax.rem(dp + step, groups))
        hot_copies.append(remote.start(hots.at[dp], hots.at[dp], device))

    def bias_block(index, carry):
        slot = lax.rem(index, PAIR_SLOTS)
        pair_copy(index).wait()
        for row_index in range(PAIR_ROWS):
            product = nt(bias_rows, pair[slot, row_index])
            place_row = lax.rem(index, blocks) * PAIR_ROWS + row_index
            for half in range(2):
                stage[half, pl.ds(place_row, 16, stride=queries_local), :] = product[
                    :, half * 128 : (half + 1) * 128
                ]

        @pl.when(index + PAIR_SLOTS < n_blocks)
        def _():
            pair_copy(index + PAIR_SLOTS).start()

        return carry

    all_rows = 4 * heads * queries_local
    bias_copies = []
    for turn in range(2):
        chain = lax.rem(chip + turn, 2)
        lax.fori_loop(turn * blocks, (turn + 1) * blocks, bias_block, 0)
        for half in range(2):
            bias_send[chain, :, :, half * 128 : (half + 1) * 128] = (
                stage[half, 0:all_rows, :].astype(BF).reshape(4 * heads, queries_local, 128)
            )
        mine = pl.ds(me * queries_local, queries_local)
        sent = []
        for owner, device in ((far, far_device), (cross, cross_device), (near, near_device)):
            sent.append(
                remote.start(
                    bias_send.at[chain, pl.ds(owner * heads, heads)],
                    bias_full.at[chain, :, mine],
                    device,
                )
            )
        bias_copies.append(sent)
        bias_full[chain, :, mine, :] = bias_send[chain, pl.ds(me * heads, heads)]
        if turn == 0:
            gather_attend.forward()
            load_output = load(output_hbm, output_weight)
            load_down = load(down_hbm, down_weight)
            load_hidden = load(hidden_hbm, hidden_weight)

    gather_down = gather(rows_down)
    gather_down.start(*range(GATHER_PARTS // 2))

    for index in range(PAIR_SLOTS):
        pair_copy(index).start()

    load_input.wait()

    def project(half):
        rows = rows_attend[pl.ds(2 * half, 2)].reshape(span, width)
        queries[half] = nt(rows, input_weight[0]).astype(BF)
        keys[half] = nt(rows, input_weight[1]).astype(BF)
        values[half] = nt(rows, input_weight[2]).astype(BF)

    gather_attend.wait_near()
    project(chip)
    gather_attend.wait_rest()
    project(away)

    head_lane = lax.broadcasted_iota(jnp.int32, (span, local_width), 1)

    def stacked(rows):
        zero = jnp.zeros_like(rows)
        return jnp.concatenate(
            [
                jnp.where((head_lane >= head * HD) & (head_lane < (head + 1) * HD), rows, zero)
                for head in range(heads)
            ],
            axis=0,
        )

    def choose(pieces):
        out = pieces[-1]
        for head in range(heads - 2, -1, -1):
            out = jnp.where(head_lane < (head + 1) * HD, pieces[head], out)
        return out

    def attend(chain):
        scores = nt(stacked(queries[chain]), keys[chain]) * HD ** (-0.5) + bias_full[
            chain
        ].reshape(heads * span, span).astype(F32)
        key_place = lax.broadcasted_iota(jnp.int32, (heads * span, span), 1)
        scores = jnp.where(key_place < length_ref[chain], scores, -1000000000.0)
        top = jnp.max(scores, axis=-1, keepdims=True)
        weights = jnp.exp(scores - top)
        weights = weights * (1.0 / jnp.sum(weights, axis=-1, keepdims=True))
        probs[chain] = weights
        soft = weights.astype(BF)
        attended[chain] = choose(
            [nn(soft[head * span : (head + 1) * span], values[chain]) for head in range(heads)]
        ).astype(BF)

    def put(target, half, rows):
        target[pl.ds(2 * half, 2)] = rows.reshape(2, local, width)

    ids = (me, near, far, cross)

    def scatter(index, source):
        return Scatter(
            remote,
            source,
            scatter_send.at[index],
            scatter_recv.at[index],
            ids,
            near_device,
            far_device,
        )

    bias_copies[0][0].wait_recv()
    bias_copies[0][1].wait_recv()
    bias_copies[1][2].wait_recv()
    attend(away)
    load_output.wait()
    put(part, away, nn(attended[away], output_weight[...]))
    scatter_attend = scatter(0, part)
    scatter_attend.pre()
    bias_copies[1][0].wait_recv()
    bias_copies[1][1].wait_recv()
    bias_copies[0][2].wait_recv()
    scatter_attend.across()
    gather_down.start(*range(GATHER_PARTS // 2, GATHER_PARTS))
    attend(chip)
    put(part, chip, nn(attended[chip], output_weight[...]))
    scatter_attend.local()

    load_down.wait()

    def back_down(half):
        rows = rows_down[pl.ds(2 * half, 2)].reshape(span, width)
        grad_active[half] = nt(rows, down_weight[...])
        for slot in range(2):
            place_slot = 2 * half + slot
            turned[:, pl.ds(pl.multiple_of(place_slot * local, local), local)] = jnp.transpose(
                rows[slot * local : (slot + 1) * local]
            )


    gate_attend = sigmoid(mod(2))
    out_total = scatter_attend.total()
    out_attend[...] = out_total
    total = tokens[...].astype(F32) + valid * gate_attend * out_total
    middle[...] = total
    normed, inverse_hidden = layer_norm(total)
    norm_hidden[...] = normed
    rows_hidden[me] = (normed * (1.0 + mod(3)) + mod(4)).astype(BF)
    gather_hidden = gather(rows_hidden)
    gather_hidden.start(*range(GATHER_PARTS))
    gather_down.forward()
    gather_down.wait_near()
    back_down(chip)
    gather_down.wait_rest()
    back_down(away)

    load_hidden.wait()

    def transition(half):
        rows = rows_hidden[pl.ds(2 * half, 2)].reshape(span, width)
        gate = nn(rows, hidden_weight[0])
        up = nn(rows, hidden_weight[1])
        squashed = sigmoid(gate)
        silu = gate * squashed
        active[half] = (silu * up).astype(BF)
        back = grad_active[half]
        grad_gate[half] = (back * up * squashed * (1.0 + gate * (1.0 - squashed))).astype(BF)
        grad_up[half] = (back * silu).astype(BF)

    def back_hidden(half):
        put(
            part,
            half,
            nt(grad_gate[half], hidden_weight[0]) + nt(grad_up[half], hidden_weight[1]),
        )

    chunk = width // groups
    per_block = max(1, 192 // chunk)

    def weight_grad(pieces, *pairs):
        for block in range(groups // per_block):
            rows = slice(block * per_block * chunk, (block + 1) * per_block * chunk)
            product = jnp.concatenate([nn(left[rows, :], right) for left, right in pairs], axis=1)
            for index in pieces:
                first, size = PIECES[index][1:3]
                for inner in range(per_block):
                    slot = slot_of(block * per_block + inner, orders[index])
                    piece_store[index][slot] = product[
                        inner * chunk : (inner + 1) * chunk, first : first + size
                    ].astype(BF)
        for index in pieces:
            sums[index] = Halving(
                remote,
                piece_store[index],
                piece_recv[index],
                dp,
                groups,
                dp_device,
                orders[index],
            )
            sums[index].send()

    sums = {}

    missing = {matrix: sum(piece[0] == matrix for piece in PIECES) for matrix in range(4)}

    def take_sum(index):
        matrix, first, size = PIECES[index][:3]
        sums[index].sum()
        if sums[index].done():
            final_weights[matrix, :, first : first + size] = sums[index].result
            missing[matrix] -= 1
            if missing[matrix] == 0:
                store(final_weights.at[matrix], weights_out.at[matrix])

    def advance(place):
        for index in SUMS[place]:
            take_sum(index)

    def take_rest():
        while any(missing.values()):
            for index in range(len(PIECES)):
                if not sums[index].done():
                    take_sum(index)

    def flat(ref):
        return ref[...].reshape(chains * span, ref.shape[-1])

    def turn_rows(source, target):
        for slot in range(4):
            target[:, slot * local : (slot + 1) * local] = jnp.transpose(source[slot])

    gather_hidden.wait_near()
    transition(chip)
    gather_hidden.forward()
    back_hidden(chip)
    put(part_down, chip, nn(active[chip], down_weight[...]))
    gather_hidden.wait_rest()
    transition(away)
    weight_grad((0, 1), (turned, flat(active)))
    back_hidden(away)
    scatter_hidden = scatter(1, part)
    scatter_hidden.pre()
    put(part_down, away, nn(active[away], down_weight[...]))
    scatter_hidden.across()
    scatter_hidden.local()
    scatter_down = scatter(2, part_down)
    scatter_down.pre()

    turn_rows(rows_hidden, turned_more)
    weight_grad((2, 3), (turned_more, flat(grad_gate)))

    grad_h = scatter_hidden.total()
    normed = norm_hidden[...]
    back = cotangent[...].astype(F32) + norm_back(grad_h * (1.0 + mod(3)), normed, inverse_hidden)
    grad_middle[...] = back
    rows_out[me] = (back * valid * gate_attend).astype(BF)
    gather_out = gather(rows_out)
    gather_out.start(*range(GATHER_PARTS))

    weight_grad((4, 5), (turned_more, flat(grad_up)))

    def keep_mod(index, rows):
        mod_part[index : index + 1, :] = jnp.sum(rows, axis=0, keepdims=True)

    mod_part[...] = jnp.zeros_like(mod_part)
    keep_mod(3, grad_h * normed)
    keep_mod(4, grad_h)
    keep_mod(2, back * valid * out_attend[...] * gate_attend * (1.0 - gate_attend))
    turn_rows(rows_attend, turned)

    score_copies = []

    def back_attend(chain):
        rows = rows_out[pl.ds(2 * chain, 2)].reshape(span, width)
        grad_heads = stacked(nt(rows, output_weight[...]).astype(BF))
        weights = probs[chain]
        grad_probs = nt(grad_heads, values[chain])
        grad_logits = (
            weights * (grad_probs - jnp.sum(grad_probs * weights, axis=-1, keepdims=True))
        ).astype(BF)
        grad_scores[chain] = grad_logits.reshape(heads, span, span)
        sent = []
        for owner, device in ((far, far_device), (cross, cross_device), (near, near_device)):
            sent.append(
                remote.start(
                    grad_scores.at[chain, :, pl.ds(owner * queries_local, queries_local)],
                    scores_own.at[chain, pl.ds(me * heads, heads)],
                    device,
                )
            )
        score_copies.append(sent)
        scores_own[chain, pl.ds(me * heads, heads)] = grad_scores[
            chain, :, pl.ds(me * queries_local, queries_local), :
        ]
        query_stack = stacked(queries[chain])
        grad_query = (
            choose(
                [
                    nn(grad_logits[head * span : (head + 1) * span], keys[chain])
                    for head in range(heads)
                ]
            )
            * HD ** (-0.5)
        ).astype(BF)
        grad_key = (tn(grad_logits, query_stack) * HD ** (-0.5)).astype(BF)
        grad_value = tn(weights.astype(BF), grad_heads).astype(BF)
        grad_projected[chain] = jnp.concatenate([grad_query, grad_key, grad_value], axis=1)
        put(
            part,
            chain,
            nn(grad_query, input_weight[0])
            + nn(grad_key, input_weight[1])
            + nn(grad_value, input_weight[2]),
        )

    gather_out.wait_near()
    gather_out.forward()
    back_attend(chip)
    advance(0)
    gather_out.wait_rest()
    back_attend(away)
    scatter_input = scatter(3, part)
    scatter_input.pre()
    turn_rows(rows_out, turned_more)
    scatter_input.across()
    scatter_input.local()
    scatter_down.across()
    scatter_down.local()
    weight_grad((6, 7, 8), (turned, flat(grad_projected)), (turned_more, flat(attended)))
    advance(1)
    for sent in score_copies:
        for copy in sent:
            copy.wait_recv()
    store(scores_own, scores_out)
    def bias_grad_block(index, total):
        slot = lax.rem(index, PAIR_SLOTS)
        pair_copy(index).wait()
        for row_index in range(PAIR_ROWS):
            place_row = lax.rem(index, blocks) * PAIR_ROWS + row_index
            rows = jnp.concatenate(
                [
                    stage[half, pl.ds(place_row, 16, stride=queries_local), :].astype(BF)
                    for half in range(2)
                ],
                axis=1,
            )
            total = total + nn(rows, pair[slot, row_index])

        @pl.when(index + PAIR_SLOTS < n_blocks)
        def _():
            pair_copy(index + PAIR_SLOTS).start()

        return total

    def bias_grad_chain(turn, total):
        chain = lax.rem(chip + turn, 2)
        for half in range(2):
            stage[half, 0:all_rows, :] = (
                scores_own[chain, :, :, half * 128 : (half + 1) * 128]
                .reshape(all_rows, 128)
                .astype(F32)
            )
            stage[half, all_rows:, :] = jnp.zeros((16 * queries_local - all_rows, 128), F32)
        return lax.fori_loop(turn * blocks, (turn + 1) * blocks, bias_grad_block, total)

    total = bias_grad_chain(0, jnp.zeros((16, pair_hbm.shape[3]), F32))
    advance(2)
    total = bias_grad_chain(1, total)
    half = total.shape[1] // 2
    for quarter in range(4):
        rows, lanes = quarter // 2 * 8, quarter % 2 * half
        bias_quarters[quarter] = total[rows : rows + 8, lanes : lanes + half]
    tensor_devices = ((near, near_device), (far, far_device), (cross, cross_device))
    tensor_copies = [
        remote.start(bias_quarters.at[owner], bias_parts.at[me], device)
        for owner, device in tensor_devices
    ]
    bias_parts[me] = bias_quarters[me]

    grad_h = scatter_input.total()
    normed = norm_attend[...]
    grad_tokens[...] = (
        grad_middle[...] + norm_back(grad_h * (1.0 + mod(0)), normed, inverse_attend)
    ).astype(BF)
    keep_mod(0, grad_h * normed)
    keep_mod(1, grad_h)
    out_total = scatter_down.total()
    result[...] = (middle[...] + valid * gate_hidden * out_total).astype(BF)
    keep_mod(
        5, cotangent[...].astype(F32) * valid * out_total * gate_hidden * (1.0 - gate_hidden)
    )
    to_near = remote.start(mod_part, mod_near, near_device)

    store(result, result_out)
    store(grad_tokens, grad_tokens_out)

    advance(3)

    to_near.wait_recv()
    chain_mods = mod_part[...] + mod_near[...]
    mod_halves[0] = chain_mods[:, : width // 2].astype(BF)
    mod_halves[1] = chain_mods[:, width // 2 :].astype(BF)
    mods_gather[dp] = mod_halves[core]
    mod_copies = [
        remote.start(mods_gather.at[dp], mods_gather.at[dp], dp_device(lax.rem(dp + step, groups)))
        for step in range(1, groups)
    ]
    for copy in tensor_copies:
        copy.wait_recv()
    bias_sums[0] = bias_parts[0] + bias_parts[1] + bias_parts[2] + bias_parts[3]
    bias_copies = [
        remote.start(bias_sums.at[0], bias_sums.at[step], dp_device(lax.rem(dp + step, groups)))
        for step in range(1, groups)
    ]
    advance(4)
    advance(5)
    for copy in mod_copies:
        copy.wait_recv()
    mods_all[me] = mods_gather[...]
    mod_copies = [
        remote.start(mods_gather, mods_all.at[me], device) for _, device in tensor_devices
    ]
    for copy in bias_copies:
        copy.wait_recv()
    bias_grad[me] = jnp.sum(bias_sums[...], axis=0)
    bias_copies = [
        remote.start(bias_grad.at[me], bias_grad.at[me], device) for _, device in tensor_devices
    ]
    for copy in hot_copies:
        copy.wait_recv()
    rows_all = chains * groups * 8
    hot = jnp.concatenate(
        [hots[:, chain].reshape(groups * 8, n_table) for chain in range(chains)], axis=0
    ).astype(BF)
    hot_lane = lax.broadcasted_iota(jnp.int32, hot.shape, 1)
    zero = jnp.zeros_like(hot)
    time_rows = nn(jnp.where(hot_lane < times, hot, zero), tables[...])
    class_rows = nn(jnp.where(hot_lane < times, zero, hot), tables[...])
    expanded[:, :rows_all] = jnp.transpose(time_rows)
    expanded[:, rows_all:] = jnp.transpose(class_rows)
    store(expanded, expanded_out)
    advance(6)
    for copy in mod_copies:
        copy.wait_recv()
    store(mods_all, mods_out)
    rows = mod_rows(mods_all)
    member = lax.rem(lax.broadcasted_iota(jnp.int32, (rows_all, 1), 0), 8)
    rest = jnp.zeros((rows_all, tables.shape[1]), F32)
    for vector in range(6):
        product = nt(rows, modulation_weight[:, vector * width : (vector + 1) * width])
        rest = rest + jnp.where(member == vector, product, 0.0)
    table = jnp.zeros((n_table, tables.shape[1]), F32)
    for _ in range(3):
        piece = rest.astype(BF)
        table = table + tn(hot, piece)
        rest = rest - piece.astype(F32)
    tables_grad[...] = table
    store(tables_grad, tables_out)
    for copy in bias_copies:
        copy.wait_recv()
    store(bias_grad, bias_grad_out)
    advance(7)
    take_rest()
    for copy in stores:
        copy.wait()
    remote.finish()


def finish_kernel(
    dims,
    result_hbm,
    grad_tokens_hbm,
    weights_hbm,
    scores_hbm,
    mods_hbm,
    expanded_hbm,
    tables_hbm,
    bias_grad_hbm,
    bias_hbm,
    result_out,
    grad_tokens_out,
    pair_out,
    bias_grad_out,
    input_out,
    output_out,
    hidden_out,
    down_out,
    modulation_out,
    time_out,
    class_out,
    rows_pass,
    weights,
    scores,
    mods,
    expanded,
    tables,
    bias_grad,
    bias,
    places,
    pair,
    modulation,
    input_grad,
    output_grad,
    bias_rows,
    load_sems,
    pair_sems,
    store_sems,
):
    (groups, chains, span, local, width, local_width, queries_local, hidden) = dims
    heads = local_width // HD
    blocks = queries_local // PAIR_ROWS
    times = time_out.shape[0]

    def start(src, dst, semaphore):
        copy = pltpu.make_async_copy(src, dst, semaphore)
        copy.start()
        return copy

    moves = (
        (bias_hbm, bias),
        (expanded_hbm, expanded),
        (mods_hbm, mods),
        (scores_hbm.at[0], scores.at[0]),
        (scores_hbm.at[1], scores.at[1]),
        (weights_hbm, weights),
        (result_hbm, rows_pass.at[0]),
        (grad_tokens_hbm, rows_pass.at[1]),
        (tables_hbm, tables),
        (bias_grad_hbm, bias_grad),
    )
    loads = [start(src, dst, load_sems.at[index]) for index, (src, dst) in enumerate(moves)]

    loads[0].wait()
    weight_rows = bias[...].astype(F32)
    spread = jnp.concatenate(
        [
            jnp.broadcast_to(weight_rows[head : head + 1], (PAIR_ROWS, weight_rows.shape[1]))
            for head in range(4 * heads)
        ],
        axis=0,
    )
    member = lax.rem(lax.broadcasted_iota(jnp.int32, spread.shape, 0), PAIR_ROWS)
    for row_index in range(PAIR_ROWS):
        places[row_index] = jnp.where(member == row_index, spread, 0.0).astype(BF)

    def pair_copy(index):
        slot = lax.rem(index, PAIR_SLOTS)
        return pltpu.make_async_copy(
            pair.at[slot],
            pair_out.at[
                index // blocks, pl.ds(lax.rem(index, blocks) * PAIR_ROWS, PAIR_ROWS)
            ],
            pair_sems.at[slot],
        )

    def pair_block(index, carry):
        @pl.when(index >= PAIR_SLOTS)
        def _():
            pair_copy(index - PAIR_SLOTS).wait()

        rows = scores[index // blocks, :, pl.ds(lax.rem(index, blocks) * PAIR_ROWS, PAIR_ROWS)]
        across = jnp.transpose(rows.reshape(4 * heads * PAIR_ROWS, rows.shape[2]))
        slot = lax.rem(index, PAIR_SLOTS)
        for row_index in range(PAIR_ROWS):
            pair[slot, row_index] = nn(across, places[row_index]).astype(BF)
        pair_copy(index).start()
        return carry

    stores = []

    def store(src, dst):
        stores.append(start(src, dst, store_sems.at[len(stores)]))

    loads[1].wait()
    loads[2].wait()
    rows = mod_rows(mods)
    both = jnp.concatenate([rows, rows], axis=0)
    lane = lax.rem(lax.broadcasted_iota(jnp.int32, expanded.shape, 1), 8)
    for vector in range(6):
        left = jnp.where(lane == vector, expanded[...], 0.0).astype(BF)
        modulation[vector] = nn(left, both)
        store(modulation.at[vector], modulation_out.at[:, pl.ds(vector * width, width)])
    n_blocks = chains * blocks
    loads[3].wait()
    loads[4].wait()
    lax.fori_loop(0, n_blocks, pair_block, 0)

    for copy in loads[5:]:
        copy.wait()
    store(weights.at[0], down_out)
    store(weights.at[2], hidden_out.at[0])
    store(weights.at[3], hidden_out.at[1])
    store(rows_pass.at[0], result_out)
    store(rows_pass.at[1], grad_tokens_out)
    store(tables.at[pl.ds(0, times)], time_out)
    store(tables.at[pl.ds(times, class_out.shape[0])], class_out)
    bias_rows[...] = jnp.concatenate(
        [
            jnp.concatenate([bias_grad[0], bias_grad[1]], axis=1),
            jnp.concatenate([bias_grad[2], bias_grad[3]], axis=1),
        ],
        axis=0,
    )[: 4 * heads]
    store(bias_rows, bias_grad_out)
    for index in range(3):
        input_grad[index] = weights[1, :, index * local_width : (index + 1) * local_width]
    store(input_grad, input_out)
    output_grad[...] = jnp.transpose(weights[1, :, 3 * local_width :])
    store(output_grad, output_out)
    for index in range(n_blocks - PAIR_SLOTS, n_blocks):
        pair_copy(index).wait()
    for copy in stores:
        copy.wait()


def body(
    groups,
    tokens,
    pair_features,
    cotangent,
    chain_length,
    time_bin,
    cath_class,
    bias_weight,
    input_weight,
    output_weight,
    hidden_weight,
    down_weight,
    modulation_weight,
    time_table,
    class_table,
):
    chains, queries_local, span, channels = pair_features.shape
    local, width = tokens.shape
    local_width = input_weight.shape[2]
    hidden = down_weight.shape[0]
    heads = local_width // HD
    rows = chains * span
    chunk = width // groups
    assert chains == 2 and rows == 4 * local and span == 2 * local
    assert span == 256 and channels == 256 and 4 * local_width == width == hidden
    assert queries_local % PAIR_ROWS == 0
    dims = (groups, chains, span, local, width, local_width, queries_local, hidden)
    bits = groups.bit_length() - 1
    assert groups == 1 << bits
    straight = tuple(range(bits))
    turns = (straight, straight[1:2] + straight[:1] + straight[2:], straight[1:] + straight[:1])
    orders = tuple(turns[piece[3]] for piece in PIECES)
    n_table = time_table.shape[0] + class_table.shape[0]
    input_turned = jnp.swapaxes(input_weight, 1, 2)
    bias_turned = bias_weight.T

    anywhere = pl.BlockSpec(memory_space=pl.ANY)
    scalars = pl.BlockSpec(memory_space=pltpu.SMEM)
    vmem = pltpu.VMEM
    half_rows = (chains, span, width)
    slots = (4, local, width)
    messages = 4 * 3 * (1 + GATHER_PARTS) + 6 * 2 + len(PIECES) * bits + 3 * (groups - 1) + 10
    weights_shape = (4, chunk, width)
    outs = pl.pallas_call(
        functools.partial(layer_kernel, dims, orders),
        out_shape=(
            jax.ShapeDtypeStruct((local, width), BF),
            jax.ShapeDtypeStruct((local, width), BF),
            jax.ShapeDtypeStruct((chains, 4 * heads, queries_local, span), BF),
            jax.ShapeDtypeStruct((4, groups, 8, width // 2), BF),
            jax.ShapeDtypeStruct((time_table.shape[1], 2 * groups * 16), F32),
            jax.ShapeDtypeStruct((n_table, time_table.shape[1]), F32),
            jax.ShapeDtypeStruct((4, 8, channels // 2), F32),
            jax.ShapeDtypeStruct(weights_shape, F32),
        ),
        in_specs=[scalars] * 3 + [anywhere] * 11,
        out_specs=[anywhere] * 8,
        scratch_shapes=[
            vmem((local, width), BF),
            vmem((local, width), BF),
            vmem((PAIR_SLOTS, PAIR_ROWS, span, channels), BF),
            vmem(bias_turned.shape, BF),
            vmem(input_turned.shape, BF),
            vmem(output_weight.shape, BF),
            vmem(hidden_weight.shape, BF),
            vmem(down_weight.shape, BF),
            vmem(modulation_weight.shape, BF),
            vmem((n_table, time_table.shape[1]), BF),
            vmem((8, modulation_weight.shape[1]), F32),
            vmem((2, 16 * queries_local, 128), F32),
            vmem((groups, chains, 8, n_table), F32),
            vmem((4, groups, 8, width // 2), BF),
            vmem((groups, 8, width // 2), BF),
            vmem((2, 8, width // 2), BF),
            vmem(slots, BF),
            vmem(slots, BF),
            vmem(slots, BF),
            vmem(slots, BF),
            vmem((chains, 4 * heads, queries_local, span), BF),
            vmem((chains, heads, span, span), BF),
            vmem((chains, span, local_width), BF),
            vmem((chains, span, local_width), BF),
            vmem((chains, span, local_width), BF),
            vmem((chains, heads * span, span), F32),
            vmem((chains, span, local_width), BF),
            vmem(slots, F32),
            vmem(slots, F32),
            vmem(half_rows, F32),
            vmem(half_rows, BF),
            vmem(half_rows, BF),
            vmem(half_rows, BF),
            vmem((chains, heads, span, span), BF),
            vmem((chains, 4 * heads, queries_local, span), BF),
            vmem((chains, span, 3 * local_width), BF),
            vmem((4, 3, local, width), BF),
            vmem((4, 3, local, width), BF),
            vmem((width, rows), BF),
            vmem((width, rows), BF),
            vmem(weights_shape, F32),
            vmem((local, width), F32),
            vmem((local, width), F32),
            vmem((local, width), F32),
            vmem((local, width), F32),
            vmem((local, width), F32),
            vmem((local, width), BF),
            vmem((local, width), BF),
            vmem((8, width), F32),
            vmem((8, width), F32),
            vmem((4, 8, channels // 2), F32),
            vmem((4, 8, channels // 2), F32),
            vmem((groups, 8, channels // 2), F32),
            vmem((4, 8, channels // 2), F32),
            vmem((time_table.shape[1], 2 * groups * 16), F32),
            vmem((n_table, time_table.shape[1]), F32),
            pltpu.SemaphoreType.DMA((11,)),
            pltpu.SemaphoreType.DMA((PAIR_SLOTS,)),
            pltpu.SemaphoreType.DMA((14,)),
            pltpu.SemaphoreType.DMA((messages,)),
            pltpu.SemaphoreType.DMA((messages,)),
        ]
        + [vmem((groups, chunk, piece[2]), BF) for piece in PIECES] * 2,
        compiler_params=pltpu.CompilerParams(
            collective_id=0, has_side_effects=True, vmem_limit_bytes=VMEM_BYTES
        ),
        name="layer",
    )(
        chain_length,
        time_bin,
        cath_class,
        tokens,
        cotangent,
        pair_features,
        bias_turned,
        input_turned,
        output_weight,
        hidden_weight,
        down_weight,
        modulation_weight,
        time_table,
        class_table,
    )
    result, grad_tokens, scores, mods_all, expanded, tables, bias_grad, weights = outs

    outs = pl.pallas_call(
        functools.partial(finish_kernel, dims),
        out_shape=(
            jax.ShapeDtypeStruct((local, width), BF),
            jax.ShapeDtypeStruct((local, width), BF),
            jax.ShapeDtypeStruct(pair_features.shape, BF),
            jax.ShapeDtypeStruct(bias_turned.shape, F32),
            jax.ShapeDtypeStruct((3, chunk, local_width), F32),
            jax.ShapeDtypeStruct((local_width, chunk), F32),
            jax.ShapeDtypeStruct((2, chunk, hidden), F32),
            jax.ShapeDtypeStruct((chunk, hidden), F32),
            jax.ShapeDtypeStruct(modulation_weight.shape, F32),
            jax.ShapeDtypeStruct(time_table.shape, F32),
            jax.ShapeDtypeStruct(class_table.shape, F32),
        ),
        in_specs=[anywhere] * 9,
        out_specs=[anywhere] * 11,
        scratch_shapes=[
            vmem((2, local, width), BF),
            vmem(weights.shape, F32),
            vmem(scores.shape, BF),
            vmem(mods_all.shape, BF),
            vmem(expanded.shape, F32),
            vmem(tables.shape, F32),
            vmem(bias_grad.shape, F32),
            vmem(bias_turned.shape, BF),
            vmem((PAIR_ROWS, 4 * heads * PAIR_ROWS, channels), BF),
            vmem((PAIR_SLOTS, PAIR_ROWS, span, channels), BF),
            vmem((6, modulation_weight.shape[0], width), F32),
            vmem((3, chunk, local_width), F32),
            vmem((local_width, chunk), F32),
            vmem(bias_turned.shape, F32),
            pltpu.SemaphoreType.DMA((10,)),
            pltpu.SemaphoreType.DMA((PAIR_SLOTS,)),
            pltpu.SemaphoreType.DMA((16,)),
        ],
        compiler_params=pltpu.CompilerParams(vmem_limit_bytes=VMEM_BYTES),
        name="finish",
    )(
        result,
        grad_tokens,
        weights,
        scores,
        mods_all,
        expanded,
        tables,
        bias_grad,
        bias_turned,
    )
    outs = list(outs)
    outs[3], outs[7] = outs[3].T, outs[7].T
    return tuple(outs)


def solution(mesh):
    placed = (
        P(("dp", "tensor"), None),
        P("dp", "tensor", None, None),
        P(("dp", "tensor"), None),
        P("dp"),
        P("dp"),
        P("dp"),
        P(),
        P(None, None, "tensor"),
        P("tensor", None),
        P(None, None, "tensor"),
        P("tensor", None),
        P(),
        P(),
        P(),
    )
    assert mesh.shape["tensor"] == 4
    return jax.shard_map(
        functools.partial(body, mesh.shape["dp"]),
        mesh=mesh,
        in_specs=placed,
        out_specs=(
            P(("dp", "tensor"), None),
            P(("dp", "tensor"), None),
            P("dp", "tensor", None, None),
            P(),
            P(None, "dp", "tensor"),
            P("tensor", "dp"),
            P(None, "dp", "tensor"),
            P("tensor", "dp"),
            P(),
            P(),
            P(),
        ),
        check_vma=False,
    )
```

```python
import functools

import jax
import jax.numpy as jnp
from jax import lax
from jax.experimental import pallas as pl
from jax.experimental.pallas import tpu as pltpu
from jax.sharding import PartitionSpec as P

HD = 64
EPSILON = 1e-05
BF = jnp.bfloat16
F32 = jnp.float32
MESH = pl.DeviceIdType.MESH
PAIR_SLOTS = 4
PAIR_ROWS = 16
GATHER_PARTS = 2
VMEM_BYTES = 60 << 20
PIECES = (
    (0, 0, 384, 0),
    (0, 384, 384, 2),
    (2, 0, 384, 1),
    (2, 384, 384, 0),
    (3, 0, 384, 0),
    (3, 384, 384, 1),
    (1, 0, 256, 0),
    (1, 256, 256, 0),
    (1, 512, 256, 0),
)
SUMS = (
    (0, 2,),
    (1, 3, 2,),
    (0, 4,),
    (1, 3,),
    (5,),
    (2, 4, 6, 3,),
    (5, 7, 4, 6, 8,),
    (0, 5, 7, 1, 6, 8, 7, 8,),
)


def nn(a, b):
    return lax.dot_general(a, b, (((1,), (0,)), ((), ())), preferred_element_type=F32)


def nt(a, b):
    return lax.dot_general(a, b, (((1,), (1,)), ((), ())), preferred_element_type=F32)


def tn(a, b):
    return lax.dot_general(a, b, (((0,), (0,)), ((), ())), preferred_element_type=F32)


def sigmoid(x):
    return 1.0 / (1.0 + jnp.exp(-x))


def layer_norm(rows):
    centre = rows - jnp.mean(rows, axis=-1, keepdims=True)
    inverse = lax.rsqrt(jnp.mean(centre * centre, axis=-1, keepdims=True) + EPSILON)
    return centre * inverse, inverse


def norm_back(grad, normed, inverse):
    return inverse * (
        grad
        - jnp.mean(grad, axis=-1, keepdims=True)
        - normed * jnp.mean(grad * normed, axis=-1, keepdims=True)
    )


class Remote:
    def __init__(self, send_sems, recv_sems):
        self.send_sems, self.recv_sems, self.started = send_sems, recv_sems, []

    def start(self, src, dst, device):
        index = len(self.started)
        copy = pltpu.make_async_remote_copy(
            src_ref=src,
            dst_ref=dst,
            send_sem=self.send_sems.at[index],
            recv_sem=self.recv_sems.at[index],
            device_id=device,
            device_id_type=MESH,
        )
        copy.start()
        self.started.append(copy)
        return copy

    def finish(self):
        for copy in self.started:
            copy.wait_send()


class Gather:
    def __init__(self, remote, slots, here, far, near_device, far_device):
        self.remote, self.slots, self.here, self.far = remote, slots, here, far
        self.near_device, self.far_device = near_device, far_device
        self.rows = slots.shape[1] // GATHER_PARTS
        self.to_far, self.to_near, self.passed = [], [], []

    def view(self, slot, part):
        return self.slots.at[slot, pl.ds(part * self.rows, self.rows)]

    def start(self, *parts):
        for part in parts:
            own = self.view(self.here, part)
            self.to_far.append(self.remote.start(own, own, self.far_device))
        for part in parts:
            own = self.view(self.here, part)
            self.to_near.append(self.remote.start(own, own, self.near_device))

    def forward(self):
        for part, copy in enumerate(self.to_far):
            copy.wait_recv()
            other = self.view(self.far, part)
            self.passed.append(self.remote.start(other, other, self.near_device))

    def wait_near(self):
        for copy in self.to_near:
            copy.wait_recv()

    def wait_rest(self):
        for copy in self.passed:
            copy.wait_recv()


class Scatter:
    def __init__(self, remote, part, out, arrived, ids, near_device, far_device):
        self.remote, self.part, self.out, self.arrived = remote, part, out, arrived
        self.here, self.near, self.far, self.cross = ids
        self.near_device, self.far_device = near_device, far_device

    def pre(self):
        self.out[0] = self.part[self.cross].astype(BF)
        self.first = self.remote.start(self.out.at[0], self.arrived.at[0], self.near_device)

    def across(self):
        self.first.wait_recv()
        self.out[1] = (self.part[self.far] + self.arrived[0].astype(F32)).astype(BF)
        self.second = self.remote.start(self.out.at[1], self.arrived.at[1], self.far_device)

    def local(self):
        self.out[2] = self.part[self.near].astype(BF)
        self.third = self.remote.start(self.out.at[2], self.arrived.at[2], self.near_device)
        self.own = self.part[self.here]

    def total(self):
        self.third.wait_recv()
        self.second.wait_recv()
        return self.own + self.arrived[2].astype(F32) + self.arrived[1].astype(F32)


class Halving:
    def __init__(self, remote, store, arrived, rank, count, device, order):
        self.remote, self.store, self.arrived = remote, store, arrived
        self.rank, self.count, self.device = rank, count, device
        self.order, self.step, self.offset, self.landing = order, 0, 0, 0

    def send(self):
        bit = self.order[self.step]
        self.half = self.count >> (self.step + 1)
        mine = lax.rem(self.rank // (1 << bit), 2)
        partner = self.rank + (1 - 2 * mine) * (1 << bit)
        away = self.offset + (1 - mine) * self.half
        self.offset = self.offset + mine * self.half
        self.copy = self.remote.start(
            self.store.at[pl.ds(away, self.half)],
            self.arrived.at[pl.ds(self.landing, self.half)],
            self.device(partner),
        )

    def sum(self):
        self.copy.wait_recv()
        keep = pl.ds(self.offset, self.half)
        total = self.store[keep].astype(F32) + self.arrived[
            pl.ds(self.landing, self.half)
        ].astype(F32)
        self.landing += self.half
        self.step += 1
        if self.step == len(self.order):
            self.result = total[0]
            return
        self.store[keep] = total.astype(BF)
        self.send()

    def done(self):
        return self.step == len(self.order)


def padded(rows):
    more = jnp.zeros((16 - rows.shape[0], rows.shape[1]), F32)
    return jnp.concatenate([rows.astype(F32), more], axis=0).astype(BF)


def mod_rows(gathered):
    half = gathered.shape[3]
    pieces = [gathered[index].reshape(-1, half) for index in range(4)]
    return jnp.concatenate(
        [jnp.concatenate(pieces[2 * chain : 2 * chain + 2], axis=1) for chain in range(2)], axis=0
    )


def slot_of(chunk, order):
    slot = 0
    for bit in order:
        slot = slot * 2 + (chunk >> bit) % 2
    return slot


def layer_kernel(
    dims,
    orders,
    length_ref,
    time_ref,
    class_ref,
    tokens_hbm,
    cotangent_hbm,
    pair_hbm,
    bias_hbm,
    input_hbm,
    output_hbm,
    hidden_hbm,
    down_hbm,
    modulation_hbm,
    time_hbm,
    class_hbm,
    result_out,
    grad_tokens_out,
    scores_out,
    mods_out,
    expanded_out,
    tables_out,
    bias_grad_out,
    weights_out,
    tokens,
    cotangent,
    pair,
    bias_weight,
    input_weight,
    output_weight,
    hidden_weight,
    down_weight,
    modulation_weight,
    tables,
    mods,
    stage,
    hots,
    mods_all,
    mods_gather,
    mod_halves,
    rows_attend,
    rows_hidden,
    rows_down,
    rows_out,
    bias_send,
    bias_full,
    queries,
    keys,
    values,
    probs,
    attended,
    part,
    part_down,
    grad_active,
    active,
    grad_gate,
    grad_up,
    grad_scores,
    scores_own,
    grad_projected,
    scatter_send,
    scatter_recv,
    turned,
    turned_more,
    final_weights,
    norm_attend,
    norm_hidden,
    middle,
    out_attend,
    grad_middle,
    result,
    grad_tokens,
    mod_part,
    mod_near,
    bias_quarters,
    bias_parts,
    bias_sums,
    bias_grad,
    expanded,
    tables_grad,
    load_sems,
    pair_sems,
    store_sems,
    send_sems,
    recv_sems,
    *piece_refs,
):
    piece_store, piece_recv = piece_refs[: len(PIECES)], piece_refs[len(PIECES) :]
    (groups, chains, span, local, width, local_width, queries_local, hidden) = dims
    heads = local_width // HD
    dp = lax.axis_index("dp")
    me = lax.axis_index("tensor")
    core = lax.rem(me, 2)
    chip = me // 2
    near = me + 1 - 2 * core
    far = lax.rem(me + 2, 4)
    cross = 3 - me
    away = 1 - chip
    near_device, far_device, cross_device = (dp, near), (dp, far), (dp, cross)

    def dp_device(index):
        return (index, me)

    def gather(slots):
        return Gather(remote, slots, me, far, near_device, far_device)

    barrier = pltpu.get_barrier_semaphore()
    for device in (near_device, far_device, cross_device):
        pl.semaphore_signal(barrier, inc=1, device_id=device, device_id_type=MESH)
    for step in range(1, groups):
        pl.semaphore_signal(
            barrier, inc=1, device_id=dp_device(lax.rem(dp + step, groups)), device_id_type=MESH
        )

    loads = []

    def load(src, dst):
        copy = pltpu.make_async_copy(src, dst, load_sems.at[len(loads)])
        copy.start()
        loads.append(copy)
        return copy

    blocks = queries_local // PAIR_ROWS
    n_blocks = chains * blocks

    def pair_copy(index):
        chain = lax.rem(chip + index // blocks, chains)
        slot = lax.rem(index, PAIR_SLOTS)
        return pltpu.make_async_copy(
            pair_hbm.at[chain, pl.ds(lax.rem(index, blocks) * PAIR_ROWS, PAIR_ROWS)],
            pair.at[slot],
            pair_sems.at[slot],
        )

    times = time_hbm.shape[0]
    load_time = load(time_hbm, tables.at[pl.ds(0, times)])
    load_class = load(class_hbm, tables.at[pl.ds(times, class_hbm.shape[0])])
    load_tokens = load(tokens_hbm, tokens)
    first = pl.ds(0, 2 * width)
    other = pl.ds(2 * width, 4 * width)
    load_modulation = load(modulation_hbm.at[:, first], modulation_weight.at[:, first])
    load_more = load(modulation_hbm.at[:, other], modulation_weight.at[:, other])
    load_cotangent = load(cotangent_hbm, cotangent)
    load_bias = load(bias_hbm, bias_weight)
    pair_copy(0).start()

    remote = Remote(send_sems, recv_sems)
    stores = []

    def store(src, dst):
        copy = pltpu.make_async_copy(src, dst, store_sems.at[len(stores)])
        copy.start()
        stores.append(copy)

    n_table = tables.shape[0]
    lane = lax.broadcasted_iota(jnp.int32, (16, n_table), 1)
    row = lax.broadcasted_iota(jnp.int32, (16, n_table), 0)
    hot_lane = lax.broadcasted_iota(jnp.int32, (8, n_table), 1)
    picked = ((row == 0) & (lane == time_ref[chip])) | (
        (row == 1) & (lane == times + class_ref[chip])
    )
    for chain in range(chains):
        hots[dp, chain] = jnp.where(
            (hot_lane == time_ref[chain]) | (hot_lane == times + class_ref[chain]), 1.0, 0.0
        )
    load_time.wait()
    load_class.wait()
    condition = nn(jnp.where(picked, 1.0, 0.0).astype(BF), tables[...]).astype(BF)
    load_modulation.wait()
    for index in range(1, PAIR_SLOTS):
        pair_copy(index).start()
    load_input = load(input_hbm, input_weight)

    def modulate(columns):
        both = nn(condition, modulation_weight[:, columns])
        mods[:, columns] = jnp.broadcast_to(both[0:1] + both[1:2], (8, both.shape[1]))

    modulate(slice(0, 2 * width))

    def mod(index):
        return mods[0:1, index * width : (index + 1) * width]

    place = lax.rem(me * local, span) + lax.broadcasted_iota(jnp.int32, (local, 1), 0)
    valid = jnp.where(place < length_ref[chip], 1.0, 0.0)

    load_tokens.wait()
    normed, inverse_attend = layer_norm(tokens[...].astype(F32))
    norm_attend[...] = normed
    rows_attend[me] = (normed * (1.0 + mod(0)) + mod(1)).astype(BF)
    pl.semaphore_wait(barrier, 3 + groups - 1)
    gather_attend = gather(rows_attend)
    gather_attend.start(*range(GATHER_PARTS))
    load_more.wait()
    modulate(slice(2 * width, 6 * width))
    load_cotangent.wait()
    gate_hidden = sigmoid(mod(5))
    rows_down[me] = (cotangent[...].astype(F32) * valid * gate_hidden).astype(BF)
    load_bias.wait()
    bias_rows = padded(bias_weight[...])

    hot_copies = []
    for step in range(1, groups):
        device = dp_device(lax.rem(dp + step, groups))
        hot_copies.append(remote.start(hots.at[dp], hots.at[dp], device))

    def bias_block(index, carry):
        slot = lax.rem(index, PAIR_SLOTS)
        pair_copy(index).wait()
        for row_index in range(PAIR_ROWS):
            product = nt(bias_rows, pair[slot, row_index])
            place_row = lax.rem(index, blocks) * PAIR_ROWS + row_index
            for half in range(2):
                stage[half, pl.ds(place_row, 16, stride=queries_local), :] = product[
                    :, half * 128 : (half + 1) * 128
                ]

        @pl.when(index + PAIR_SLOTS < n_blocks)
        def _():
            pair_copy(index + PAIR_SLOTS).start()

        return carry

    all_rows = 4 * heads * queries_local
    bias_copies = []
    for turn in range(2):
        chain = lax.rem(chip + turn, 2)
        lax.fori_loop(turn * blocks, (turn + 1) * blocks, bias_block, 0)
        for half in range(2):
            bias_send[chain, :, :, half * 128 : (half + 1) * 128] = (
                stage[half, 0:all_rows, :].astype(BF).reshape(4 * heads, queries_local, 128)
            )
        mine = pl.ds(me * queries_local, queries_local)
        sent = []
        for owner, device in ((far, far_device), (cross, cross_device), (near, near_device)):
            sent.append(
                remote.start(
                    bias_send.at[chain, pl.ds(owner * heads, heads)],
                    bias_full.at[chain, :, mine],
                    device,
                )
            )
        bias_copies.append(sent)
        bias_full[chain, :, mine, :] = bias_send[chain, pl.ds(me * heads, heads)]
        if turn == 0:
            gather_attend.forward()
            load_output = load(output_hbm, output_weight)
            load_down = load(down_hbm, down_weight)
            load_hidden = load(hidden_hbm, hidden_weight)

    gather_down = gather(rows_down)
    gather_down.start(*range(GATHER_PARTS // 2))

    for index in range(PAIR_SLOTS):
        pair_copy(index).start()

    load_input.wait()

    def project(half):
        rows = rows_attend[pl.ds(2 * half, 2)].reshape(span, width)
        queries[half] = nt(rows, input_weight[0]).astype(BF)
        keys[half] = nt(rows, input_weight[1]).astype(BF)
        values[half] = nt(rows, input_weight[2]).astype(BF)

    gather_attend.wait_near()
    project(chip)
    gather_attend.wait_rest()
    project(away)

    head_lane = lax.broadcasted_iota(jnp.int32, (span, local_width), 1)

    def stacked(rows):
        zero = jnp.zeros_like(rows)
        return jnp.concatenate(
            [
                jnp.where((head_lane >= head * HD) & (head_lane < (head + 1) * HD), rows, zero)
                for head in range(heads)
            ],
            axis=0,
        )

    def choose(pieces):
        out = pieces[-1]
        for head in range(heads - 2, -1, -1):
            out = jnp.where(head_lane < (head + 1) * HD, pieces[head], out)
        return out

    def attend(chain):
        scores = nt(stacked(queries[chain]), keys[chain]) * HD ** (-0.5) + bias_full[
            chain
        ].reshape(heads * span, span).astype(F32)
        key_place = lax.broadcasted_iota(jnp.int32, (heads * span, span), 1)
        scores = jnp.where(key_place < length_ref[chain], scores, -1000000000.0)
        top = jnp.max(scores, axis=-1, keepdims=True)
        weights = jnp.exp(scores - top)
        weights = weights * (1.0 / jnp.sum(weights, axis=-1, keepdims=True))
        probs[chain] = weights
        soft = weights.astype(BF)
        attended[chain] = choose(
            [nn(soft[head * span : (head + 1) * span], values[chain]) for head in range(heads)]
        ).astype(BF)

    def put(target, half, rows):
        target[pl.ds(2 * half, 2)] = rows.reshape(2, local, width)

    ids = (me, near, far, cross)

    def scatter(index, source):
        return Scatter(
            remote,
            source,
            scatter_send.at[index],
            scatter_recv.at[index],
            ids,
            near_device,
            far_device,
        )

    bias_copies[0][0].wait_recv()
    bias_copies[0][1].wait_recv()
    bias_copies[1][2].wait_recv()
    attend(away)
    load_output.wait()
    put(part, away, nn(attended[away], output_weight[...]))
    scatter_attend = scatter(0, part)
    scatter_attend.pre()
    bias_copies[1][0].wait_recv()
    bias_copies[1][1].wait_recv()
    bias_copies[0][2].wait_recv()
    scatter_attend.across()
    gather_down.start(*range(GATHER_PARTS // 2, GATHER_PARTS))
    attend(chip)
    put(part, chip, nn(attended[chip], output_weight[...]))
    scatter_attend.local()

    load_down.wait()

    def back_down(half):
        rows = rows_down[pl.ds(2 * half, 2)].reshape(span, width)
        grad_active[half] = nt(rows, down_weight[...])
        for slot in range(2):
            place_slot = 2 * half + slot
            turned[:, pl.ds(pl.multiple_of(place_slot * local, local), local)] = jnp.transpose(
                rows[slot * local : (slot + 1) * local]
            )


    gate_attend = sigmoid(mod(2))
    out_total = scatter_attend.total()
    out_attend[...] = out_total
    total = tokens[...].astype(F32) + valid * gate_attend * out_total
    middle[...] = total
    normed, inverse_hidden = layer_norm(total)
    norm_hidden[...] = normed
    rows_hidden[me] = (normed * (1.0 + mod(3)) + mod(4)).astype(BF)
    gather_hidden = gather(rows_hidden)
    gather_hidden.start(*range(GATHER_PARTS))
    gather_down.forward()
    gather_down.wait_near()
    back_down(chip)
    gather_down.wait_rest()
    back_down(away)

    load_hidden.wait()

    def transition(half):
        rows = rows_hidden[pl.ds(2 * half, 2)].reshape(span, width)
        gate = nn(rows, hidden_weight[0])
        up = nn(rows, hidden_weight[1])
        squashed = sigmoid(gate)
        silu = gate * squashed
        active[half] = (silu * up).astype(BF)
        back = grad_active[half]
        grad_gate[half] = (back * up * squashed * (1.0 + gate * (1.0 - squashed))).astype(BF)
        grad_up[half] = (back * silu).astype(BF)

    def back_hidden(half):
        put(
            part,
            half,
            nt(grad_gate[half], hidden_weight[0]) + nt(grad_up[half], hidden_weight[1]),
        )

    chunk = width // groups
    per_block = max(1, 192 // chunk)

    def weight_grad(pieces, *pairs):
        for block in range(groups // per_block):
            rows = slice(block * per_block * chunk, (block + 1) * per_block * chunk)
            product = jnp.concatenate([nn(left[rows, :], right) for left, right in pairs], axis=1)
            for index in pieces:
                first, size = PIECES[index][1:3]
                for inner in range(per_block):
                    slot = slot_of(block * per_block + inner, orders[index])
                    piece_store[index][slot] = product[
                        inner * chunk : (inner + 1) * chunk, first : first + size
                    ].astype(BF)
        for index in pieces:
            sums[index] = Halving(
                remote,
                piece_store[index],
                piece_recv[index],
                dp,
                groups,
                dp_device,
                orders[index],
            )
            sums[index].send()

    sums = {}

    missing = {matrix: sum(piece[0] == matrix for piece in PIECES) for matrix in range(4)}

    def take_sum(index):
        matrix, first, size = PIECES[index][:3]
        sums[index].sum()
        if sums[index].done():
            final_weights[matrix, :, first : first + size] = sums[index].result
            missing[matrix] -= 1
            if missing[matrix] == 0:
                store(final_weights.at[matrix], weights_out.at[matrix])

    def advance(place):
        for index in SUMS[place]:
            take_sum(index)

    def take_rest():
        while any(missing.values()):
            for index in range(len(PIECES)):
                if not sums[index].done():
                    take_sum(index)

    def flat(ref):
        return ref[...].reshape(chains * span, ref.shape[-1])

    def turn_rows(source, target):
        for slot in range(4):
            target[:, slot * local : (slot + 1) * local] = jnp.transpose(source[slot])

    gather_hidden.wait_near()
    transition(chip)
    back_hidden(chip)
    put(part_down, chip, nn(active[chip], down_weight[...]))
    gather_hidden.forward()
    gather_hidden.wait_rest()
    transition(away)
    weight_grad((0, 1), (turned, flat(active)))
    back_hidden(away)
    scatter_hidden = scatter(1, part)
    scatter_hidden.pre()
    put(part_down, away, nn(active[away], down_weight[...]))
    scatter_hidden.across()
    scatter_hidden.local()
    scatter_down = scatter(2, part_down)
    scatter_down.pre()

    turn_rows(rows_hidden, turned_more)
    weight_grad((2, 3), (turned_more, flat(grad_gate)))

    grad_h = scatter_hidden.total()
    normed = norm_hidden[...]
    back = cotangent[...].astype(F32) + norm_back(grad_h * (1.0 + mod(3)), normed, inverse_hidden)
    grad_middle[...] = back
    rows_out[me] = (back * valid * gate_attend).astype(BF)
    gather_out = gather(rows_out)
    gather_out.start(*range(GATHER_PARTS))

    weight_grad((4, 5), (turned_more, flat(grad_up)))

    def keep_mod(index, rows):
        mod_part[index : index + 1, :] = jnp.sum(rows, axis=0, keepdims=True)

    mod_part[...] = jnp.zeros_like(mod_part)
    keep_mod(3, grad_h * normed)
    keep_mod(4, grad_h)
    keep_mod(2, back * valid * out_attend[...] * gate_attend * (1.0 - gate_attend))
    turn_rows(rows_attend, turned)

    score_copies = []

    def back_attend(chain):
        rows = rows_out[pl.ds(2 * chain, 2)].reshape(span, width)
        grad_heads = stacked(nt(rows, output_weight[...]).astype(BF))
        weights = probs[chain]
        grad_probs = nt(grad_heads, values[chain])
        grad_logits = (
            weights * (grad_probs - jnp.sum(grad_probs * weights, axis=-1, keepdims=True))
        ).astype(BF)
        grad_scores[chain] = grad_logits.reshape(heads, span, span)
        sent = []
        for owner, device in ((far, far_device), (cross, cross_device), (near, near_device)):
            sent.append(
                remote.start(
                    grad_scores.at[chain, :, pl.ds(owner * queries_local, queries_local)],
                    scores_own.at[chain, pl.ds(me * heads, heads)],
                    device,
                )
            )
        score_copies.append(sent)
        scores_own[chain, pl.ds(me * heads, heads)] = grad_scores[
            chain, :, pl.ds(me * queries_local, queries_local), :
        ]
        query_stack = stacked(queries[chain])
        grad_query = (
            choose(
                [
                    nn(grad_logits[head * span : (head + 1) * span], keys[chain])
                    for head in range(heads)
                ]
            )
            * HD ** (-0.5)
        ).astype(BF)
        grad_key = (tn(grad_logits, query_stack) * HD ** (-0.5)).astype(BF)
        grad_value = tn(weights.astype(BF), grad_heads).astype(BF)
        grad_projected[chain] = jnp.concatenate([grad_query, grad_key, grad_value], axis=1)
        put(
            part,
            chain,
            nn(grad_query, input_weight[0])
            + nn(grad_key, input_weight[1])
            + nn(grad_value, input_weight[2]),
        )

    gather_out.wait_near()
    back_attend(chip)
    gather_out.forward()
    advance(0)
    gather_out.wait_rest()
    back_attend(away)
    scatter_input = scatter(3, part)
    scatter_input.pre()
    turn_rows(rows_out, turned_more)
    scatter_input.across()
    scatter_input.local()
    scatter_down.across()
    scatter_down.local()
    weight_grad((6, 7, 8), (turned, flat(grad_projected)), (turned_more, flat(attended)))
    advance(1)
    for sent in score_copies:
        for copy in sent:
            copy.wait_recv()
    store(scores_own, scores_out)
    def bias_grad_block(index, total):
        slot = lax.rem(index, PAIR_SLOTS)
        pair_copy(index).wait()
        for row_index in range(PAIR_ROWS):
            place_row = lax.rem(index, blocks) * PAIR_ROWS + row_index
            rows = jnp.concatenate(
                [
                    stage[half, pl.ds(place_row, 16, stride=queries_local), :].astype(BF)
                    for half in range(2)
                ],
                axis=1,
            )
            total = total + nn(rows, pair[slot, row_index])

        @pl.when(index + PAIR_SLOTS < n_blocks)
        def _():
            pair_copy(index + PAIR_SLOTS).start()

        return total

    def bias_grad_chain(turn, total):
        chain = lax.rem(chip + turn, 2)
        for half in range(2):
            stage[half, 0:all_rows, :] = (
                scores_own[chain, :, :, half * 128 : (half + 1) * 128]
                .reshape(all_rows, 128)
                .astype(F32)
            )
            stage[half, all_rows:, :] = jnp.zeros((16 * queries_local - all_rows, 128), F32)
        return lax.fori_loop(turn * blocks, (turn + 1) * blocks, bias_grad_block, total)

    total = bias_grad_chain(0, jnp.zeros((16, pair_hbm.shape[3]), F32))
    advance(2)
    total = bias_grad_chain(1, total)
    half = total.shape[1] // 2
    for quarter in range(4):
        rows, lanes = quarter // 2 * 8, quarter % 2 * half
        bias_quarters[quarter] = total[rows : rows + 8, lanes : lanes + half]
    tensor_devices = ((near, near_device), (far, far_device), (cross, cross_device))
    tensor_copies = [
        remote.start(bias_quarters.at[owner], bias_parts.at[me], device)
        for owner, device in tensor_devices
    ]
    bias_parts[me] = bias_quarters[me]

    grad_h = scatter_input.total()
    normed = norm_attend[...]
    grad_tokens[...] = (
        grad_middle[...] + norm_back(grad_h * (1.0 + mod(0)), normed, inverse_attend)
    ).astype(BF)
    keep_mod(0, grad_h * normed)
    keep_mod(1, grad_h)
    out_total = scatter_down.total()
    result[...] = (middle[...] + valid * gate_hidden * out_total).astype(BF)
    keep_mod(
        5, cotangent[...].astype(F32) * valid * out_total * gate_hidden * (1.0 - gate_hidden)
    )
    to_near = remote.start(mod_part, mod_near, near_device)

    store(result, result_out)
    store(grad_tokens, grad_tokens_out)

    advance(3)

    to_near.wait_recv()
    chain_mods = mod_part[...] + mod_near[...]
    mod_halves[0] = chain_mods[:, : width // 2].astype(BF)
    mod_halves[1] = chain_mods[:, width // 2 :].astype(BF)
    mods_gather[dp] = mod_halves[core]
    mod_copies = [
        remote.start(mods_gather.at[dp], mods_gather.at[dp], dp_device(lax.rem(dp + step, groups)))
        for step in range(1, groups)
    ]
    for copy in tensor_copies:
        copy.wait_recv()
    bias_sums[0] = bias_parts[0] + bias_parts[1] + bias_parts[2] + bias_parts[3]
    bias_copies = [
        remote.start(bias_sums.at[0], bias_sums.at[step], dp_device(lax.rem(dp + step, groups)))
        for step in range(1, groups)
    ]
    advance(4)
    advance(5)
    for copy in mod_copies:
        copy.wait_recv()
    mods_all[me] = mods_gather[...]
    mod_copies = [
        remote.start(mods_gather, mods_all.at[me], device) for _, device in tensor_devices
    ]
    for copy in bias_copies:
        copy.wait_recv()
    bias_grad[me] = jnp.sum(bias_sums[...], axis=0)
    bias_copies = [
        remote.start(bias_grad.at[me], bias_grad.at[me], device) for _, device in tensor_devices
    ]
    for copy in hot_copies:
        copy.wait_recv()
    rows_all = chains * groups * 8
    hot = jnp.concatenate(
        [hots[:, chain].reshape(groups * 8, n_table) for chain in range(chains)], axis=0
    ).astype(BF)
    hot_lane = lax.broadcasted_iota(jnp.int32, hot.shape, 1)
    zero = jnp.zeros_like(hot)
    time_rows = nn(jnp.where(hot_lane < times, hot, zero), tables[...])
    class_rows = nn(jnp.where(hot_lane < times, zero, hot), tables[...])
    expanded[:, :rows_all] = jnp.transpose(time_rows)
    expanded[:, rows_all:] = jnp.transpose(class_rows)
    store(expanded, expanded_out)
    advance(6)
    for copy in mod_copies:
        copy.wait_recv()
    store(mods_all, mods_out)
    rows = mod_rows(mods_all)
    member = lax.rem(lax.broadcasted_iota(jnp.int32, (rows_all, 1), 0), 8)
    rest = jnp.zeros((rows_all, tables.shape[1]), F32)
    for vector in range(6):
        product = nt(rows, modulation_weight[:, vector * width : (vector + 1) * width])
        rest = rest + jnp.where(member == vector, product, 0.0)
    table = jnp.zeros((n_table, tables.shape[1]), F32)
    for _ in range(3):
        piece = rest.astype(BF)
        table = table + tn(hot, piece)
        rest = rest - piece.astype(F32)
    tables_grad[...] = table
    store(tables_grad, tables_out)
    for copy in bias_copies:
        copy.wait_recv()
    store(bias_grad, bias_grad_out)
    advance(7)
    take_rest()
    for copy in stores:
        copy.wait()
    remote.finish()


def finish_kernel(
    dims,
    result_hbm,
    grad_tokens_hbm,
    weights_hbm,
    scores_hbm,
    mods_hbm,
    expanded_hbm,
    tables_hbm,
    bias_grad_hbm,
    bias_hbm,
    result_out,
    grad_tokens_out,
    pair_out,
    bias_grad_out,
    input_out,
    output_out,
    hidden_out,
    down_out,
    modulation_out,
    time_out,
    class_out,
    rows_pass,
    weights,
    scores,
    mods,
    expanded,
    tables,
    bias_grad,
    bias,
    places,
    pair,
    modulation,
    input_grad,
    output_grad,
    bias_rows,
    load_sems,
    pair_sems,
    store_sems,
):
    (groups, chains, span, local, width, local_width, queries_local, hidden) = dims
    heads = local_width // HD
    blocks = queries_local // PAIR_ROWS
    times = time_out.shape[0]

    def start(src, dst, semaphore):
        copy = pltpu.make_async_copy(src, dst, semaphore)
        copy.start()
        return copy

    moves = (
        (bias_hbm, bias),
        (expanded_hbm, expanded),
        (mods_hbm, mods),
        (scores_hbm.at[0], scores.at[0]),
        (scores_hbm.at[1], scores.at[1]),
        (weights_hbm, weights),
        (result_hbm, rows_pass.at[0]),
        (grad_tokens_hbm, rows_pass.at[1]),
        (tables_hbm, tables),
        (bias_grad_hbm, bias_grad),
    )
    loads = [start(src, dst, load_sems.at[index]) for index, (src, dst) in enumerate(moves)]

    loads[0].wait()
    weight_rows = bias[...].astype(F32)
    spread = jnp.concatenate(
        [
            jnp.broadcast_to(weight_rows[head : head + 1], (PAIR_ROWS, weight_rows.shape[1]))
            for head in range(4 * heads)
        ],
        axis=0,
    )
    member = lax.rem(lax.broadcasted_iota(jnp.int32, spread.shape, 0), PAIR_ROWS)
    for row_index in range(PAIR_ROWS):
        places[row_index] = jnp.where(member == row_index, spread, 0.0).astype(BF)

    def pair_copy(index):
        slot = lax.rem(index, PAIR_SLOTS)
        return pltpu.make_async_copy(
            pair.at[slot],
            pair_out.at[
                index // blocks, pl.ds(lax.rem(index, blocks) * PAIR_ROWS, PAIR_ROWS)
            ],
            pair_sems.at[slot],
        )

    def pair_block(index, carry):
        @pl.when(index >= PAIR_SLOTS)
        def _():
            pair_copy(index - PAIR_SLOTS).wait()

        rows = scores[index // blocks, :, pl.ds(lax.rem(index, blocks) * PAIR_ROWS, PAIR_ROWS)]
        across = jnp.transpose(rows.reshape(4 * heads * PAIR_ROWS, rows.shape[2]))
        slot = lax.rem(index, PAIR_SLOTS)
        for row_index in range(PAIR_ROWS):
            pair[slot, row_index] = nn(across, places[row_index]).astype(BF)
        pair_copy(index).start()
        return carry

    stores = []

    def store(src, dst):
        stores.append(start(src, dst, store_sems.at[len(stores)]))

    loads[1].wait()
    loads[2].wait()
    rows = mod_rows(mods)
    both = jnp.concatenate([rows, rows], axis=0)
    lane = lax.rem(lax.broadcasted_iota(jnp.int32, expanded.shape, 1), 8)
    for vector in range(6):
        left = jnp.where(lane == vector, expanded[...], 0.0).astype(BF)
        modulation[vector] = nn(left, both)
        store(modulation.at[vector], modulation_out.at[:, pl.ds(vector * width, width)])
    n_blocks = chains * blocks
    loads[3].wait()
    loads[4].wait()
    lax.fori_loop(0, n_blocks, pair_block, 0)

    for copy in loads[5:]:
        copy.wait()
    store(weights.at[0], down_out)
    store(weights.at[2], hidden_out.at[0])
    store(weights.at[3], hidden_out.at[1])
    store(rows_pass.at[0], result_out)
    store(rows_pass.at[1], grad_tokens_out)
    store(tables.at[pl.ds(0, times)], time_out)
    store(tables.at[pl.ds(times, class_out.shape[0])], class_out)
    bias_rows[...] = jnp.concatenate(
        [
            jnp.concatenate([bias_grad[0], bias_grad[1]], axis=1),
            jnp.concatenate([bias_grad[2], bias_grad[3]], axis=1),
        ],
        axis=0,
    )[: 4 * heads]
    store(bias_rows, bias_grad_out)
    for index in range(3):
        input_grad[index] = weights[1, :, index * local_width : (index + 1) * local_width]
    store(input_grad, input_out)
    output_grad[...] = jnp.transpose(weights[1, :, 3 * local_width :])
    store(output_grad, output_out)
    for index in range(n_blocks - PAIR_SLOTS, n_blocks):
        pair_copy(index).wait()
    for copy in stores:
        copy.wait()


def body(
    groups,
    tokens,
    pair_features,
    cotangent,
    chain_length,
    time_bin,
    cath_class,
    bias_weight,
    input_weight,
    output_weight,
    hidden_weight,
    down_weight,
    modulation_weight,
    time_table,
    class_table,
):
    chains, queries_local, span, channels = pair_features.shape
    local, width = tokens.shape
    local_width = input_weight.shape[2]
    hidden = down_weight.shape[0]
    heads = local_width // HD
    rows = chains * span
    chunk = width // groups
    assert chains == 2 and rows == 4 * local and span == 2 * local
    assert span == 256 and channels == 256 and 4 * local_width == width == hidden
    assert queries_local % PAIR_ROWS == 0
    dims = (groups, chains, span, local, width, local_width, queries_local, hidden)
    bits = groups.bit_length() - 1
    assert groups == 1 << bits
    straight = tuple(range(bits))
    turns = (straight, straight[1:2] + straight[:1] + straight[2:], straight[1:] + straight[:1])
    orders = tuple(turns[piece[3]] for piece in PIECES)
    n_table = time_table.shape[0] + class_table.shape[0]
    input_turned = jnp.swapaxes(input_weight, 1, 2)
    bias_turned = bias_weight.T

    anywhere = pl.BlockSpec(memory_space=pl.ANY)
    scalars = pl.BlockSpec(memory_space=pltpu.SMEM)
    vmem = pltpu.VMEM
    half_rows = (chains, span, width)
    slots = (4, local, width)
    messages = 4 * 3 * (1 + GATHER_PARTS) + 6 * 2 + len(PIECES) * bits + 3 * (groups - 1) + 10
    weights_shape = (4, chunk, width)
    outs = pl.pallas_call(
        functools.partial(layer_kernel, dims, orders),
        out_shape=(
            jax.ShapeDtypeStruct((local, width), BF),
            jax.ShapeDtypeStruct((local, width), BF),
            jax.ShapeDtypeStruct((chains, 4 * heads, queries_local, span), BF),
            jax.ShapeDtypeStruct((4, groups, 8, width // 2), BF),
            jax.ShapeDtypeStruct((time_table.shape[1], 2 * groups * 16), F32),
            jax.ShapeDtypeStruct((n_table, time_table.shape[1]), F32),
            jax.ShapeDtypeStruct((4, 8, channels // 2), F32),
            jax.ShapeDtypeStruct(weights_shape, F32),
        ),
        in_specs=[scalars] * 3 + [anywhere] * 11,
        out_specs=[anywhere] * 8,
        scratch_shapes=[
            vmem((local, width), BF),
            vmem((local, width), BF),
            vmem((PAIR_SLOTS, PAIR_ROWS, span, channels), BF),
            vmem(bias_turned.shape, BF),
            vmem(input_turned.shape, BF),
            vmem(output_weight.shape, BF),
            vmem(hidden_weight.shape, BF),
            vmem(down_weight.shape, BF),
            vmem(modulation_weight.shape, BF),
            vmem((n_table, time_table.shape[1]), BF),
            vmem((8, modulation_weight.shape[1]), F32),
            vmem((2, 16 * queries_local, 128), F32),
            vmem((groups, chains, 8, n_table), F32),
            vmem((4, groups, 8, width // 2), BF),
            vmem((groups, 8, width // 2), BF),
            vmem((2, 8, width // 2), BF),
            vmem(slots, BF),
            vmem(slots, BF),
            vmem(slots, BF),
            vmem(slots, BF),
            vmem((chains, 4 * heads, queries_local, span), BF),
            vmem((chains, heads, span, span), BF),
            vmem((chains, span, local_width), BF),
            vmem((chains, span, local_width), BF),
            vmem((chains, span, local_width), BF),
            vmem((chains, heads * span, span), F32),
            vmem((chains, span, local_width), BF),
            vmem(slots, F32),
            vmem(slots, F32),
            vmem(half_rows, F32),
            vmem(half_rows, BF),
            vmem(half_rows, BF),
            vmem(half_rows, BF),
            vmem((chains, heads, span, span), BF),
            vmem((chains, 4 * heads, queries_local, span), BF),
            vmem((chains, span, 3 * local_width), BF),
            vmem((4, 3, local, width), BF),
            vmem((4, 3, local, width), BF),
            vmem((width, rows), BF),
            vmem((width, rows), BF),
            vmem(weights_shape, F32),
            vmem((local, width), F32),
            vmem((local, width), F32),
            vmem((local, width), F32),
            vmem((local, width), F32),
            vmem((local, width), F32),
            vmem((local, width), BF),
            vmem((local, width), BF),
            vmem((8, width), F32),
            vmem((8, width), F32),
            vmem((4, 8, channels // 2), F32),
            vmem((4, 8, channels // 2), F32),
            vmem((groups, 8, channels // 2), F32),
            vmem((4, 8, channels // 2), F32),
            vmem((time_table.shape[1], 2 * groups * 16), F32),
            vmem((n_table, time_table.shape[1]), F32),
            pltpu.SemaphoreType.DMA((11,)),
            pltpu.SemaphoreType.DMA((PAIR_SLOTS,)),
            pltpu.SemaphoreType.DMA((14,)),
            pltpu.SemaphoreType.DMA((messages,)),
            pltpu.SemaphoreType.DMA((messages,)),
        ]
        + [vmem((groups, chunk, piece[2]), BF) for piece in PIECES] * 2,
        compiler_params=pltpu.CompilerParams(
            collective_id=0, has_side_effects=True, vmem_limit_bytes=VMEM_BYTES
        ),
        name="layer",
    )(
        chain_length,
        time_bin,
        cath_class,
        tokens,
        cotangent,
        pair_features,
        bias_turned,
        input_turned,
        output_weight,
        hidden_weight,
        down_weight,
        modulation_weight,
        time_table,
        class_table,
    )
    result, grad_tokens, scores, mods_all, expanded, tables, bias_grad, weights = outs

    outs = pl.pallas_call(
        functools.partial(finish_kernel, dims),
        out_shape=(
            jax.ShapeDtypeStruct((local, width), BF),
            jax.ShapeDtypeStruct((local, width), BF),
            jax.ShapeDtypeStruct(pair_features.shape, BF),
            jax.ShapeDtypeStruct(bias_turned.shape, F32),
            jax.ShapeDtypeStruct((3, chunk, local_width), F32),
            jax.ShapeDtypeStruct((local_width, chunk), F32),
            jax.ShapeDtypeStruct((2, chunk, hidden), F32),
            jax.ShapeDtypeStruct((chunk, hidden), F32),
            jax.ShapeDtypeStruct(modulation_weight.shape, F32),
            jax.ShapeDtypeStruct(time_table.shape, F32),
            jax.ShapeDtypeStruct(class_table.shape, F32),
        ),
        in_specs=[anywhere] * 9,
        out_specs=[anywhere] * 11,
        scratch_shapes=[
            vmem((2, local, width), BF),
            vmem(weights.shape, F32),
            vmem(scores.shape, BF),
            vmem(mods_all.shape, BF),
            vmem(expanded.shape, F32),
            vmem(tables.shape, F32),
            vmem(bias_grad.shape, F32),
            vmem(bias_turned.shape, BF),
            vmem((PAIR_ROWS, 4 * heads * PAIR_ROWS, channels), BF),
            vmem((PAIR_SLOTS, PAIR_ROWS, span, channels), BF),
            vmem((6, modulation_weight.shape[0], width), F32),
            vmem((3, chunk, local_width), F32),
            vmem((local_width, chunk), F32),
            vmem(bias_turned.shape, F32),
            pltpu.SemaphoreType.DMA((10,)),
            pltpu.SemaphoreType.DMA((PAIR_SLOTS,)),
            pltpu.SemaphoreType.DMA((16,)),
        ],
        compiler_params=pltpu.CompilerParams(vmem_limit_bytes=VMEM_BYTES),
        name="finish",
    )(
        result,
        grad_tokens,
        weights,
        scores,
        mods_all,
        expanded,
        tables,
        bias_grad,
        bias_turned,
    )
    outs = list(outs)
    outs[3], outs[7] = outs[3].T, outs[7].T
    return tuple(outs)


def solution(mesh):
    placed = (
        P(("dp", "tensor"), None),
        P("dp", "tensor", None, None),
        P(("dp", "tensor"), None),
        P("dp"),
        P("dp"),
        P("dp"),
        P(),
        P(None, None, "tensor"),
        P("tensor", None),
        P(None, None, "tensor"),
        P("tensor", None),
        P(),
        P(),
        P(),
    )
    assert mesh.shape["tensor"] == 4
    return jax.shard_map(
        functools.partial(body, mesh.shape["dp"]),
        mesh=mesh,
        in_specs=placed,
        out_specs=(
            P(("dp", "tensor"), None),
            P(("dp", "tensor"), None),
            P("dp", "tensor", None, None),
            P(),
            P(None, "dp", "tensor"),
            P("tensor", "dp"),
            P(None, "dp", "tensor"),
            P("tensor", "dp"),
            P(),
            P(),
            P(),
        ),
        check_vma=False,
    )
```

```python
import functools

import jax
import jax.numpy as jnp
from jax import lax
from jax.experimental import pallas as pl
from jax.experimental.pallas import tpu as pltpu
from jax.sharding import PartitionSpec as P

HD = 64
EPSILON = 1e-05
BF = jnp.bfloat16
F32 = jnp.float32
MESH = pl.DeviceIdType.MESH
PAIR_SLOTS = 4
PAIR_ROWS = 16
GATHER_PARTS = 2
VMEM_BYTES = 60 << 20
PIECES = (
    (0, 0, 384, 0),
    (0, 384, 384, 2),
    (2, 0, 384, 1),
    (2, 384, 384, 0),
    (3, 0, 384, 0),
    (3, 384, 384, 1),
    (1, 0, 256, 0),
    (1, 256, 256, 0),
    (1, 512, 256, 0),
)
SUMS = (
    (0, 2,),
    (1, 3, 2,),
    (0, 4,),
    (1, 3,),
    (5,),
    (2, 4, 6, 3,),
    (5, 7, 4, 6, 8,),
    (0, 5, 7, 1, 6, 8, 7, 8,),
)


def nn(a, b):
    return lax.dot_general(a, b, (((1,), (0,)), ((), ())), preferred_element_type=F32)


def nt(a, b):
    return lax.dot_general(a, b, (((1,), (1,)), ((), ())), preferred_element_type=F32)


def tn(a, b):
    return lax.dot_general(a, b, (((0,), (0,)), ((), ())), preferred_element_type=F32)


def sigmoid(x):
    return 1.0 / (1.0 + jnp.exp(-x))


def layer_norm(rows):
    centre = rows - jnp.mean(rows, axis=-1, keepdims=True)
    inverse = lax.rsqrt(jnp.mean(centre * centre, axis=-1, keepdims=True) + EPSILON)
    return centre * inverse, inverse


def norm_back(grad, normed, inverse):
    return inverse * (
        grad
        - jnp.mean(grad, axis=-1, keepdims=True)
        - normed * jnp.mean(grad * normed, axis=-1, keepdims=True)
    )


class Remote:
    def __init__(self, send_sems, recv_sems):
        self.send_sems, self.recv_sems, self.started = send_sems, recv_sems, []

    def start(self, src, dst, device):
        index = len(self.started)
        copy = pltpu.make_async_remote_copy(
            src_ref=src,
            dst_ref=dst,
            send_sem=self.send_sems.at[index],
            recv_sem=self.recv_sems.at[index],
            device_id=device,
            device_id_type=MESH,
        )
        copy.start()
        self.started.append(copy)
        return copy

    def finish(self):
        for copy in self.started:
            copy.wait_send()


class Gather:
    def __init__(self, remote, slots, here, far, near_device, far_device):
        self.remote, self.slots, self.here, self.far = remote, slots, here, far
        self.near_device, self.far_device = near_device, far_device
        self.rows = slots.shape[1] // GATHER_PARTS
        self.to_far, self.to_near, self.passed = [], [], []

    def view(self, slot, part):
        return self.slots.at[slot, pl.ds(part * self.rows, self.rows)]

    def start(self, *parts):
        for part in parts:
            own = self.view(self.here, part)
            self.to_far.append(self.remote.start(own, own, self.far_device))
        for part in parts:
            own = self.view(self.here, part)
            self.to_near.append(self.remote.start(own, own, self.near_device))

    def forward(self):
        for part, copy in enumerate(self.to_far):
            copy.wait_recv()
            other = self.view(self.far, part)
            self.passed.append(self.remote.start(other, other, self.near_device))

    def wait_near(self):
        for copy in self.to_near:
            copy.wait_recv()

    def wait_rest(self):
        for copy in self.passed:
            copy.wait_recv()


class Scatter:
    def __init__(self, remote, part, out, arrived, ids, near_device, far_device):
        self.remote, self.part, self.out, self.arrived = remote, part, out, arrived
        self.here, self.near, self.far, self.cross = ids
        self.near_device, self.far_device = near_device, far_device

    def pre(self):
        self.out[0] = self.part[self.cross].astype(BF)
        self.first = self.remote.start(self.out.at[0], self.arrived.at[0], self.near_device)

    def across(self):
        self.first.wait_recv()
        self.out[1] = (self.part[self.far] + self.arrived[0].astype(F32)).astype(BF)
        self.second = self.remote.start(self.out.at[1], self.arrived.at[1], self.far_device)

    def local(self):
        self.out[2] = self.part[self.near].astype(BF)
        self.third = self.remote.start(self.out.at[2], self.arrived.at[2], self.near_device)
        self.own = self.part[self.here]

    def total(self):
        self.third.wait_recv()
        self.second.wait_recv()
        return self.own + self.arrived[2].astype(F32) + self.arrived[1].astype(F32)


class Halving:
    def __init__(self, remote, store, arrived, rank, count, device, order):
        self.remote, self.store, self.arrived = remote, store, arrived
        self.rank, self.count, self.device = rank, count, device
        self.order, self.step, self.offset, self.landing = order, 0, 0, 0

    def send(self):
        bit = self.order[self.step]
        self.half = self.count >> (self.step + 1)
        mine = lax.rem(self.rank // (1 << bit), 2)
        partner = self.rank + (1 - 2 * mine) * (1 << bit)
        away = self.offset + (1 - mine) * self.half
        self.offset = self.offset + mine * self.half
        self.copy = self.remote.start(
            self.store.at[pl.ds(away, self.half)],
            self.arrived.at[pl.ds(self.landing, self.half)],
            self.device(partner),
        )

    def sum(self):
        self.copy.wait_recv()
        keep = pl.ds(self.offset, self.half)
        total = self.store[keep].astype(F32) + self.arrived[
            pl.ds(self.landing, self.half)
        ].astype(F32)
        self.landing += self.half
        self.step += 1
        if self.step == len(self.order):
            self.result = total[0]
            return
        self.store[keep] = total.astype(BF)
        self.send()

    def done(self):
        return self.step == len(self.order)


def padded(rows):
    more = jnp.zeros((16 - rows.shape[0], rows.shape[1]), F32)
    return jnp.concatenate([rows.astype(F32), more], axis=0).astype(BF)


def mod_rows(gathered):
    half = gathered.shape[3]
    pieces = [gathered[index].reshape(-1, half) for index in range(4)]
    return jnp.concatenate(
        [jnp.concatenate(pieces[2 * chain : 2 * chain + 2], axis=1) for chain in range(2)], axis=0
    )


def slot_of(chunk, order):
    slot = 0
    for bit in order:
        slot = slot * 2 + (chunk >> bit) % 2
    return slot


def layer_kernel(
    dims,
    orders,
    length_ref,
    time_ref,
    class_ref,
    tokens_hbm,
    cotangent_hbm,
    pair_hbm,
    bias_hbm,
    input_hbm,
    output_hbm,
    hidden_hbm,
    down_hbm,
    modulation_hbm,
    time_hbm,
    class_hbm,
    result_out,
    grad_tokens_out,
    scores_out,
    mods_out,
    expanded_out,
    tables_out,
    bias_grad_out,
    weights_out,
    tokens,
    cotangent,
    pair,
    bias_weight,
    input_weight,
    output_weight,
    hidden_weight,
    down_weight,
    modulation_weight,
    tables,
    mods,
    stage,
    hots,
    mods_all,
    mods_gather,
    mod_halves,
    rows_attend,
    rows_hidden,
    rows_down,
    rows_out,
    bias_send,
    bias_full,
    queries,
    keys,
    values,
    probs,
    attended,
    part,
    part_down,
    grad_active,
    active,
    grad_gate,
    grad_up,
    grad_scores,
    scores_own,
    grad_projected,
    scatter_send,
    scatter_recv,
    turned,
    turned_more,
    final_weights,
    norm_attend,
    norm_hidden,
    middle,
    out_attend,
    grad_middle,
    result,
    grad_tokens,
    mod_part,
    mod_near,
    bias_quarters,
    bias_parts,
    bias_sums,
    bias_grad,
    expanded,
    tables_grad,
    load_sems,
    pair_sems,
    store_sems,
    send_sems,
    recv_sems,
    *piece_refs,
):
    piece_store, piece_recv = piece_refs[: len(PIECES)], piece_refs[len(PIECES) :]
    (groups, chains, span, local, width, local_width, queries_local, hidden) = dims
    heads = local_width // HD
    dp = lax.axis_index("dp")
    me = lax.axis_index("tensor")
    core = lax.rem(me, 2)
    chip = me // 2
    near = me + 1 - 2 * core
    far = lax.rem(me + 2, 4)
    cross = 3 - me
    away = 1 - chip
    near_device, far_device, cross_device = (dp, near), (dp, far), (dp, cross)

    def dp_device(index):
        return (index, me)

    def gather(slots):
        return Gather(remote, slots, me, far, near_device, far_device)

    barrier = pltpu.get_barrier_semaphore()
    for device in (near_device, far_device, cross_device):
        pl.semaphore_signal(barrier, inc=1, device_id=device, device_id_type=MESH)
    for step in range(1, groups):
        pl.semaphore_signal(
            barrier, inc=1, device_id=dp_device(lax.rem(dp + step, groups)), device_id_type=MESH
        )

    loads = []

    def load(src, dst):
        copy = pltpu.make_async_copy(src, dst, load_sems.at[len(loads)])
        copy.start()
        loads.append(copy)
        return copy

    blocks = queries_local // PAIR_ROWS
    n_blocks = chains * blocks

    def pair_copy(index):
        chain = lax.rem(chip + index // blocks, chains)
        slot = lax.rem(index, PAIR_SLOTS)
        return pltpu.make_async_copy(
            pair_hbm.at[chain, pl.ds(lax.rem(index, blocks) * PAIR_ROWS, PAIR_ROWS)],
            pair.at[slot],
            pair_sems.at[slot],
        )

    times = time_hbm.shape[0]
    load_time = load(time_hbm, tables.at[pl.ds(0, times)])
    load_class = load(class_hbm, tables.at[pl.ds(times, class_hbm.shape[0])])
    load_tokens = load(tokens_hbm, tokens)
    first = pl.ds(0, 2 * width)
    other = pl.ds(2 * width, 4 * width)
    load_modulation = load(modulation_hbm.at[:, first], modulation_weight.at[:, first])
    load_more = load(modulation_hbm.at[:, other], modulation_weight.at[:, other])
    load_cotangent = load(cotangent_hbm, cotangent)
    load_bias = load(bias_hbm, bias_weight)
    pair_copy(0).start()

    remote = Remote(send_sems, recv_sems)
    stores = []

    def store(src, dst):
        copy = pltpu.make_async_copy(src, dst, store_sems.at[len(stores)])
        copy.start()
        stores.append(copy)

    n_table = tables.shape[0]
    lane = lax.broadcasted_iota(jnp.int32, (16, n_table), 1)
    row = lax.broadcasted_iota(jnp.int32, (16, n_table), 0)
    hot_lane = lax.broadcasted_iota(jnp.int32, (8, n_table), 1)
    picked = ((row == 0) & (lane == time_ref[chip])) | (
        (row == 1) & (lane == times + class_ref[chip])
    )
    for chain in range(chains):
        hots[dp, chain] = jnp.where(
            (hot_lane == time_ref[chain]) | (hot_lane == times + class_ref[chain]), 1.0, 0.0
        )
    load_time.wait()
    load_class.wait()
    condition = nn(jnp.where(picked, 1.0, 0.0).astype(BF), tables[...]).astype(BF)
    load_modulation.wait()
    for index in range(1, PAIR_SLOTS):
        pair_copy(index).start()
    load_input = load(input_hbm, input_weight)

    def modulate(columns):
        both = nn(condition, modulation_weight[:, columns])
        mods[:, columns] = jnp.broadcast_to(both[0:1] + both[1:2], (8, both.shape[1]))

    modulate(slice(0, 2 * width))

    def mod(index):
        return mods[0:1, index * width : (index + 1) * width]

    place = lax.rem(me * local, span) + lax.broadcasted_iota(jnp.int32, (local, 1), 0)
    valid = jnp.where(place < length_ref[chip], 1.0, 0.0)

    load_tokens.wait()
    normed, inverse_attend = layer_norm(tokens[...].astype(F32))
    norm_attend[...] = normed
    rows_attend[me] = (normed * (1.0 + mod(0)) + mod(1)).astype(BF)
    pl.semaphore_wait(barrier, 3 + groups - 1)
    gather_attend = gather(rows_attend)
    gather_attend.start(*range(GATHER_PARTS))
    load_more.wait()
    modulate(slice(2 * width, 6 * width))
    load_cotangent.wait()
    gate_hidden = sigmoid(mod(5))
    rows_down[me] = (cotangent[...].astype(F32) * valid * gate_hidden).astype(BF)
    load_bias.wait()
    bias_rows = padded(bias_weight[...])

    hot_copies = []
    for step in range(1, groups):
        device = dp_device(lax.rem(dp + step, groups))
        hot_copies.append(remote.start(hots.at[dp], hots.at[dp], device))

    def bias_block(index, carry):
        slot = lax.rem(index, PAIR_SLOTS)
        pair_copy(index).wait()
        for row_index in range(PAIR_ROWS):
            product = nt(bias_rows, pair[slot, row_index])
            place_row = lax.rem(index, blocks) * PAIR_ROWS + row_index
            for half in range(2):
                stage[half, pl.ds(place_row, 16, stride=queries_local), :] = product[
                    :, half * 128 : (half + 1) * 128
                ]

        @pl.when(index + PAIR_SLOTS < n_blocks)
        def _():
            pair_copy(index + PAIR_SLOTS).start()

        return carry

    all_rows = 4 * heads * queries_local
    bias_copies = []
    for turn in range(2):
        chain = lax.rem(chip + turn, 2)
        lax.fori_loop(turn * blocks, (turn + 1) * blocks, bias_block, 0)
        for half in range(2):
            bias_send[chain, :, :, half * 128 : (half + 1) * 128] = (
                stage[half, 0:all_rows, :].astype(BF).reshape(4 * heads, queries_local, 128)
            )
        mine = pl.ds(me * queries_local, queries_local)
        sent = []
        for owner, device in ((far, far_device), (cross, cross_device), (near, near_device)):
            sent.append(
                remote.start(
                    bias_send.at[chain, pl.ds(owner * heads, heads)],
                    bias_full.at[chain, :, mine],
                    device,
                )
            )
        bias_copies.append(sent)
        bias_full[chain, :, mine, :] = bias_send[chain, pl.ds(me * heads, heads)]
        if turn == 0:
            gather_attend.forward()
            load_output = load(output_hbm, output_weight)
            load_down = load(down_hbm, down_weight)
            load_hidden = load(hidden_hbm, hidden_weight)

    gather_down = gather(rows_down)
    gather_down.start(*range(GATHER_PARTS // 2))

    for index in range(PAIR_SLOTS):
        pair_copy(index).start()

    load_input.wait()

    def project(half):
        rows = rows_attend[pl.ds(2 * half, 2)].reshape(span, width)
        queries[half] = nt(rows, input_weight[0]).astype(BF)
        keys[half] = nt(rows, input_weight[1]).astype(BF)
        values[half] = nt(rows, input_weight[2]).astype(BF)

    gather_attend.wait_near()
    project(chip)
    gather_attend.wait_rest()
    project(away)

    head_lane = lax.broadcasted_iota(jnp.int32, (span, local_width), 1)

    def stacked(rows):
        zero = jnp.zeros_like(rows)
        return jnp.concatenate(
            [
                jnp.where((head_lane >= head * HD) & (head_lane < (head + 1) * HD), rows, zero)
                for head in range(heads)
            ],
            axis=0,
        )

    def choose(pieces):
        out = pieces[-1]
        for head in range(heads - 2, -1, -1):
            out = jnp.where(head_lane < (head + 1) * HD, pieces[head], out)
        return out

    def attend(chain):
        scores = nt(stacked(queries[chain]), keys[chain]) * HD ** (-0.5) + bias_full[
            chain
        ].reshape(heads * span, span).astype(F32)
        key_place = lax.broadcasted_iota(jnp.int32, (heads * span, span), 1)
        scores = jnp.where(key_place < length_ref[chain], scores, -1000000000.0)
        top = jnp.max(scores, axis=-1, keepdims=True)
        weights = jnp.exp(scores - top)
        weights = weights * (1.0 / jnp.sum(weights, axis=-1, keepdims=True))
        probs[chain] = weights
        soft = weights.astype(BF)
        attended[chain] = choose(
            [nn(soft[head * span : (head + 1) * span], values[chain]) for head in range(heads)]
        ).astype(BF)

    def put(target, half, rows):
        target[pl.ds(2 * half, 2)] = rows.reshape(2, local, width)

    ids = (me, near, far, cross)

    def scatter(index, source):
        return Scatter(
            remote,
            source,
            scatter_send.at[index],
            scatter_recv.at[index],
            ids,
            near_device,
            far_device,
        )

    bias_copies[0][0].wait_recv()
    bias_copies[0][1].wait_recv()
    bias_copies[1][2].wait_recv()
    attend(away)
    load_output.wait()
    put(part, away, nn(attended[away], output_weight[...]))
    scatter_attend = scatter(0, part)
    scatter_attend.pre()
    bias_copies[1][0].wait_recv()
    bias_copies[1][1].wait_recv()
    bias_copies[0][2].wait_recv()
    scatter_attend.across()
    gather_down.start(*range(GATHER_PARTS // 2, GATHER_PARTS))
    attend(chip)
    put(part, chip, nn(attended[chip], output_weight[...]))
    scatter_attend.local()

    load_down.wait()

    def back_down(half):
        rows = rows_down[pl.ds(2 * half, 2)].reshape(span, width)
        grad_active[half] = nt(rows, down_weight[...])
        for slot in range(2):
            place_slot = 2 * half + slot
            turned[:, pl.ds(pl.multiple_of(place_slot * local, local), local)] = jnp.transpose(
                rows[slot * local : (slot + 1) * local]
            )


    gate_attend = sigmoid(mod(2))
    out_total = scatter_attend.total()
    out_attend[...] = out_total
    total = tokens[...].astype(F32) + valid * gate_attend * out_total
    middle[...] = total
    normed, inverse_hidden = layer_norm(total)
    norm_hidden[...] = normed
    rows_hidden[me] = (normed * (1.0 + mod(3)) + mod(4)).astype(BF)
    gather_hidden = gather(rows_hidden)
    gather_hidden.start(*range(GATHER_PARTS))
    gather_down.forward()
    gather_down.wait_near()
    back_down(chip)
    gather_down.wait_rest()
    back_down(away)

    load_hidden.wait()

    def transition(half):
        rows = rows_hidden[pl.ds(2 * half, 2)].reshape(span, width)
        gate = nn(rows, hidden_weight[0])
        up = nn(rows, hidden_weight[1])
        squashed = sigmoid(gate)
        silu = gate * squashed
        active[half] = (silu * up).astype(BF)
        back = grad_active[half]
        grad_gate[half] = (back * up * squashed * (1.0 + gate * (1.0 - squashed))).astype(BF)
        grad_up[half] = (back * silu).astype(BF)

    def back_hidden(half):
        put(
            part,
            half,
            nt(grad_gate[half], hidden_weight[0]) + nt(grad_up[half], hidden_weight[1]),
        )

    chunk = width // groups
    per_block = max(1, 192 // chunk)

    def weight_grad(pieces, *pairs):
        for block in range(groups // per_block):
            rows = slice(block * per_block * chunk, (block + 1) * per_block * chunk)
            product = jnp.concatenate([nn(left[rows, :], right) for left, right in pairs], axis=1)
            for index in pieces:
                first, size = PIECES[index][1:3]
                for inner in range(per_block):
                    slot = slot_of(block * per_block + inner, orders[index])
                    piece_store[index][slot] = product[
                        inner * chunk : (inner + 1) * chunk, first : first + size
                    ].astype(BF)
        for index in pieces:
            sums[index] = Halving(
                remote,
                piece_store[index],
                piece_recv[index],
                dp,
                groups,
                dp_device,
                orders[index],
            )
            sums[index].send()

    sums = {}

    missing = {matrix: sum(piece[0] == matrix for piece in PIECES) for matrix in range(4)}

    def take_sum(index):
        matrix, first, size = PIECES[index][:3]
        sums[index].sum()
        if sums[index].done():
            final_weights[matrix, :, first : first + size] = sums[index].result
            missing[matrix] -= 1
            if missing[matrix] == 0:
                store(final_weights.at[matrix], weights_out.at[matrix])

    def advance(place):
        for index in SUMS[place]:
            take_sum(index)

    def take_rest():
        while any(missing.values()):
            for index in range(len(PIECES)):
                if not sums[index].done():
                    take_sum(index)

    def flat(ref):
        return ref[...].reshape(chains * span, ref.shape[-1])

    def turn_rows(source, target):
        for slot in range(4):
            target[:, slot * local : (slot + 1) * local] = jnp.transpose(source[slot])

    gather_hidden.wait_near()
    transition(chip)
    back_hidden(chip)
    put(part_down, chip, nn(active[chip], down_weight[...]))
    gather_hidden.forward()
    gather_hidden.wait_rest()
    transition(away)
    weight_grad((0, 1), (turned, flat(active)))
    back_hidden(away)
    scatter_hidden = scatter(1, part)
    scatter_hidden.pre()
    put(part_down, away, nn(active[away], down_weight[...]))
    scatter_hidden.across()
    scatter_hidden.local()
    scatter_down = scatter(2, part_down)
    scatter_down.pre()

    turn_rows(rows_hidden, turned_more)
    weight_grad((2, 3), (turned_more, flat(grad_gate)))

    grad_h = scatter_hidden.total()
    normed = norm_hidden[...]
    back = cotangent[...].astype(F32) + norm_back(grad_h * (1.0 + mod(3)), normed, inverse_hidden)
    grad_middle[...] = back
    rows_out[me] = (back * valid * gate_attend).astype(BF)
    gather_out = gather(rows_out)
    gather_out.start(*range(GATHER_PARTS))

    weight_grad((4, 5), (turned_more, flat(grad_up)))

    def keep_mod(index, rows):
        mod_part[index : index + 1, :] = jnp.sum(rows, axis=0, keepdims=True)

    mod_part[...] = jnp.zeros_like(mod_part)
    keep_mod(3, grad_h * normed)
    keep_mod(4, grad_h)
    keep_mod(2, back * valid * out_attend[...] * gate_attend * (1.0 - gate_attend))
    turn_rows(rows_attend, turned)

    score_copies = []

    def back_attend(chain):
        rows = rows_out[pl.ds(2 * chain, 2)].reshape(span, width)
        grad_heads = stacked(nt(rows, output_weight[...]).astype(BF))
        weights = probs[chain]
        grad_probs = nt(grad_heads, values[chain])
        grad_logits = (
            weights * (grad_probs - jnp.sum(grad_probs * weights, axis=-1, keepdims=True))
        ).astype(BF)
        grad_scores[chain] = grad_logits.reshape(heads, span, span)
        sent = []
        for owner, device in ((far, far_device), (cross, cross_device), (near, near_device)):
            sent.append(
                remote.start(
                    grad_scores.at[chain, :, pl.ds(owner * queries_local, queries_local)],
                    scores_own.at[chain, pl.ds(me * heads, heads)],
                    device,
                )
            )
        score_copies.append(sent)
        scores_own[chain, pl.ds(me * heads, heads)] = grad_scores[
            chain, :, pl.ds(me * queries_local, queries_local), :
        ]
        query_stack = stacked(queries[chain])
        grad_query = (
            choose(
                [
                    nn(grad_logits[head * span : (head + 1) * span], keys[chain])
                    for head in range(heads)
                ]
            )
            * HD ** (-0.5)
        ).astype(BF)
        grad_key = (tn(grad_logits, query_stack) * HD ** (-0.5)).astype(BF)
        grad_value = tn(weights.astype(BF), grad_heads).astype(BF)
        grad_projected[chain] = jnp.concatenate([grad_query, grad_key, grad_value], axis=1)
        put(
            part,
            chain,
            nn(grad_query, input_weight[0])
            + nn(grad_key, input_weight[1])
            + nn(grad_value, input_weight[2]),
        )

    gather_out.wait_near()
    back_attend(chip)
    gather_out.forward()
    advance(0)
    gather_out.wait_rest()
    back_attend(away)
    scatter_input = scatter(3, part)
    scatter_input.pre()
    turn_rows(rows_out, turned_more)
    scatter_input.across()
    scatter_input.local()
    scatter_down.across()
    scatter_down.local()
    weight_grad((6, 7, 8), (turned, flat(grad_projected)), (turned_more, flat(attended)))
    advance(1)
    for sent in score_copies:
        for copy in sent:
            copy.wait_recv()
    store(scores_own, scores_out)
    def bias_grad_block(index, total):
        slot = lax.rem(index, PAIR_SLOTS)
        pair_copy(index).wait()
        for row_index in range(PAIR_ROWS):
            place_row = lax.rem(index, blocks) * PAIR_ROWS + row_index
            rows = jnp.concatenate(
                [
                    stage[half, pl.ds(place_row, 16, stride=queries_local), :].astype(BF)
                    for half in range(2)
                ],
                axis=1,
            )
            total = total + nn(rows, pair[slot, row_index])

        @pl.when(index + PAIR_SLOTS < n_blocks)
        def _():
            pair_copy(index + PAIR_SLOTS).start()

        return total

    def bias_grad_chain(turn, total):
        chain = lax.rem(chip + turn, 2)
        for half in range(2):
            stage[half, 0:all_rows, :] = (
                scores_own[chain, :, :, half * 128 : (half + 1) * 128]
                .reshape(all_rows, 128)
                .astype(F32)
            )
            stage[half, all_rows:, :] = jnp.zeros((16 * queries_local - all_rows, 128), F32)
        return lax.fori_loop(turn * blocks, (turn + 1) * blocks, bias_grad_block, total)

    total = bias_grad_chain(0, jnp.zeros((16, pair_hbm.shape[3]), F32))
    advance(2)
    total = bias_grad_chain(1, total)
    half = total.shape[1] // 2
    for quarter in range(4):
        rows, lanes = quarter // 2 * 8, quarter % 2 * half
        bias_quarters[quarter] = total[rows : rows + 8, lanes : lanes + half]
    tensor_devices = ((near, near_device), (far, far_device), (cross, cross_device))
    tensor_copies = [
        remote.start(bias_quarters.at[owner], bias_parts.at[me], device)
        for owner, device in tensor_devices
    ]
    bias_parts[me] = bias_quarters[me]

    grad_h = scatter_input.total()
    normed = norm_attend[...]
    grad_tokens[...] = (
        grad_middle[...] + norm_back(grad_h * (1.0 + mod(0)), normed, inverse_attend)
    ).astype(BF)
    keep_mod(0, grad_h * normed)
    keep_mod(1, grad_h)
    out_total = scatter_down.total()
    result[...] = (middle[...] + valid * gate_hidden * out_total).astype(BF)
    keep_mod(
        5, cotangent[...].astype(F32) * valid * out_total * gate_hidden * (1.0 - gate_hidden)
    )
    to_near = remote.start(mod_part, mod_near, near_device)

    store(result, result_out)
    store(grad_tokens, grad_tokens_out)

    advance(3)

    to_near.wait_recv()
    chain_mods = mod_part[...] + mod_near[...]
    mod_halves[0] = chain_mods[:, : width // 2].astype(BF)
    mod_halves[1] = chain_mods[:, width // 2 :].astype(BF)
    mods_gather[dp] = mod_halves[core]
    mod_copies = [
        remote.start(mods_gather.at[dp], mods_gather.at[dp], dp_device(lax.rem(dp + step, groups)))
        for step in range(1, groups)
    ]
    for copy in tensor_copies:
        copy.wait_recv()
    bias_sums[0] = bias_parts[0] + bias_parts[1] + bias_parts[2] + bias_parts[3]
    bias_copies = [
        remote.start(bias_sums.at[0], bias_sums.at[step], dp_device(lax.rem(dp + step, groups)))
        for step in range(1, groups)
    ]
    advance(4)
    advance(5)
    for copy in mod_copies:
        copy.wait_recv()
    mods_all[me] = mods_gather[...]
    mod_copies = [
        remote.start(mods_gather, mods_all.at[me], device) for _, device in tensor_devices
    ]
    for copy in bias_copies:
        copy.wait_recv()
    bias_grad[me] = jnp.sum(bias_sums[...], axis=0)
    bias_copies = [
        remote.start(bias_grad.at[me], bias_grad.at[me], device) for _, device in tensor_devices
    ]
    for copy in hot_copies:
        copy.wait_recv()
    rows_all = chains * groups * 8
    hot = jnp.concatenate(
        [hots[:, chain].reshape(groups * 8, n_table) for chain in range(chains)], axis=0
    ).astype(BF)
    hot_lane = lax.broadcasted_iota(jnp.int32, hot.shape, 1)
    zero = jnp.zeros_like(hot)
    time_rows = nn(jnp.where(hot_lane < times, hot, zero), tables[...])
    class_rows = nn(jnp.where(hot_lane < times, zero, hot), tables[...])
    expanded[:, :rows_all] = jnp.transpose(time_rows)
    expanded[:, rows_all:] = jnp.transpose(class_rows)
    store(expanded, expanded_out)
    advance(6)
    for copy in mod_copies:
        copy.wait_recv()
    store(mods_all, mods_out)
    rows = mod_rows(mods_all)
    member = lax.rem(lax.broadcasted_iota(jnp.int32, (rows_all, 1), 0), 8)
    rest = jnp.zeros((rows_all, tables.shape[1]), F32)
    for vector in range(6):
        product = nt(rows, modulation_weight[:, vector * width : (vector + 1) * width])
        rest = rest + jnp.where(member == vector, product, 0.0)
    table = jnp.zeros((n_table, tables.shape[1]), F32)
    for _ in range(3):
        piece = rest.astype(BF)
        table = table + tn(hot, piece)
        rest = rest - piece.astype(F32)
    tables_grad[...] = table
    store(tables_grad, tables_out)
    for copy in bias_copies:
        copy.wait_recv()
    store(bias_grad, bias_grad_out)
    advance(7)
    take_rest()
    for copy in stores:
        copy.wait()
    remote.finish()


def finish_kernel(
    dims,
    result_hbm,
    grad_tokens_hbm,
    weights_hbm,
    scores_hbm,
    mods_hbm,
    expanded_hbm,
    tables_hbm,
    bias_grad_hbm,
    bias_hbm,
    result_out,
    grad_tokens_out,
    pair_out,
    bias_grad_out,
    input_out,
    output_out,
    hidden_out,
    down_out,
    modulation_out,
    time_out,
    class_out,
    rows_pass,
    weights,
    scores,
    mods,
    expanded,
    tables,
    bias_grad,
    bias,
    places,
    pair,
    modulation,
    input_grad,
    output_grad,
    bias_rows,
    load_sems,
    pair_sems,
    store_sems,
):
    (groups, chains, span, local, width, local_width, queries_local, hidden) = dims
    heads = local_width // HD
    blocks = queries_local // PAIR_ROWS
    times = time_out.shape[0]

    def start(src, dst, semaphore):
        copy = pltpu.make_async_copy(src, dst, semaphore)
        copy.start()
        return copy

    moves = (
        (bias_hbm, bias),
        (expanded_hbm, expanded),
        (mods_hbm, mods),
        (scores_hbm.at[0], scores.at[0]),
        (scores_hbm.at[1], scores.at[1]),
        (weights_hbm, weights),
        (result_hbm, rows_pass.at[0]),
        (grad_tokens_hbm, rows_pass.at[1]),
        (tables_hbm, tables),
        (bias_grad_hbm, bias_grad),
    )
    loads = [start(src, dst, load_sems.at[index]) for index, (src, dst) in enumerate(moves)]

    loads[0].wait()
    weight_rows = bias[...].astype(F32)
    spread = jnp.concatenate(
        [
            jnp.broadcast_to(weight_rows[head : head + 1], (PAIR_ROWS, weight_rows.shape[1]))
            for head in range(4 * heads)
        ],
        axis=0,
    )
    member = lax.rem(lax.broadcasted_iota(jnp.int32, spread.shape, 0), PAIR_ROWS)
    for row_index in range(PAIR_ROWS):
        places[row_index] = jnp.where(member == row_index, spread, 0.0).astype(BF)

    def pair_copy(index):
        slot = lax.rem(index, PAIR_SLOTS)
        return pltpu.make_async_copy(
            pair.at[slot],
            pair_out.at[
                index // blocks, pl.ds(lax.rem(index, blocks) * PAIR_ROWS, PAIR_ROWS)
            ],
            pair_sems.at[slot],
        )

    def pair_block(index, carry):
        @pl.when(index >= PAIR_SLOTS)
        def _():
            pair_copy(index - PAIR_SLOTS).wait()

        rows = scores[index // blocks, :, pl.ds(lax.rem(index, blocks) * PAIR_ROWS, PAIR_ROWS)]
        across = jnp.transpose(rows.reshape(4 * heads * PAIR_ROWS, rows.shape[2]))
        slot = lax.rem(index, PAIR_SLOTS)
        for row_index in range(PAIR_ROWS):
            pair[slot, row_index] = nn(across, places[row_index]).astype(BF)
        pair_copy(index).start()
        return carry

    stores = []

    def store(src, dst):
        stores.append(start(src, dst, store_sems.at[len(stores)]))

    loads[1].wait()
    loads[2].wait()
    rows = mod_rows(mods)
    both = jnp.concatenate([rows, rows], axis=0)
    lane = lax.rem(lax.broadcasted_iota(jnp.int32, expanded.shape, 1), 8)
    for vector in range(6):
        left = jnp.where(lane == vector, expanded[...], 0.0).astype(BF)
        modulation[vector] = nn(left, both)
        store(modulation.at[vector], modulation_out.at[:, pl.ds(vector * width, width)])
    n_blocks = chains * blocks
    loads[3].wait()
    loads[4].wait()
    lax.fori_loop(0, blocks, pair_block, 0)
    for copy in loads[5:]:
        copy.wait()
    store(weights.at[0], down_out)
    store(weights.at[2], hidden_out.at[0])
    store(weights.at[3], hidden_out.at[1])
    store(rows_pass.at[0], result_out)
    store(rows_pass.at[1], grad_tokens_out)
    store(tables.at[pl.ds(0, times)], time_out)
    store(tables.at[pl.ds(times, class_out.shape[0])], class_out)
    bias_rows[...] = jnp.concatenate(
        [
            jnp.concatenate([bias_grad[0], bias_grad[1]], axis=1),
            jnp.concatenate([bias_grad[2], bias_grad[3]], axis=1),
        ],
        axis=0,
    )[: 4 * heads]
    store(bias_rows, bias_grad_out)
    for index in range(3):
        input_grad[index] = weights[1, :, index * local_width : (index + 1) * local_width]
    store(input_grad, input_out)
    output_grad[...] = jnp.transpose(weights[1, :, 3 * local_width :])
    store(output_grad, output_out)
    lax.fori_loop(blocks, n_blocks, pair_block, 0)

    for index in range(n_blocks - PAIR_SLOTS, n_blocks):
        pair_copy(index).wait()
    for copy in stores:
        copy.wait()


def body(
    groups,
    tokens,
    pair_features,
    cotangent,
    chain_length,
    time_bin,
    cath_class,
    bias_weight,
    input_weight,
    output_weight,
    hidden_weight,
    down_weight,
    modulation_weight,
    time_table,
    class_table,
):
    chains, queries_local, span, channels = pair_features.shape
    local, width = tokens.shape
    local_width = input_weight.shape[2]
    hidden = down_weight.shape[0]
    heads = local_width // HD
    rows = chains * span
    chunk = width // groups
    assert chains == 2 and rows == 4 * local and span == 2 * local
    assert span == 256 and channels == 256 and 4 * local_width == width == hidden
    assert queries_local % PAIR_ROWS == 0
    dims = (groups, chains, span, local, width, local_width, queries_local, hidden)
    bits = groups.bit_length() - 1
    assert groups == 1 << bits
    straight = tuple(range(bits))
    turns = (straight, straight[1:2] + straight[:1] + straight[2:], straight[1:] + straight[:1])
    orders = tuple(turns[piece[3]] for piece in PIECES)
    n_table = time_table.shape[0] + class_table.shape[0]
    input_turned = jnp.swapaxes(input_weight, 1, 2)
    bias_turned = bias_weight.T

    anywhere = pl.BlockSpec(memory_space=pl.ANY)
    scalars = pl.BlockSpec(memory_space=pltpu.SMEM)
    vmem = pltpu.VMEM
    half_rows = (chains, span, width)
    slots = (4, local, width)
    messages = 4 * 3 * (1 + GATHER_PARTS) + 6 * 2 + len(PIECES) * bits + 3 * (groups - 1) + 10
    weights_shape = (4, chunk, width)
    outs = pl.pallas_call(
        functools.partial(layer_kernel, dims, orders),
        out_shape=(
            jax.ShapeDtypeStruct((local, width), BF),
            jax.ShapeDtypeStruct((local, width), BF),
            jax.ShapeDtypeStruct((chains, 4 * heads, queries_local, span), BF),
            jax.ShapeDtypeStruct((4, groups, 8, width // 2), BF),
            jax.ShapeDtypeStruct((time_table.shape[1], 2 * groups * 16), F32),
            jax.ShapeDtypeStruct((n_table, time_table.shape[1]), F32),
            jax.ShapeDtypeStruct((4, 8, channels // 2), F32),
            jax.ShapeDtypeStruct(weights_shape, F32),
        ),
        in_specs=[scalars] * 3 + [anywhere] * 11,
        out_specs=[anywhere] * 8,
        scratch_shapes=[
            vmem((local, width), BF),
            vmem((local, width), BF),
            vmem((PAIR_SLOTS, PAIR_ROWS, span, channels), BF),
            vmem(bias_turned.shape, BF),
            vmem(input_turned.shape, BF),
            vmem(output_weight.shape, BF),
            vmem(hidden_weight.shape, BF),
            vmem(down_weight.shape, BF),
            vmem(modulation_weight.shape, BF),
            vmem((n_table, time_table.shape[1]), BF),
            vmem((8, modulation_weight.shape[1]), F32),
            vmem((2, 16 * queries_local, 128), F32),
            vmem((groups, chains, 8, n_table), F32),
            vmem((4, groups, 8, width // 2), BF),
            vmem((groups, 8, width // 2), BF),
            vmem((2, 8, width // 2), BF),
            vmem(slots, BF),
            vmem(slots, BF),
            vmem(slots, BF),
            vmem(slots, BF),
            vmem((chains, 4 * heads, queries_local, span), BF),
            vmem((chains, heads, span, span), BF),
            vmem((chains, span, local_width), BF),
            vmem((chains, span, local_width), BF),
            vmem((chains, span, local_width), BF),
            vmem((chains, heads * span, span), F32),
            vmem((chains, span, local_width), BF),
            vmem(slots, F32),
            vmem(slots, F32),
            vmem(half_rows, F32),
            vmem(half_rows, BF),
            vmem(half_rows, BF),
            vmem(half_rows, BF),
            vmem((chains, heads, span, span), BF),
            vmem((chains, 4 * heads, queries_local, span), BF),
            vmem((chains, span, 3 * local_width), BF),
            vmem((4, 3, local, width), BF),
            vmem((4, 3, local, width), BF),
            vmem((width, rows), BF),
            vmem((width, rows), BF),
            vmem(weights_shape, F32),
            vmem((local, width), F32),
            vmem((local, width), F32),
            vmem((local, width), F32),
            vmem((local, width), F32),
            vmem((local, width), F32),
            vmem((local, width), BF),
            vmem((local, width), BF),
            vmem((8, width), F32),
            vmem((8, width), F32),
            vmem((4, 8, channels // 2), F32),
            vmem((4, 8, channels // 2), F32),
            vmem((groups, 8, channels // 2), F32),
            vmem((4, 8, channels // 2), F32),
            vmem((time_table.shape[1], 2 * groups * 16), F32),
            vmem((n_table, time_table.shape[1]), F32),
            pltpu.SemaphoreType.DMA((11,)),
            pltpu.SemaphoreType.DMA((PAIR_SLOTS,)),
            pltpu.SemaphoreType.DMA((14,)),
            pltpu.SemaphoreType.DMA((messages,)),
            pltpu.SemaphoreType.DMA((messages,)),
        ]
        + [vmem((groups, chunk, piece[2]), BF) for piece in PIECES] * 2,
        compiler_params=pltpu.CompilerParams(
            collective_id=0, has_side_effects=True, vmem_limit_bytes=VMEM_BYTES
        ),
        name="layer",
    )(
        chain_length,
        time_bin,
        cath_class,
        tokens,
        cotangent,
        pair_features,
        bias_turned,
        input_turned,
        output_weight,
        hidden_weight,
        down_weight,
        modulation_weight,
        time_table,
        class_table,
    )
    result, grad_tokens, scores, mods_all, expanded, tables, bias_grad, weights = outs

    outs = pl.pallas_call(
        functools.partial(finish_kernel, dims),
        out_shape=(
            jax.ShapeDtypeStruct((local, width), BF),
            jax.ShapeDtypeStruct((local, width), BF),
            jax.ShapeDtypeStruct(pair_features.shape, BF),
            jax.ShapeDtypeStruct(bias_turned.shape, F32),
            jax.ShapeDtypeStruct((3, chunk, local_width), F32),
            jax.ShapeDtypeStruct((local_width, chunk), F32),
            jax.ShapeDtypeStruct((2, chunk, hidden), F32),
            jax.ShapeDtypeStruct((chunk, hidden), F32),
            jax.ShapeDtypeStruct(modulation_weight.shape, F32),
            jax.ShapeDtypeStruct(time_table.shape, F32),
            jax.ShapeDtypeStruct(class_table.shape, F32),
        ),
        in_specs=[anywhere] * 9,
        out_specs=[anywhere] * 11,
        scratch_shapes=[
            vmem((2, local, width), BF),
            vmem(weights.shape, F32),
            vmem(scores.shape, BF),
            vmem(mods_all.shape, BF),
            vmem(expanded.shape, F32),
            vmem(tables.shape, F32),
            vmem(bias_grad.shape, F32),
            vmem(bias_turned.shape, BF),
            vmem((PAIR_ROWS, 4 * heads * PAIR_ROWS, channels), BF),
            vmem((PAIR_SLOTS, PAIR_ROWS, span, channels), BF),
            vmem((6, modulation_weight.shape[0], width), F32),
            vmem((3, chunk, local_width), F32),
            vmem((local_width, chunk), F32),
            vmem(bias_turned.shape, F32),
            pltpu.SemaphoreType.DMA((10,)),
            pltpu.SemaphoreType.DMA((PAIR_SLOTS,)),
            pltpu.SemaphoreType.DMA((16,)),
        ],
        compiler_params=pltpu.CompilerParams(vmem_limit_bytes=VMEM_BYTES),
        name="finish",
    )(
        result,
        grad_tokens,
        weights,
        scores,
        mods_all,
        expanded,
        tables,
        bias_grad,
        bias_turned,
    )
    outs = list(outs)
    outs[3], outs[7] = outs[3].T, outs[7].T
    return tuple(outs)


def solution(mesh):
    placed = (
        P(("dp", "tensor"), None),
        P("dp", "tensor", None, None),
        P(("dp", "tensor"), None),
        P("dp"),
        P("dp"),
        P("dp"),
        P(),
        P(None, None, "tensor"),
        P("tensor", None),
        P(None, None, "tensor"),
        P("tensor", None),
        P(),
        P(),
        P(),
    )
    assert mesh.shape["tensor"] == 4
    return jax.shard_map(
        functools.partial(body, mesh.shape["dp"]),
        mesh=mesh,
        in_specs=placed,
        out_specs=(
            P(("dp", "tensor"), None),
            P(("dp", "tensor"), None),
            P("dp", "tensor", None, None),
            P(),
            P(None, "dp", "tensor"),
            P("tensor", "dp"),
            P(None, "dp", "tensor"),
            P("tensor", "dp"),
            P(),
            P(),
            P(),
        ),
        check_vma=False,
    )
```
